256 devices in a mesh: seq: 64 (over z, y, core), ch: 4 (over x).
Axes of the slice: x: 4, y: 4, z: 8, core: 2. Of those that a mesh axis runs over, the one named last changes fastest.
Arguments:
- query_proj: bfloat16 [8192, 2048], P('seq', 'ch'), may hold values from -6 to 6
- key_proj: bfloat16 [8192, 2048], P('seq', 'ch'), may hold values from -6 to 6
- value_proj: bfloat16 [8192, 2048], P('seq', 'ch'), may hold values from -6 to 6
- short_filter: float32 [3, 3, 2048], P(None, None, 'ch'), may hold values from -3.5 to 3.5
- long_filter: float32 [8192, 2048], P('seq', 'ch'), may hold values from -0.0625 to 0.0625
- skip_gain: float32 [2048], P('ch'), may hold values from 0.5 to 1.5
- out_weight: bfloat16 [2048, 4096], P('ch'), may hold values from -0.125 to 0.125
- cotangent: bfloat16 [8192, 4096], P('seq', 'ch'), may hold values from -16 to 16
Outputs:
- layer_out: bfloat16 [8192, 4096], P('seq', 'ch')
- grad_query: float32 [8192, 2048], P('seq', 'ch')
- grad_key: float32 [8192, 2048], P('seq', 'ch')
- grad_value: float32 [8192, 2048], P('seq', 'ch')
- grad_short: float32 [3, 3, 2048], P(None, None, 'ch')
- grad_filter: float32 [8192, 2048], P('seq', 'ch')
- grad_skip: float32 [2048], P('ch')
- grad_w_out_t: float32 [4096, 2048], P('seq', 'ch')
The draws below stay inside these ranges and needn't reach their ends.
All inputs are finite; a program needn't handle non-finite values.
Results may differ from the reference program's by a relative error of at most 0.011.
Values may be sent and summed in bfloat16 or wider, within the bound.
A program may use at most 128 MiB of HBM per device.

```python
import jax
import jax.numpy as jnp

D = 4096
C = 2048
KS = 3
L = 8192


def spiked(values, own_key, source, target, shards_of, factor):
    def block_of(dim):
        return (jnp.arange(values.shape[dim]) // (values.shape[dim] // shards_of)).reshape((-1,) + (1,) * (values.ndim - 1 - dim))

    one_side = jax.random.permutation(own_key, shards_of)[block_of(target)]
    far = (block_of(target) + shards_of // 2) % shards_of
    return jnp.where((block_of(source) == one_side) | (block_of(source) == far), factor * values, values)


def shard_levels(rng, shape, pieces, smallest, high):
    level, own = 1.0, jax.random.fold_in(rng, 6)
    for axis_at, shards_of in pieces:
        steps = jnp.exp(jax.random.uniform(jax.random.fold_in(own, axis_at), (shards_of,), jnp.float32, smallest / len(pieces), high / len(pieces)))
        level = level * jnp.repeat(steps, shape[axis_at] // shards_of).reshape([-1 if axis == axis_at else 1 for axis in range(len(shape))])
    return level


def normal_values(own_key, dims, width, limit, shards=(), held_as=jnp.bfloat16):
    entries = jax.random.normal(own_key, dims, jnp.float32) * width
    if len(shards) > 0:
        entries = shard_levels(own_key, dims, shards, -0.22, 0.18) * entries
    return jnp.clip(entries, min=-limit, max=limit).astype(held_as)


def gaussian_with(rng, extent, scale, limit, cuts, heavy, kind=jnp.bfloat16):
    result = scale * jax.random.normal(rng, extent, jnp.float32)
    if cuts:
        result = result * shard_levels(rng, extent, cuts, -0.22, 0.18)
    return jnp.clip(spiked(result, jax.random.fold_in(rng, 3), *heavy), -limit, limit).astype(kind)


def setup_inputs(seed: int = 0) -> dict:
    key_list = jax.random.split(jax.random.key(seed), 9)
    return {
        "query_proj": normal_values(key_list[0], (L, C), 1.0, 6.0, ((0, 64), (1, 4))),
        "key_proj": normal_values(key_list[1], (L, C), 1.0, 6.0, ((0, 64), (1, 4))),
        "value_proj": normal_values(key_list[2], (L, C), 1.0, 6.0, ((0, 64), (1, 4))),
        "short_filter": normal_values(key_list[3], (3, KS, C), KS ** -0.5, 3.5, ((2, 4),), jnp.float32),
        "long_filter": normal_values(key_list[4], (L, C), L ** -0.5, 0.0625, ((0, 64), (1, 4)), jnp.float32),
        "skip_gain": jnp.clip(0.5 + 1.0 * jax.random.uniform(key_list[5], (C,), jnp.float32) ** shard_levels(key_list[5], (C,), ((0, 4),), -0.2, 0.2), 0.5, 1.5),
        "out_weight": normal_values(key_list[6], (C, D), C ** -0.5, 0.125, ((0, 4),)),
        "cotangent": gaussian_with(key_list[7], (L, D), 1.0, 16.0, ((0, 64), (1, 4)), (0, 1, 64, 4.0)),
    }


def causal_conv(signal, kernel):
    length = signal.shape[0]
    spectrum = jnp.fft.rfft(signal, n=2 * length, axis=0) * jnp.fft.rfft(kernel, n=2 * length, axis=0)
    return jnp.fft.irfft(spectrum, n=2 * length, axis=0)[:length].astype(signal.dtype)


def correlate(signal, kernel):
    length = signal.shape[0]
    spectrum = jnp.conj(jnp.fft.rfft(kernel, n=2 * length, axis=0)) * jnp.fft.rfft(signal, n=2 * length, axis=0)
    return jnp.fft.irfft(spectrum, n=2 * length, axis=0)[:length].astype(signal.dtype)


def reference(query_proj, key_proj, value_proj, short_filter, long_filter, skip_gain, out_weight, cotangent):
    streams = jnp.stack([query_proj, key_proj, value_proj]).astype(jnp.float32)
    row_count = streams.shape[1]
    padded = jnp.pad(streams, ((0, 0), (KS - 1, 0), (0, 0)))
    shifted = [padded[:, KS - 1 - offset:KS - 1 - offset + row_count] for offset in range(KS)]
    filtered = sum(short_filter[:, offset][:, None, :] * shifted[offset] for offset in range(KS))
    query_short, key_short, value_short = filtered[0], filtered[1], filtered[2]
    product = key_short * value_short
    mixed_seq = causal_conv(product, long_filter) + skip_gain * product
    gated_values = (query_short * mixed_seq).astype(jnp.bfloat16)
    layer_out = jnp.dot(gated_values, out_weight, preferred_element_type=jnp.float32).astype(jnp.bfloat16)
    grad_gated = jnp.dot(cotangent, out_weight.T, preferred_element_type=jnp.float32)
    grad_w_out_t = jnp.dot(cotangent.T, gated_values, preferred_element_type=jnp.float32)
    grad_mixed = grad_gated * query_short
    grad_query_short = grad_gated * mixed_seq
    grad_product = correlate(grad_mixed, long_filter) + skip_gain * grad_mixed
    grad_filter = correlate(grad_mixed, product)
    grad_skip = jnp.sum(grad_mixed * product, axis=0)
    grad_streams = jnp.stack([grad_query_short, grad_product * value_short, grad_product * key_short])
    grad_short = jnp.stack([jnp.sum(grad_streams * shifted[offset], axis=1) for offset in range(KS)], axis=1)
    tail_pad = jnp.pad(grad_streams, ((0, 0), (0, KS - 1), (0, 0)))
    grad_inputs = sum(short_filter[:, offset][:, None, :] * tail_pad[:, offset:offset + row_count] for offset in range(KS))
    return (layer_out, grad_inputs[0], grad_inputs[1], grad_inputs[2], grad_short, grad_filter, grad_skip, grad_w_out_t)
```

```python
import math

import jax
import jax.numpy as jnp
from jax import lax
from jax.sharding import PartitionSpec as P

exact_mode = lax.Precision.HIGHEST


def from_behind(shard, axis, by):
    size = lax.axis_size(axis)
    pairs = [(i, i + by) for i in range(size) if 0 <= i + by < size]
    return lax.ppermute(shard, axis, pairs)


def as_sent(shard):

    def short(part):
        return part.astype(jnp.bfloat16) if part.dtype == jnp.float32 else part

    return jax.tree.map(short, shard)


def tables(rows_out, cols_in, period):
    row_index = lax.broadcasted_iota(jnp.int32, (rows_out, cols_in), 0)
    col_index = lax.broadcasted_iota(jnp.int32, (rows_out, cols_in), 1)
    phase_angle = (row_index * col_index % period).astype(jnp.float32) * (2.0 * math.pi / period)
    return (jnp.cos(phase_angle), jnp.sin(phase_angle))


def along_rows(factor, values):
    return jnp.tensordot(factor, values, axes=1, precision=exact_mode)


def rows_spectrum(signal, basis_pair):
    return (along_rows(basis_pair[0], signal), -along_rows(basis_pair[1], signal))


def rows_inverse(complex_pair, basis_pair):
    total = along_rows(basis_pair[0], complex_pair[0]) - along_rows(basis_pair[1], complex_pair[1])
    return total / basis_pair[0].shape[1]


def block_forward(complex_pair, basis_pair):
    cosine_part, sine_part = basis_pair
    real_part = along_rows(cosine_part, complex_pair[0]) + along_rows(sine_part, complex_pair[1])
    imag_part = along_rows(cosine_part, complex_pair[1]) - along_rows(sine_part, complex_pair[0])
    return (real_part, imag_part)


def block_inverse(complex_pair, basis_pair):
    cosine_part, sine_part = basis_pair
    norming = 1.0 / cosine_part.shape[1]
    real_part = along_rows(cosine_part, complex_pair[0]) - along_rows(sine_part, complex_pair[1])
    imag_part = along_rows(cosine_part, complex_pair[1]) + along_rows(sine_part, complex_pair[0])
    return (real_part * norming, imag_part * norming)


def complex_product(first_pair, second_pair):
    return (
        first_pair[0] * second_pair[0] - first_pair[1] * second_pair[1],
        first_pair[0] * second_pair[1] + first_pair[1] * second_pair[0],
    )


def conj_product(first_pair, second_pair):
    return (
        first_pair[0] * second_pair[0] + first_pair[1] * second_pair[1],
        first_pair[0] * second_pair[1] - first_pair[1] * second_pair[0],
    )


def on_device(
    query_proj, key_proj, value_proj, short_filter, long_filter, skip_gain, out_weight, cotangent
):
    block_rows = query_proj.shape[0]
    tap_count = short_filter.shape[1]
    block_count = lax.axis_size("seq")
    streams = jnp.stack([query_proj, key_proj, value_proj])
    earlier = from_behind(streams[:, block_rows - (tap_count - 1) :], "seq", 1)
    extended = jnp.concatenate([earlier, streams], axis=1).astype(jnp.float32)
    shifted = [
        extended[:, tap_count - 1 - offset : tap_count - 1 - offset + block_rows]
        for offset in range(tap_count)
    ]
    filtered = sum(
        (short_filter[:, offset][:, None, :] * shifted[offset] for offset in range(tap_count))
    )
    query_short, key_short, value_short = (filtered[0], filtered[1], filtered[2])
    product = key_short * value_short
    forward_basis = tables(2 * block_rows, block_rows, 2 * block_rows)
    full_basis = tables(2 * block_rows, 2 * block_rows, 2 * block_rows)
    half_basis = tables(block_rows, 2 * block_rows, 2 * block_rows)
    block_basis = tables(2 * block_count, block_count, 2 * block_count)
    return_basis = tables(block_count, 2 * block_count, 2 * block_count)
    input_pair = rows_spectrum(product, forward_basis)
    filter_pair = rows_spectrum(long_filter, forward_basis)
    moved_data = (
        lax.all_to_all(input_pair[0][None], "seq", split_axis=1, concat_axis=0, tiled=True),
        lax.all_to_all(input_pair[1][None], "seq", split_axis=1, concat_axis=0, tiled=True),
        lax.all_to_all(filter_pair[0][None], "seq", split_axis=1, concat_axis=0, tiled=True),
        lax.all_to_all(filter_pair[1][None], "seq", split_axis=1, concat_axis=0, tiled=True),
    )
    input_spectrum = block_forward((moved_data[0], moved_data[1]), block_basis)
    filter_spectrum = block_forward((moved_data[2], moved_data[3]), block_basis)
    inverse_pair = block_inverse(complex_product(filter_spectrum, input_spectrum), return_basis)
    returned = (
        lax.all_to_all(inverse_pair[0], "seq", split_axis=0, concat_axis=1, tiled=True),
        lax.all_to_all(inverse_pair[1], "seq", split_axis=0, concat_axis=1, tiled=True),
    )
    folded = rows_inverse((returned[0][0], returned[1][0]), full_basis)
    carried = from_behind(folded[block_rows:], "seq", 1)
    convolved = folded[:block_rows] + carried
    mixed_seq = convolved + skip_gain * product
    gated_values = (query_short * mixed_seq).astype(jnp.bfloat16)
    partial_value = jnp.dot(gated_values, out_weight, preferred_element_type=jnp.float32)
    layer_out = lax.psum_scatter(partial_value, "ch", scatter_dimension=1, tiled=True).astype(
        jnp.bfloat16
    )
    full_cotangent = lax.all_gather(cotangent, "ch", axis=1, tiled=True)
    grad_gated = lax.dot_general(
        full_cotangent, out_weight, (((1,), (1,)), ((), ())), preferred_element_type=jnp.float32
    )
    weight_terms = lax.dot_general(
        full_cotangent,
        gated_values,
        (((0,), (0,)), ((), ())),
        preferred_element_type=jnp.float32,
    )
    grad_mixed = grad_gated * query_short
    grad_query_short = grad_gated * mixed_seq
    following = from_behind(grad_mixed.astype(jnp.bfloat16), "seq", -1).astype(grad_mixed.dtype)
    spread = jnp.concatenate([grad_mixed, following], axis=0)
    grad_pair = rows_spectrum(spread, full_basis)
    moved_grad = (
        lax.all_to_all(
            grad_pair[0][None].astype(jnp.bfloat16), "seq", split_axis=1, concat_axis=0, tiled=True
        ).astype(jnp.float32),
        lax.all_to_all(
            grad_pair[1][None].astype(jnp.bfloat16), "seq", split_axis=1, concat_axis=0, tiled=True
        ).astype(jnp.float32),
    )
    grad_spectrum = block_forward(moved_grad, block_basis)
    input_back = block_inverse(conj_product(filter_spectrum, grad_spectrum), return_basis)
    filter_back = block_inverse(conj_product(input_spectrum, grad_spectrum), return_basis)
    returned_grad = (
        lax.all_to_all(as_sent(input_back[0]), "seq", split_axis=0, concat_axis=1, tiled=True),
        lax.all_to_all(as_sent(input_back[1]), "seq", split_axis=0, concat_axis=1, tiled=True),
        lax.all_to_all(as_sent(filter_back[0]), "seq", split_axis=0, concat_axis=1, tiled=True),
        lax.all_to_all(as_sent(filter_back[1]), "seq", split_axis=0, concat_axis=1, tiled=True),
    )
    conv_grad = rows_inverse((returned_grad[0][0], returned_grad[1][0]), half_basis)
    grad_filter = rows_inverse((returned_grad[2][0], returned_grad[3][0]), half_basis)
    grad_product = conv_grad + skip_gain * grad_mixed
    grad_streams = jnp.stack(
        [grad_query_short, grad_product * value_short, grad_product * key_short]
    )
    later_rows = from_behind(grad_streams[:, : tap_count - 1], "seq", -1)
    padded_grad = jnp.concatenate([grad_streams, later_rows], axis=1)
    grad_inputs = sum(
        (
            short_filter[:, offset][:, None, :] * padded_grad[:, offset : offset + block_rows]
            for offset in range(tap_count)
        )
    )
    short_terms = jnp.stack(
        [jnp.sum(grad_streams * shifted[offset], axis=1) for offset in range(tap_count)], axis=1
    )
    skip_terms = jnp.sum(grad_mixed * product, axis=0)
    channel_count = skip_terms.shape[0]
    sum_rows = short_terms.shape[0] * short_terms.shape[1] + 1
    padded_rows = -(-sum_rows // 8) * 8
    small_terms = jnp.concatenate(
        [
            short_terms.reshape(sum_rows - 1, channel_count),
            skip_terms[None],
            jnp.zeros((padded_rows - sum_rows, channel_count), jnp.float32),
        ]
    )
    weight_blocks = weight_terms.reshape(block_count, -1, channel_count)
    block_height = weight_blocks.shape[1]
    combined = jnp.concatenate(
        [weight_blocks, jnp.broadcast_to(small_terms, (block_count, padded_rows, channel_count))],
        axis=1,
    )
    reduced = lax.psum_scatter(
        combined.reshape(-1, channel_count), "seq", scatter_dimension=0, tiled=True
    )
    grad_w_out_t = reduced[:block_height]
    grad_short = reduced[block_height : block_height + sum_rows - 1].reshape(short_terms.shape)
    grad_skip = reduced[block_height + sum_rows - 1]
    return (
        layer_out,
        grad_inputs[0],
        grad_inputs[1],
        grad_inputs[2],
        grad_short,
        grad_filter,
        grad_skip,
        grad_w_out_t,
    )


def solution(mesh):
    in_specs = (
        P("seq", "ch"),
        P("seq", "ch"),
        P("seq", "ch"),
        P(None, None, "ch"),
        P("seq", "ch"),
        P("ch"),
        P("ch", None),
        P("seq", "ch"),
    )
    out_specs = (
        P("seq", "ch"),
        P("seq", "ch"),
        P("seq", "ch"),
        P("seq", "ch"),
        P(None, None, "ch"),
        P("seq", "ch"),
        P("ch"),
        P("seq", "ch"),
    )
    return jax.shard_map(
        on_device, mesh=mesh, in_specs=in_specs, out_specs=out_specs, check_vma=False
    )
```

```python
import math

import jax
import jax.numpy as jnp
from jax import lax
from jax.sharding import PartitionSpec as P

exact_mode = lax.Precision.HIGHEST


def from_behind(shard, axis, by):
    size = lax.axis_size(axis)
    pairs = [(i, i + by) for i in range(size) if 0 <= i + by < size]
    return lax.ppermute(shard, axis, pairs)


def as_sent(shard):

    def short(part):
        return part.astype(jnp.bfloat16) if part.dtype == jnp.float32 else part

    return jax.tree.map(short, shard)


def split_lanes(merged, lanes):
    return tuple(
        merged[..., start : start + lanes] for start in range(0, merged.shape[-1], lanes)
    )


def tables(rows_out, cols_in, period):
    row_index = lax.broadcasted_iota(jnp.int32, (rows_out, cols_in), 0)
    col_index = lax.broadcasted_iota(jnp.int32, (rows_out, cols_in), 1)
    phase_angle = (row_index * col_index % period).astype(jnp.float32) * (2.0 * math.pi / period)
    return (jnp.cos(phase_angle), jnp.sin(phase_angle))


def along_rows(factor, values):
    return jnp.tensordot(factor, values, axes=1, precision=exact_mode)


def rows_spectrum(signal, basis_pair):
    return (along_rows(basis_pair[0], signal), -along_rows(basis_pair[1], signal))


def rows_inverse(complex_pair, basis_pair):
    total = along_rows(basis_pair[0], complex_pair[0]) - along_rows(basis_pair[1], complex_pair[1])
    return total / basis_pair[0].shape[1]


def block_forward(complex_pair, basis_pair):
    cosine_part, sine_part = basis_pair
    real_part = along_rows(cosine_part, complex_pair[0]) + along_rows(sine_part, complex_pair[1])
    imag_part = along_rows(cosine_part, complex_pair[1]) - along_rows(sine_part, complex_pair[0])
    return (real_part, imag_part)


def block_inverse(complex_pair, basis_pair):
    cosine_part, sine_part = basis_pair
    norming = 1.0 / cosine_part.shape[1]
    real_part = along_rows(cosine_part, complex_pair[0]) - along_rows(sine_part, complex_pair[1])
    imag_part = along_rows(cosine_part, complex_pair[1]) + along_rows(sine_part, complex_pair[0])
    return (real_part * norming, imag_part * norming)


def complex_product(first_pair, second_pair):
    return (
        first_pair[0] * second_pair[0] - first_pair[1] * second_pair[1],
        first_pair[0] * second_pair[1] + first_pair[1] * second_pair[0],
    )


def conj_product(first_pair, second_pair):
    return (
        first_pair[0] * second_pair[0] + first_pair[1] * second_pair[1],
        first_pair[0] * second_pair[1] - first_pair[1] * second_pair[0],
    )


def on_device(
    query_proj, key_proj, value_proj, short_filter, long_filter, skip_gain, out_weight, cotangent
):
    block_rows = query_proj.shape[0]
    tap_count = short_filter.shape[1]
    block_count = lax.axis_size("seq")
    streams = jnp.stack([query_proj, key_proj, value_proj])
    earlier = from_behind(streams[:, block_rows - (tap_count - 1) :], "seq", 1)
    extended = jnp.concatenate([earlier, streams], axis=1).astype(jnp.float32)
    shifted = [
        extended[:, tap_count - 1 - offset : tap_count - 1 - offset + block_rows]
        for offset in range(tap_count)
    ]
    filtered = sum(
        (short_filter[:, offset][:, None, :] * shifted[offset] for offset in range(tap_count))
    )
    query_short, key_short, value_short = (filtered[0], filtered[1], filtered[2])
    product = key_short * value_short
    forward_basis = tables(2 * block_rows, block_rows, 2 * block_rows)
    full_basis = tables(2 * block_rows, 2 * block_rows, 2 * block_rows)
    half_basis = tables(block_rows, 2 * block_rows, 2 * block_rows)
    block_basis = tables(2 * block_count, block_count, 2 * block_count)
    return_basis = tables(block_count, 2 * block_count, 2 * block_count)
    input_pair = rows_spectrum(product, forward_basis)
    filter_pair = rows_spectrum(long_filter, forward_basis)
    lanes = product.shape[1]
    moved_data = split_lanes(
        lax.all_to_all(
            jnp.concatenate([input_pair[0], input_pair[1], filter_pair[0], filter_pair[1]], axis=1)[
                None
            ],
            "seq",
            split_axis=1,
            concat_axis=0,
            tiled=True,
        ),
        lanes,
    )
    input_spectrum = block_forward((moved_data[0], moved_data[1]), block_basis)
    filter_spectrum = block_forward((moved_data[2], moved_data[3]), block_basis)
    inverse_pair = block_inverse(complex_product(filter_spectrum, input_spectrum), return_basis)
    returned = split_lanes(
        lax.all_to_all(
            jnp.concatenate(inverse_pair, axis=-1), "seq", split_axis=0, concat_axis=1, tiled=True
        ),
        lanes,
    )
    folded = rows_inverse((returned[0][0], returned[1][0]), full_basis)
    carried = from_behind(folded[block_rows:], "seq", 1)
    convolved = folded[:block_rows] + carried
    mixed_seq = convolved + skip_gain * product
    gated_values = (query_short * mixed_seq).astype(jnp.bfloat16)
    partial_value = jnp.dot(gated_values, out_weight, preferred_element_type=jnp.float32)
    layer_out = lax.psum_scatter(partial_value, "ch", scatter_dimension=1, tiled=True).astype(
        jnp.bfloat16
    )
    full_cotangent = lax.all_gather(cotangent, "ch", axis=1, tiled=True)
    grad_gated = lax.dot_general(
        full_cotangent, out_weight, (((1,), (1,)), ((), ())), preferred_element_type=jnp.float32
    )
    weight_terms = lax.dot_general(
        full_cotangent,
        gated_values,
        (((0,), (0,)), ((), ())),
        preferred_element_type=jnp.float32,
    )
    grad_mixed = grad_gated * query_short
    grad_query_short = grad_gated * mixed_seq
    following = from_behind(grad_mixed.astype(jnp.bfloat16), "seq", -1).astype(grad_mixed.dtype)
    spread = jnp.concatenate([grad_mixed, following], axis=0)
    grad_pair = rows_spectrum(spread, full_basis)
    moved_grad = split_lanes(
        lax.all_to_all(
            jnp.concatenate(grad_pair, axis=1)[None].astype(jnp.bfloat16),
            "seq",
            split_axis=1,
            concat_axis=0,
            tiled=True,
        ).astype(jnp.float32),
        lanes,
    )
    grad_spectrum = block_forward(moved_grad, block_basis)
    input_back = block_inverse(conj_product(filter_spectrum, grad_spectrum), return_basis)
    filter_back = block_inverse(conj_product(input_spectrum, grad_spectrum), return_basis)
    returned_grad = split_lanes(
        lax.all_to_all(
            as_sent(jnp.concatenate(input_back + filter_back, axis=-1)),
            "seq",
            split_axis=0,
            concat_axis=1,
            tiled=True,
        ),
        lanes,
    )
    conv_grad = rows_inverse((returned_grad[0][0], returned_grad[1][0]), half_basis)
    grad_filter = rows_inverse((returned_grad[2][0], returned_grad[3][0]), half_basis)
    grad_product = conv_grad + skip_gain * grad_mixed
    grad_streams = jnp.stack(
        [grad_query_short, grad_product * value_short, grad_product * key_short]
    )
    later_rows = from_behind(grad_streams[:, : tap_count - 1], "seq", -1)
    padded_grad = jnp.concatenate([grad_streams, later_rows], axis=1)
    grad_inputs = sum(
        (
            short_filter[:, offset][:, None, :] * padded_grad[:, offset : offset + block_rows]
            for offset in range(tap_count)
        )
    )
    short_terms = jnp.stack(
        [jnp.sum(grad_streams * shifted[offset], axis=1) for offset in range(tap_count)], axis=1
    )
    skip_terms = jnp.sum(grad_mixed * product, axis=0)
    channel_count = skip_terms.shape[0]
    sum_rows = short_terms.shape[0] * short_terms.shape[1] + 1
    padded_rows = -(-sum_rows // 8) * 8
    small_terms = jnp.concatenate(
        [
            short_terms.reshape(sum_rows - 1, channel_count),
            skip_terms[None],
            jnp.zeros((padded_rows - sum_rows, channel_count), jnp.float32),
        ]
    )
    weight_blocks = weight_terms.reshape(block_count, -1, channel_count)
    block_height = weight_blocks.shape[1]
    combined = jnp.concatenate(
        [weight_blocks, jnp.broadcast_to(small_terms, (block_count, padded_rows, channel_count))],
        axis=1,
    )
    reduced = lax.psum_scatter(
        combined.reshape(-1, channel_count), "seq", scatter_dimension=0, tiled=True
    )
    grad_w_out_t = reduced[:block_height]
    grad_short = reduced[block_height : block_height + sum_rows - 1].reshape(short_terms.shape)
    grad_skip = reduced[block_height + sum_rows - 1]
    return (
        layer_out,
        grad_inputs[0],
        grad_inputs[1],
        grad_inputs[2],
        grad_short,
        grad_filter,
        grad_skip,
        grad_w_out_t,
    )


def solution(mesh):
    in_specs = (
        P("seq", "ch"),
        P("seq", "ch"),
        P("seq", "ch"),
        P(None, None, "ch"),
        P("seq", "ch"),
        P("ch"),
        P("ch", None),
        P("seq", "ch"),
    )
    out_specs = (
        P("seq", "ch"),
        P("seq", "ch"),
        P("seq", "ch"),
        P("seq", "ch"),
        P(None, None, "ch"),
        P("seq", "ch"),
        P("ch"),
        P("seq", "ch"),
    )
    return jax.shard_map(
        on_device, mesh=mesh, in_specs=in_specs, out_specs=out_specs, check_vma=False
    )
```

```python
import functools
import math

import jax
import jax.numpy as jnp
from jax import lax
from jax.experimental import pallas as pl
from jax.experimental.pallas import tpu as pltpu
from jax.sharding import PartitionSpec as P

exact_mode = lax.Precision.HIGHEST
SEQ = ("seq_hi", "seq_lo")


def from_behind(shard, axis, by):
    size = lax.axis_size(axis)
    pairs = [(i, i + by) for i in range(size) if 0 <= i + by < size]
    return lax.ppermute(shard, axis, pairs)


def as_sent(shard):

    def short(part):
        return part.astype(jnp.bfloat16) if part.dtype == jnp.float32 else part

    return jax.tree.map(short, shard)


def gather_sum_kernel(count, part_ref, out_ref, slots, local_sem, send_sems, recv_sems):
    me = lax.axis_index(SEQ)
    inner = lax.axis_size("seq_lo")
    group = lax.axis_index("ch")
    own = pltpu.make_async_copy(part_ref, slots.at[me], local_sem)
    own.start()

    def send(step, carry):
        peer = lax.rem(me + step, count)
        pltpu.make_async_remote_copy(
            src_ref=part_ref,
            dst_ref=slots.at[me],
            send_sem=send_sems.at[step],
            recv_sem=recv_sems.at[me],
            device_id=(peer // inner, peer % inner, group),
            device_id_type=pl.DeviceIdType.MESH,
        ).start()
        return carry

    lax.fori_loop(1, count, send, 0)
    own.wait()

    def finish(step, carry):
        peer = lax.rem(me + step, count)
        source = lax.rem(me + count - step, count)
        pltpu.make_async_remote_copy(
            src_ref=part_ref,
            dst_ref=slots.at[me],
            send_sem=send_sems.at[step],
            recv_sem=recv_sems.at[me],
            device_id=(peer // inner, peer % inner, group),
            device_id_type=pl.DeviceIdType.MESH,
        ).wait_send()
        pltpu.make_async_remote_copy(
            src_ref=part_ref,
            dst_ref=slots.at[source],
            send_sem=send_sems.at[step],
            recv_sem=recv_sems.at[source],
            device_id=(source // inner, source % inner, group),
            device_id_type=pl.DeviceIdType.MESH,
        ).wait_recv()
        return carry

    lax.fori_loop(1, count, finish, 0)

    def accumulate(slot, total):
        return total + slots[slot]

    out_ref[...] = lax.fori_loop(1, count, accumulate, slots[0])


def sum_over_seq(part):
    count = lax.axis_size(SEQ)
    return pl.pallas_call(
        functools.partial(gather_sum_kernel, count),
        out_shape=jax.ShapeDtypeStruct(part.shape, part.dtype),
        in_specs=[pl.BlockSpec(memory_space=pltpu.VMEM)],
        out_specs=pl.BlockSpec(memory_space=pltpu.VMEM),
        scratch_shapes=[
            pltpu.VMEM((count,) + part.shape, part.dtype),
            pltpu.SemaphoreType.DMA(()),
            pltpu.SemaphoreType.DMA((count,)),
            pltpu.SemaphoreType.DMA((count,)),
        ],
        compiler_params=pltpu.CompilerParams(has_side_effects=True),
    )(part)


def split_lanes(merged, lanes):
    return tuple(
        merged[..., start : start + lanes] for start in range(0, merged.shape[-1], lanes)
    )


def tables(rows_out, cols_in, period):
    row_index = lax.broadcasted_iota(jnp.int32, (rows_out, cols_in), 0)
    col_index = lax.broadcasted_iota(jnp.int32, (rows_out, cols_in), 1)
    phase_angle = (row_index * col_index % period).astype(jnp.float32) * (2.0 * math.pi / period)
    return (jnp.cos(phase_angle), jnp.sin(phase_angle))


def along_rows(factor, values):
    return jnp.tensordot(factor, values, axes=1, precision=exact_mode)


def rows_spectrum(signal, basis_pair):
    return (along_rows(basis_pair[0], signal), -along_rows(basis_pair[1], signal))


def rows_inverse(complex_pair, basis_pair):
    total = along_rows(basis_pair[0], complex_pair[0]) - along_rows(basis_pair[1], complex_pair[1])
    return total / basis_pair[0].shape[1]


def block_forward(complex_pair, basis_pair):
    cosine_part, sine_part = basis_pair
    real_part = along_rows(cosine_part, complex_pair[0]) + along_rows(sine_part, complex_pair[1])
    imag_part = along_rows(cosine_part, complex_pair[1]) - along_rows(sine_part, complex_pair[0])
    return (real_part, imag_part)


def block_inverse(complex_pair, basis_pair):
    cosine_part, sine_part = basis_pair
    norming = 1.0 / cosine_part.shape[1]
    real_part = along_rows(cosine_part, complex_pair[0]) - along_rows(sine_part, complex_pair[1])
    imag_part = along_rows(cosine_part, complex_pair[1]) + along_rows(sine_part, complex_pair[0])
    return (real_part * norming, imag_part * norming)


def complex_product(first_pair, second_pair):
    return (
        first_pair[0] * second_pair[0] - first_pair[1] * second_pair[1],
        first_pair[0] * second_pair[1] + first_pair[1] * second_pair[0],
    )


def conj_product(first_pair, second_pair):
    return (
        first_pair[0] * second_pair[0] + first_pair[1] * second_pair[1],
        first_pair[0] * second_pair[1] - first_pair[1] * second_pair[0],
    )


def on_device(
    query_proj, key_proj, value_proj, short_filter, long_filter, skip_gain, out_weight, cotangent
):
    block_rows = query_proj.shape[0]
    tap_count = short_filter.shape[1]
    block_count = lax.axis_size(SEQ)
    streams = jnp.stack([query_proj, key_proj, value_proj])
    earlier = from_behind(streams[:, block_rows - (tap_count - 1) :], SEQ, 1)
    extended = jnp.concatenate([earlier, streams], axis=1).astype(jnp.float32)
    shifted = [
        extended[:, tap_count - 1 - offset : tap_count - 1 - offset + block_rows]
        for offset in range(tap_count)
    ]
    filtered = sum(
        (short_filter[:, offset][:, None, :] * shifted[offset] for offset in range(tap_count))
    )
    query_short, key_short, value_short = (filtered[0], filtered[1], filtered[2])
    product = key_short * value_short
    forward_basis = tables(2 * block_rows, block_rows, 2 * block_rows)
    full_basis = tables(2 * block_rows, 2 * block_rows, 2 * block_rows)
    half_basis = tables(block_rows, 2 * block_rows, 2 * block_rows)
    block_basis = tables(2 * block_count, block_count, 2 * block_count)
    return_basis = tables(block_count, 2 * block_count, 2 * block_count)
    input_pair = rows_spectrum(product, forward_basis)
    filter_pair = rows_spectrum(long_filter, forward_basis)
    lanes = product.shape[1]
    moved_data = split_lanes(
        lax.all_to_all(
            jnp.concatenate([input_pair[0], input_pair[1], filter_pair[0], filter_pair[1]], axis=1)[
                None
            ],
            SEQ,
            split_axis=1,
            concat_axis=0,
            tiled=True,
        ),
        lanes,
    )
    input_spectrum = block_forward((moved_data[0], moved_data[1]), block_basis)
    filter_spectrum = block_forward((moved_data[2], moved_data[3]), block_basis)
    inverse_pair = block_inverse(complex_product(filter_spectrum, input_spectrum), return_basis)
    returned = split_lanes(
        lax.all_to_all(
            jnp.concatenate(inverse_pair, axis=-1), SEQ, split_axis=0, concat_axis=1, tiled=True
        ),
        lanes,
    )
    folded = rows_inverse((returned[0][0], returned[1][0]), full_basis)
    carried = from_behind(folded[block_rows:], SEQ, 1)
    convolved = folded[:block_rows] + carried
    mixed_seq = convolved + skip_gain * product
    gated_values = (query_short * mixed_seq).astype(jnp.bfloat16)
    partial_value = jnp.dot(gated_values, out_weight, preferred_element_type=jnp.float32)
    layer_out = lax.psum_scatter(partial_value, "ch", scatter_dimension=1, tiled=True).astype(
        jnp.bfloat16
    )
    full_cotangent = lax.all_gather(cotangent, "ch", axis=1, tiled=True)
    grad_gated = lax.dot_general(
        full_cotangent, out_weight, (((1,), (1,)), ((), ())), preferred_element_type=jnp.float32
    )
    inner = lax.axis_size("seq_lo")
    feature_rows = full_cotangent.shape[1] // (block_count // inner) // inner
    local_rows = lax.all_gather(gated_values, "seq_lo", axis=0, tiled=True)
    local_features = lax.all_to_all(
        full_cotangent.reshape(block_rows, block_count // inner, inner, feature_rows),
        "seq_lo",
        split_axis=2,
        concat_axis=0,
        tiled=True,
    ).reshape(block_rows * inner, -1)
    grad_w_out_t = lax.psum_scatter(
        lax.dot_general(
            local_features,
            local_rows,
            (((0,), (0,)), ((), ())),
            preferred_element_type=jnp.float32,
        ),
        "seq_hi",
        scatter_dimension=0,
        tiled=True,
    )
    grad_mixed = grad_gated * query_short
    grad_query_short = grad_gated * mixed_seq
    following = from_behind(grad_mixed.astype(jnp.bfloat16), SEQ, -1).astype(grad_mixed.dtype)
    spread = jnp.concatenate([grad_mixed, following], axis=0)
    grad_pair = rows_spectrum(spread, full_basis)
    moved_grad = split_lanes(
        lax.all_to_all(
            jnp.concatenate(grad_pair, axis=1)[None].astype(jnp.bfloat16),
            SEQ,
            split_axis=1,
            concat_axis=0,
            tiled=True,
        ).astype(jnp.float32),
        lanes,
    )
    grad_spectrum = block_forward(moved_grad, block_basis)
    input_back = block_inverse(conj_product(filter_spectrum, grad_spectrum), return_basis)
    filter_back = block_inverse(conj_product(input_spectrum, grad_spectrum), return_basis)
    returned_grad = split_lanes(
        lax.all_to_all(
            as_sent(jnp.concatenate(input_back + filter_back, axis=-1)),
            SEQ,
            split_axis=0,
            concat_axis=1,
            tiled=True,
        ),
        lanes,
    )
    conv_grad = rows_inverse((returned_grad[0][0], returned_grad[1][0]), half_basis)
    grad_filter = rows_inverse((returned_grad[2][0], returned_grad[3][0]), half_basis)
    grad_product = conv_grad + skip_gain * grad_mixed
    grad_streams = jnp.stack(
        [grad_query_short, grad_product * value_short, grad_product * key_short]
    )
    later_rows = from_behind(grad_streams[:, : tap_count - 1], SEQ, -1)
    padded_grad = jnp.concatenate([grad_streams, later_rows], axis=1)
    grad_inputs = sum(
        (
            short_filter[:, offset][:, None, :] * padded_grad[:, offset : offset + block_rows]
            for offset in range(tap_count)
        )
    )
    short_terms = jnp.stack(
        [jnp.sum(grad_streams * shifted[offset], axis=1) for offset in range(tap_count)], axis=1
    )
    skip_terms = jnp.sum(grad_mixed * product, axis=0)
    channel_count = skip_terms.shape[0]
    sum_rows = short_terms.shape[0] * short_terms.shape[1] + 1
    padded_rows = -(-sum_rows // 8) * 8
    small_terms = jnp.concatenate(
        [
            short_terms.reshape(sum_rows - 1, channel_count),
            skip_terms[None],
            jnp.zeros((padded_rows - sum_rows, channel_count), jnp.float32),
        ]
    )
    summed = sum_over_seq(small_terms)
    grad_short = summed[: sum_rows - 1].reshape(short_terms.shape)
    grad_skip = summed[sum_rows - 1]
    return (
        layer_out,
        grad_inputs[0],
        grad_inputs[1],
        grad_inputs[2],
        grad_short,
        grad_filter,
        grad_skip,
        grad_w_out_t,
    )


def solution(mesh):
    in_specs = (
        P(SEQ, "ch"),
        P(SEQ, "ch"),
        P(SEQ, "ch"),
        P(None, None, "ch"),
        P(SEQ, "ch"),
        P("ch"),
        P("ch", None),
        P(SEQ, "ch"),
    )
    out_specs = (
        P(SEQ, "ch"),
        P(SEQ, "ch"),
        P(SEQ, "ch"),
        P(SEQ, "ch"),
        P(None, None, "ch"),
        P(SEQ, "ch"),
        P("ch"),
        P(SEQ, "ch"),
    )
    inner = 8
    seq_mesh = jax.sharding.Mesh(
        mesh.devices.reshape(mesh.shape["seq"] // inner, inner, mesh.shape["ch"]),
        ("seq_hi", "seq_lo", "ch"),
    )
    return jax.shard_map(
        on_device, mesh=seq_mesh, in_specs=in_specs, out_specs=out_specs, check_vma=False
    )
```

```python
import functools
import math

import jax
import jax.numpy as jnp
from jax import lax
from jax.experimental import pallas as pl
from jax.experimental.pallas import tpu as pltpu
from jax.sharding import PartitionSpec as P

exact_mode = lax.Precision.HIGHEST
SEQ = ("seq_hi", "seq_lo")


def from_behind(shard, axis, by):
    size = lax.axis_size(axis)
    pairs = [(i, i + by) for i in range(size) if 0 <= i + by < size]
    return lax.ppermute(shard, axis, pairs)


def as_sent(shard):

    def short(part):
        return part.astype(jnp.bfloat16) if part.dtype == jnp.float32 else part

    return jax.tree.map(short, shard)


def group_sum_kernel(axis, blocks_ref, out_ref, slots, local_sem, send_sems, recv_sems):
    count = lax.axis_size(axis)
    me = lax.axis_index(axis)
    place = {"seq_hi": lax.axis_index("seq_hi"), "seq_lo": lax.axis_index("seq_lo")}

    def member(index):
        where = dict(place, **{axis: index})
        return (where["seq_hi"], where["seq_lo"], lax.axis_index("ch"))

    barrier = pltpu.get_barrier_semaphore()
    for step in range(1, count):
        pl.semaphore_signal(
            barrier,
            1,
            device_id=member(lax.rem(me + step, count)),
            device_id_type=pl.DeviceIdType.MESH,
        )
    pl.semaphore_wait(barrier, count - 1)
    own = pltpu.make_async_copy(blocks_ref.at[me], slots.at[me], local_sem)
    own.start()
    outgoing = []
    for step in range(1, count):
        peer = lax.rem(me + step, count)
        copy = pltpu.make_async_remote_copy(
            src_ref=blocks_ref.at[peer],
            dst_ref=slots.at[me],
            send_sem=send_sems.at[step],
            recv_sem=recv_sems.at[me],
            device_id=member(peer),
            device_id_type=pl.DeviceIdType.MESH,
        )
        copy.start()
        outgoing.append(copy)
    own.wait()
    for step in range(1, count):
        source = lax.rem(me + count - step, count)
        outgoing[step - 1].wait_send()
        pltpu.make_async_remote_copy(
            src_ref=blocks_ref.at[source],
            dst_ref=slots.at[source],
            send_sem=send_sems.at[step],
            recv_sem=recv_sems.at[source],
            device_id=member(source),
            device_id_type=pl.DeviceIdType.MESH,
        ).wait_recv()
    total = slots[0]
    for slot in range(1, count):
        total = total + slots[slot]
    out_ref[...] = total


def sum_over_group(blocks, axis, kernel_id):
    count = blocks.shape[0]
    return pl.pallas_call(
        functools.partial(group_sum_kernel, axis),
        out_shape=jax.ShapeDtypeStruct(blocks.shape[1:], blocks.dtype),
        in_specs=[pl.BlockSpec(memory_space=pltpu.VMEM)],
        out_specs=pl.BlockSpec(memory_space=pltpu.VMEM),
        scratch_shapes=[
            pltpu.VMEM(blocks.shape, blocks.dtype),
            pltpu.SemaphoreType.DMA(()),
            pltpu.SemaphoreType.DMA((count,)),
            pltpu.SemaphoreType.DMA((count,)),
        ],
        compiler_params=pltpu.CompilerParams(collective_id=kernel_id, has_side_effects=True),
    )(blocks)


def split_lanes(merged, lanes):
    return tuple(
        merged[..., start : start + lanes] for start in range(0, merged.shape[-1], lanes)
    )


def tables(rows_out, cols_in, period):
    row_index = lax.broadcasted_iota(jnp.int32, (rows_out, cols_in), 0)
    col_index = lax.broadcasted_iota(jnp.int32, (rows_out, cols_in), 1)
    phase_angle = (row_index * col_index % period).astype(jnp.float32) * (2.0 * math.pi / period)
    return (jnp.cos(phase_angle), jnp.sin(phase_angle))


def along_rows(factor, values):
    return jnp.tensordot(factor, values, axes=1, precision=exact_mode)


def rows_spectrum(signal, basis_pair):
    return (along_rows(basis_pair[0], signal), -along_rows(basis_pair[1], signal))


def rows_inverse(complex_pair, basis_pair):
    total = along_rows(basis_pair[0], complex_pair[0]) - along_rows(basis_pair[1], complex_pair[1])
    return total / basis_pair[0].shape[1]


def block_forward(complex_pair, basis_pair):
    cosine_part, sine_part = basis_pair
    real_part = along_rows(cosine_part, complex_pair[0]) + along_rows(sine_part, complex_pair[1])
    imag_part = along_rows(cosine_part, complex_pair[1]) - along_rows(sine_part, complex_pair[0])
    return (real_part, imag_part)


def block_inverse(complex_pair, basis_pair):
    cosine_part, sine_part = basis_pair
    norming = 1.0 / cosine_part.shape[1]
    real_part = along_rows(cosine_part, complex_pair[0]) - along_rows(sine_part, complex_pair[1])
    imag_part = along_rows(cosine_part, complex_pair[1]) + along_rows(sine_part, complex_pair[0])
    return (real_part * norming, imag_part * norming)


def complex_product(first_pair, second_pair):
    return (
        first_pair[0] * second_pair[0] - first_pair[1] * second_pair[1],
        first_pair[0] * second_pair[1] + first_pair[1] * second_pair[0],
    )


def conj_product(first_pair, second_pair):
    return (
        first_pair[0] * second_pair[0] + first_pair[1] * second_pair[1],
        first_pair[0] * second_pair[1] - first_pair[1] * second_pair[0],
    )


def on_device(
    query_proj, key_proj, value_proj, short_filter, long_filter, skip_gain, out_weight, cotangent
):
    block_rows = query_proj.shape[0]
    tap_count = short_filter.shape[1]
    block_count = lax.axis_size(SEQ)
    streams = jnp.stack([query_proj, key_proj, value_proj])
    earlier = from_behind(streams[:, block_rows - (tap_count - 1) :], SEQ, 1)
    extended = jnp.concatenate([earlier, streams], axis=1).astype(jnp.float32)
    shifted = [
        extended[:, tap_count - 1 - offset : tap_count - 1 - offset + block_rows]
        for offset in range(tap_count)
    ]
    filtered = sum(
        (short_filter[:, offset][:, None, :] * shifted[offset] for offset in range(tap_count))
    )
    query_short, key_short, value_short = (filtered[0], filtered[1], filtered[2])
    product = key_short * value_short
    forward_basis = tables(2 * block_rows, block_rows, 2 * block_rows)
    full_basis = tables(2 * block_rows, 2 * block_rows, 2 * block_rows)
    half_basis = tables(block_rows, 2 * block_rows, 2 * block_rows)
    block_basis = tables(2 * block_count, block_count, 2 * block_count)
    return_basis = tables(block_count, 2 * block_count, 2 * block_count)
    input_pair = rows_spectrum(product, forward_basis)
    filter_pair = rows_spectrum(long_filter, forward_basis)
    lanes = product.shape[1]
    moved_data = split_lanes(
        lax.all_to_all(
            jnp.concatenate([input_pair[0], input_pair[1], filter_pair[0], filter_pair[1]], axis=1)[
                None
            ],
            SEQ,
            split_axis=1,
            concat_axis=0,
            tiled=True,
        ),
        lanes,
    )
    input_spectrum = block_forward((moved_data[0], moved_data[1]), block_basis)
    filter_spectrum = block_forward((moved_data[2], moved_data[3]), block_basis)
    inverse_pair = block_inverse(complex_product(filter_spectrum, input_spectrum), return_basis)
    returned = split_lanes(
        lax.all_to_all(
            jnp.concatenate(inverse_pair, axis=-1), SEQ, split_axis=0, concat_axis=1, tiled=True
        ),
        lanes,
    )
    folded = rows_inverse((returned[0][0], returned[1][0]), full_basis)
    carried = from_behind(folded[block_rows:], SEQ, 1)
    convolved = folded[:block_rows] + carried
    mixed_seq = convolved + skip_gain * product
    gated_values = (query_short * mixed_seq).astype(jnp.bfloat16)
    partial_value = jnp.dot(gated_values, out_weight, preferred_element_type=jnp.float32)
    layer_out = lax.psum_scatter(partial_value, "ch", scatter_dimension=1, tiled=True).astype(
        jnp.bfloat16
    )
    full_cotangent = lax.all_gather(cotangent, "ch", axis=1, tiled=True)
    grad_gated = lax.dot_general(
        full_cotangent, out_weight, (((1,), (1,)), ((), ())), preferred_element_type=jnp.float32
    )
    inner = lax.axis_size("seq_lo")
    feature_rows = full_cotangent.shape[1] // (block_count // inner) // inner
    local_rows = lax.all_gather(gated_values, "seq_lo", axis=0, tiled=True)
    local_features = lax.all_to_all(
        full_cotangent.reshape(block_rows, block_count // inner, inner, feature_rows),
        "seq_lo",
        split_axis=2,
        concat_axis=0,
        tiled=True,
    ).reshape(block_rows * inner, -1)
    weight_terms = lax.dot_general(
        local_features,
        local_rows,
        (((0,), (0,)), ((), ())),
        preferred_element_type=jnp.float32,
    )
    grad_mixed = grad_gated * query_short
    grad_query_short = grad_gated * mixed_seq
    following = from_behind(grad_mixed.astype(jnp.bfloat16), SEQ, -1).astype(grad_mixed.dtype)
    spread = jnp.concatenate([grad_mixed, following], axis=0)
    grad_pair = rows_spectrum(spread, full_basis)
    moved_grad = split_lanes(
        lax.all_to_all(
            jnp.concatenate(grad_pair, axis=1)[None].astype(jnp.bfloat16),
            SEQ,
            split_axis=1,
            concat_axis=0,
            tiled=True,
        ).astype(jnp.float32),
        lanes,
    )
    grad_spectrum = block_forward(moved_grad, block_basis)
    input_back = block_inverse(conj_product(filter_spectrum, grad_spectrum), return_basis)
    filter_back = block_inverse(conj_product(input_spectrum, grad_spectrum), return_basis)
    returned_grad = split_lanes(
        lax.all_to_all(
            as_sent(jnp.concatenate(input_back + filter_back, axis=-1)),
            SEQ,
            split_axis=0,
            concat_axis=1,
            tiled=True,
        ),
        lanes,
    )
    conv_grad = rows_inverse((returned_grad[0][0], returned_grad[1][0]), half_basis)
    grad_filter = rows_inverse((returned_grad[2][0], returned_grad[3][0]), half_basis)
    grad_product = conv_grad + skip_gain * grad_mixed
    grad_streams = jnp.stack(
        [grad_query_short, grad_product * value_short, grad_product * key_short]
    )
    later_rows = from_behind(grad_streams[:, : tap_count - 1], SEQ, -1)
    padded_grad = jnp.concatenate([grad_streams, later_rows], axis=1)
    grad_inputs = sum(
        (
            short_filter[:, offset][:, None, :] * padded_grad[:, offset : offset + block_rows]
            for offset in range(tap_count)
        )
    )
    short_terms = jnp.stack(
        [jnp.sum(grad_streams * shifted[offset], axis=1) for offset in range(tap_count)], axis=1
    )
    skip_terms = jnp.sum(grad_mixed * product, axis=0)
    channel_count = skip_terms.shape[0]
    sum_rows = short_terms.shape[0] * short_terms.shape[1] + 1
    padded_rows = -(-sum_rows // 8) * 8
    small_terms = jnp.concatenate(
        [
            short_terms.reshape(sum_rows - 1, channel_count),
            skip_terms[None],
            jnp.zeros((padded_rows - sum_rows, channel_count), jnp.float32),
        ]
    )
    outer = block_count // inner
    inner_sum = sum_over_group(
        jnp.broadcast_to(small_terms, (inner,) + small_terms.shape), "seq_lo", 0
    )
    weight_blocks = weight_terms.reshape(outer, -1, channel_count)
    block_height = weight_blocks.shape[1]
    reduced = sum_over_group(
        jnp.concatenate(
            [weight_blocks, jnp.broadcast_to(inner_sum, (outer,) + inner_sum.shape)], axis=1
        ),
        "seq_hi",
        1,
    )
    grad_w_out_t = reduced[:block_height]
    summed = reduced[block_height:]
    grad_short = summed[: sum_rows - 1].reshape(short_terms.shape)
    grad_skip = summed[sum_rows - 1]
    return (
        layer_out,
        grad_inputs[0],
        grad_inputs[1],
        grad_inputs[2],
        grad_short,
        grad_filter,
        grad_skip,
        grad_w_out_t,
    )


def solution(mesh):
    in_specs = (
        P(SEQ, "ch"),
        P(SEQ, "ch"),
        P(SEQ, "ch"),
        P(None, None, "ch"),
        P(SEQ, "ch"),
        P("ch"),
        P("ch", None),
        P(SEQ, "ch"),
    )
    out_specs = (
        P(SEQ, "ch"),
        P(SEQ, "ch"),
        P(SEQ, "ch"),
        P(SEQ, "ch"),
        P(None, None, "ch"),
        P(SEQ, "ch"),
        P("ch"),
        P(SEQ, "ch"),
    )
    inner = 8
    seq_mesh = jax.sharding.Mesh(
        mesh.devices.reshape(mesh.shape["seq"] // inner, inner, mesh.shape["ch"]),
        ("seq_hi", "seq_lo", "ch"),
    )
    return jax.shard_map(
        on_device, mesh=seq_mesh, in_specs=in_specs, out_specs=out_specs, check_vma=False
    )
```

```python
import functools
import math

import jax
import jax.numpy as jnp
from jax import lax
from jax.experimental import pallas as pl
from jax.experimental.pallas import tpu as pltpu
from jax.sharding import PartitionSpec as P

exact_mode = lax.Precision.HIGHEST
SEQ = ("seq_hi", "seq_lo")


def from_behind(shard, axis, by):
    size = lax.axis_size(axis)
    pairs = [(i, i + by) for i in range(size) if 0 <= i + by < size]
    return lax.ppermute(shard, axis, pairs)


def as_sent(shard):

    def short(part):
        return part.astype(jnp.bfloat16) if part.dtype == jnp.float32 else part

    return jax.tree.map(short, shard)


def group_sum_kernel(axis, blocks_ref, out_ref, slots, local_sem, send_sems, recv_sems):
    count = lax.axis_size(axis)
    me = lax.axis_index(axis)
    place = {"seq_hi": lax.axis_index("seq_hi"), "seq_lo": lax.axis_index("seq_lo")}

    def member(index):
        where = dict(place, **{axis: index})
        return (where["seq_hi"], where["seq_lo"], lax.axis_index("ch"))

    barrier = pltpu.get_barrier_semaphore()
    for step in range(1, count):
        pl.semaphore_signal(
            barrier,
            1,
            device_id=member(lax.rem(me + step, count)),
            device_id_type=pl.DeviceIdType.MESH,
        )
    pl.semaphore_wait(barrier, count - 1)
    own = pltpu.make_async_copy(blocks_ref.at[me], slots.at[me], local_sem)
    own.start()
    outgoing = []
    for step in range(1, count):
        peer = lax.rem(me + step, count)
        copy = pltpu.make_async_remote_copy(
            src_ref=blocks_ref.at[peer],
            dst_ref=slots.at[me],
            send_sem=send_sems.at[step],
            recv_sem=recv_sems.at[me],
            device_id=member(peer),
            device_id_type=pl.DeviceIdType.MESH,
        )
        copy.start()
        outgoing.append(copy)
    own.wait()
    for step in range(1, count):
        source = lax.rem(me + count - step, count)
        outgoing[step - 1].wait_send()
        pltpu.make_async_remote_copy(
            src_ref=blocks_ref.at[source],
            dst_ref=slots.at[source],
            send_sem=send_sems.at[step],
            recv_sem=recv_sems.at[source],
            device_id=member(source),
            device_id_type=pl.DeviceIdType.MESH,
        ).wait_recv()
    total = slots[0]
    for slot in range(1, count):
        total = total + slots[slot]
    out_ref[...] = total


def sum_over_group(blocks, axis, kernel_id):
    count = blocks.shape[0]
    return pl.pallas_call(
        functools.partial(group_sum_kernel, axis),
        out_shape=jax.ShapeDtypeStruct(blocks.shape[1:], blocks.dtype),
        in_specs=[pl.BlockSpec(memory_space=pltpu.VMEM)],
        out_specs=pl.BlockSpec(memory_space=pltpu.VMEM),
        scratch_shapes=[
            pltpu.VMEM(blocks.shape, blocks.dtype),
            pltpu.SemaphoreType.DMA(()),
            pltpu.SemaphoreType.DMA((count,)),
            pltpu.SemaphoreType.DMA((count,)),
        ],
        compiler_params=pltpu.CompilerParams(collective_id=kernel_id, has_side_effects=True),
    )(blocks)


def split_lanes(merged, lanes):
    return tuple(
        merged[..., start : start + lanes] for start in range(0, merged.shape[-1], lanes)
    )


def tables(rows_out, cols_in, period):
    row_index = lax.broadcasted_iota(jnp.int32, (rows_out, cols_in), 0)
    col_index = lax.broadcasted_iota(jnp.int32, (rows_out, cols_in), 1)
    phase_angle = (row_index * col_index % period).astype(jnp.float32) * (2.0 * math.pi / period)
    return (jnp.cos(phase_angle), jnp.sin(phase_angle))


def along_rows(factor, values):
    return jnp.tensordot(factor, values, axes=1, precision=exact_mode)


def rows_spectrum(signal, basis_pair):
    return (along_rows(basis_pair[0], signal), -along_rows(basis_pair[1], signal))


def rows_inverse(complex_pair, basis_pair):
    total = along_rows(basis_pair[0], complex_pair[0]) - along_rows(basis_pair[1], complex_pair[1])
    return total / basis_pair[0].shape[1]


def block_forward(complex_pair, basis_pair):
    cosine_part, sine_part = basis_pair
    real_part = along_rows(cosine_part, complex_pair[0]) + along_rows(sine_part, complex_pair[1])
    imag_part = along_rows(cosine_part, complex_pair[1]) - along_rows(sine_part, complex_pair[0])
    return (real_part, imag_part)


def block_inverse(complex_pair, basis_pair):
    cosine_part, sine_part = basis_pair
    norming = 1.0 / cosine_part.shape[1]
    real_part = along_rows(cosine_part, complex_pair[0]) - along_rows(sine_part, complex_pair[1])
    imag_part = along_rows(cosine_part, complex_pair[1]) + along_rows(sine_part, complex_pair[0])
    return (real_part * norming, imag_part * norming)


def complex_product(first_pair, second_pair):
    return (
        first_pair[0] * second_pair[0] - first_pair[1] * second_pair[1],
        first_pair[0] * second_pair[1] + first_pair[1] * second_pair[0],
    )


def conj_product(first_pair, second_pair):
    return (
        first_pair[0] * second_pair[0] + first_pair[1] * second_pair[1],
        first_pair[0] * second_pair[1] - first_pair[1] * second_pair[0],
    )


def on_device(
    query_proj, key_proj, value_proj, short_filter, long_filter, skip_gain, out_weight, cotangent
):
    block_rows = query_proj.shape[0]
    tap_count = short_filter.shape[1]
    block_count = lax.axis_size(SEQ)
    streams = jnp.stack([query_proj, key_proj, value_proj])
    earlier = from_behind(streams[:, block_rows - (tap_count - 1) :], SEQ, 1)
    extended = jnp.concatenate([earlier, streams], axis=1).astype(jnp.float32)
    shifted = [
        extended[:, tap_count - 1 - offset : tap_count - 1 - offset + block_rows]
        for offset in range(tap_count)
    ]
    filtered = sum(
        (short_filter[:, offset][:, None, :] * shifted[offset] for offset in range(tap_count))
    )
    query_short, key_short, value_short = (filtered[0], filtered[1], filtered[2])
    product = key_short * value_short
    forward_basis = tables(2 * block_rows, block_rows, 2 * block_rows)
    full_basis = tables(2 * block_rows, 2 * block_rows, 2 * block_rows)
    half_basis = tables(block_rows, 2 * block_rows, 2 * block_rows)
    block_basis = tables(2 * block_count, block_count, 2 * block_count)
    return_basis = tables(block_count, 2 * block_count, 2 * block_count)
    input_pair = rows_spectrum(product, forward_basis)
    filter_pair = rows_spectrum(long_filter, forward_basis)
    lanes = product.shape[1]
    moved_data = split_lanes(
        lax.all_to_all(
            jnp.concatenate([input_pair[0], input_pair[1], filter_pair[0], filter_pair[1]], axis=1)[
                None
            ],
            SEQ,
            split_axis=1,
            concat_axis=0,
            tiled=True,
        ),
        lanes,
    )
    input_spectrum = block_forward((moved_data[0], moved_data[1]), block_basis)
    filter_spectrum = block_forward((moved_data[2], moved_data[3]), block_basis)
    inverse_pair = block_inverse(complex_product(filter_spectrum, input_spectrum), return_basis)
    returned = split_lanes(
        lax.all_to_all(
            jnp.concatenate(inverse_pair, axis=-1), SEQ, split_axis=0, concat_axis=1, tiled=True
        ),
        lanes,
    )
    folded = rows_inverse((returned[0][0], returned[1][0]), full_basis)
    carried = from_behind(folded[block_rows:], SEQ, 1)
    convolved = folded[:block_rows] + carried
    mixed_seq = convolved + skip_gain * product
    gated_values = (query_short * mixed_seq).astype(jnp.bfloat16)
    full_cotangent = lax.all_gather(cotangent, "ch", axis=1, tiled=True)
    full_cotangent, gated_values = lax.optimization_barrier((full_cotangent, gated_values))
    partial_value = jnp.dot(gated_values, out_weight, preferred_element_type=jnp.float32)
    layer_out = lax.psum_scatter(partial_value, "ch", scatter_dimension=1, tiled=True).astype(
        jnp.bfloat16
    )
    grad_gated = lax.dot_general(
        full_cotangent, out_weight, (((1,), (1,)), ((), ())), preferred_element_type=jnp.float32
    )
    outer = lax.axis_size("seq_hi")
    inner = lax.axis_size("seq_lo")
    feature_rows = full_cotangent.shape[1] // outer // inner
    local_rows = lax.all_gather(gated_values, "seq_hi", axis=0, tiled=True)
    local_features = lax.all_to_all(
        full_cotangent.reshape(block_rows, outer, inner, feature_rows),
        "seq_hi",
        split_axis=1,
        concat_axis=0,
        tiled=True,
    ).reshape(block_rows * outer, -1)
    weight_terms = lax.dot_general(
        local_features,
        local_rows,
        (((0,), (0,)), ((), ())),
        preferred_element_type=jnp.float32,
    )
    grad_mixed = grad_gated * query_short
    grad_query_short = grad_gated * mixed_seq
    following = from_behind(grad_mixed.astype(jnp.bfloat16), SEQ, -1).astype(grad_mixed.dtype)
    spread = jnp.concatenate([grad_mixed, following], axis=0)
    grad_pair = rows_spectrum(spread, full_basis)
    moved_grad = split_lanes(
        lax.all_to_all(
            jnp.concatenate(grad_pair, axis=1)[None].astype(jnp.bfloat16),
            SEQ,
            split_axis=1,
            concat_axis=0,
            tiled=True,
        ).astype(jnp.float32),
        lanes,
    )
    grad_spectrum = block_forward(moved_grad, block_basis)
    input_back = block_inverse(conj_product(filter_spectrum, grad_spectrum), return_basis)
    filter_back = block_inverse(conj_product(input_spectrum, grad_spectrum), return_basis)
    returned_grad = split_lanes(
        lax.all_to_all(
            as_sent(jnp.concatenate(input_back + filter_back, axis=-1)),
            SEQ,
            split_axis=0,
            concat_axis=1,
            tiled=True,
        ),
        lanes,
    )
    weight_terms, layer_out, returned_grad = lax.optimization_barrier(
        (weight_terms, layer_out, returned_grad)
    )
    conv_grad = rows_inverse((returned_grad[0][0], returned_grad[1][0]), half_basis)
    grad_filter = rows_inverse((returned_grad[2][0], returned_grad[3][0]), half_basis)
    grad_product = conv_grad + skip_gain * grad_mixed
    grad_streams = jnp.stack(
        [grad_query_short, grad_product * value_short, grad_product * key_short]
    )
    later_rows = from_behind(grad_streams[:, : tap_count - 1], SEQ, -1)
    padded_grad = jnp.concatenate([grad_streams, later_rows], axis=1)
    grad_inputs = sum(
        (
            short_filter[:, offset][:, None, :] * padded_grad[:, offset : offset + block_rows]
            for offset in range(tap_count)
        )
    )
    short_terms = jnp.stack(
        [jnp.sum(grad_streams * shifted[offset], axis=1) for offset in range(tap_count)], axis=1
    )
    skip_terms = jnp.sum(grad_mixed * product, axis=0)
    channel_count = skip_terms.shape[0]
    sum_rows = short_terms.shape[0] * short_terms.shape[1] + 1
    padded_rows = -(-sum_rows // 8) * 8
    small_terms = jnp.concatenate(
        [
            short_terms.reshape(sum_rows - 1, channel_count),
            skip_terms[None],
            jnp.zeros((padded_rows - sum_rows, channel_count), jnp.float32),
        ]
    )
    outer_sum = sum_over_group(
        jnp.broadcast_to(small_terms, (outer,) + small_terms.shape), "seq_hi", 0
    )
    weight_blocks = weight_terms.reshape(inner, -1, channel_count)
    block_height = weight_blocks.shape[1]
    reduced = sum_over_group(
        jnp.concatenate(
            [weight_blocks, jnp.broadcast_to(outer_sum, (inner,) + outer_sum.shape)], axis=1
        ),
        "seq_lo",
        1,
    )
    grad_w_out_t = reduced[:block_height]
    summed = reduced[block_height:]
    grad_short = summed[: sum_rows - 1].reshape(short_terms.shape)
    grad_skip = summed[sum_rows - 1]
    return (
        layer_out,
        grad_inputs[0],
        grad_inputs[1],
        grad_inputs[2],
        grad_short,
        grad_filter,
        grad_skip,
        grad_w_out_t,
    )


def solution(mesh):
    in_specs = (
        P(SEQ, "ch"),
        P(SEQ, "ch"),
        P(SEQ, "ch"),
        P(None, None, "ch"),
        P(SEQ, "ch"),
        P("ch"),
        P("ch", None),
        P(SEQ, "ch"),
    )
    out_specs = (
        P(SEQ, "ch"),
        P(SEQ, "ch"),
        P(SEQ, "ch"),
        P(SEQ, "ch"),
        P(None, None, "ch"),
        P(SEQ, "ch"),
        P("ch"),
        P(SEQ, "ch"),
    )
    inner = 8
    seq_mesh = jax.sharding.Mesh(
        mesh.devices.reshape(mesh.shape["seq"] // inner, inner, mesh.shape["ch"]),
        ("seq_hi", "seq_lo", "ch"),
    )
    return jax.shard_map(
        on_device, mesh=seq_mesh, in_specs=in_specs, out_specs=out_specs, check_vma=False
    )
```

```python
import functools
import math

import jax
import jax.numpy as jnp
from jax import lax
from jax.experimental import pallas as pl
from jax.experimental.pallas import tpu as pltpu
from jax.sharding import PartitionSpec as P

exact_mode = lax.Precision.HIGHEST
SEQ = ("seq_hi", "seq_lo")


def from_behind(shard, axis, by):
    size = lax.axis_size(axis)
    pairs = [(i, i + by) for i in range(size) if 0 <= i + by < size]
    return lax.ppermute(shard, axis, pairs)


def as_sent(shard):

    def short(part):
        return part.astype(jnp.bfloat16) if part.dtype == jnp.float32 else part

    return jax.tree.map(short, shard)


def group_sum_kernel(axis, blocks_ref, out_ref, slots, local_sem, send_sems, recv_sems):
    count = lax.axis_size(axis)
    me = lax.axis_index(axis)
    place = {"seq_hi": lax.axis_index("seq_hi"), "seq_lo": lax.axis_index("seq_lo")}

    def member(index):
        where = dict(place, **{axis: index})
        return (where["seq_hi"], where["seq_lo"], lax.axis_index("ch"))

    barrier = pltpu.get_barrier_semaphore()
    for step in range(1, count):
        pl.semaphore_signal(
            barrier,
            1,
            device_id=member(lax.rem(me + step, count)),
            device_id_type=pl.DeviceIdType.MESH,
        )
    pl.semaphore_wait(barrier, count - 1)
    own = pltpu.make_async_copy(blocks_ref.at[me], slots.at[me], local_sem)
    own.start()
    outgoing = []
    for step in range(1, count):
        peer = lax.rem(me + step, count)
        copy = pltpu.make_async_remote_copy(
            src_ref=blocks_ref.at[peer],
            dst_ref=slots.at[me],
            send_sem=send_sems.at[step],
            recv_sem=recv_sems.at[me],
            device_id=member(peer),
            device_id_type=pl.DeviceIdType.MESH,
        )
        copy.start()
        outgoing.append(copy)
    own.wait()
    for step in range(1, count):
        source = lax.rem(me + count - step, count)
        outgoing[step - 1].wait_send()
        pltpu.make_async_remote_copy(
            src_ref=blocks_ref.at[source],
            dst_ref=slots.at[source],
            send_sem=send_sems.at[step],
            recv_sem=recv_sems.at[source],
            device_id=member(source),
            device_id_type=pl.DeviceIdType.MESH,
        ).wait_recv()
    total = slots[0]
    for slot in range(1, count):
        total = total + slots[slot]
    out_ref[...] = total


def sum_over_group(blocks, axis, kernel_id):
    count = blocks.shape[0]
    return pl.pallas_call(
        functools.partial(group_sum_kernel, axis),
        out_shape=jax.ShapeDtypeStruct(blocks.shape[1:], blocks.dtype),
        in_specs=[pl.BlockSpec(memory_space=pltpu.VMEM)],
        out_specs=pl.BlockSpec(memory_space=pltpu.VMEM),
        scratch_shapes=[
            pltpu.VMEM(blocks.shape, blocks.dtype),
            pltpu.SemaphoreType.DMA(()),
            pltpu.SemaphoreType.DMA((count,)),
            pltpu.SemaphoreType.DMA((count,)),
        ],
        compiler_params=pltpu.CompilerParams(collective_id=kernel_id, has_side_effects=True),
    )(blocks)


def split_lanes(merged, lanes):
    return tuple(
        merged[..., start : start + lanes] for start in range(0, merged.shape[-1], lanes)
    )


def tables(rows_out, cols_in, period):
    row_index = lax.broadcasted_iota(jnp.int32, (rows_out, cols_in), 0)
    col_index = lax.broadcasted_iota(jnp.int32, (rows_out, cols_in), 1)
    phase_angle = (row_index * col_index % period).astype(jnp.float32) * (2.0 * math.pi / period)
    return (jnp.cos(phase_angle), jnp.sin(phase_angle))


def odd_tables(rows_out, cols_in, period, odd_axis):
    row_index = lax.broadcasted_iota(jnp.int32, (rows_out, cols_in), 0)
    col_index = lax.broadcasted_iota(jnp.int32, (rows_out, cols_in), 1)
    if odd_axis == 0:
        row_index = 2 * row_index + 1
    else:
        col_index = 2 * col_index + 1
    phase_angle = (row_index * col_index % (2 * period)).astype(jnp.float32) * (math.pi / period)
    return (jnp.cos(phase_angle), jnp.sin(phase_angle))


def along_rows(factor, values):
    return jnp.tensordot(factor, values, axes=1, precision=exact_mode)


def rows_spectrum(signal, basis_pair):
    return (along_rows(basis_pair[0], signal), -along_rows(basis_pair[1], signal))


def rows_inverse(complex_pair, basis_pair):
    total = along_rows(basis_pair[0], complex_pair[0]) - along_rows(basis_pair[1], complex_pair[1])
    return total / basis_pair[0].shape[1]


def block_forward(complex_pair, basis_pair):
    cosine_part, sine_part = basis_pair
    real_part = along_rows(cosine_part, complex_pair[0]) + along_rows(sine_part, complex_pair[1])
    imag_part = along_rows(cosine_part, complex_pair[1]) - along_rows(sine_part, complex_pair[0])
    return (real_part, imag_part)


def block_inverse(complex_pair, basis_pair):
    cosine_part, sine_part = basis_pair
    norming = 1.0 / cosine_part.shape[1]
    real_part = along_rows(cosine_part, complex_pair[0]) - along_rows(sine_part, complex_pair[1])
    imag_part = along_rows(cosine_part, complex_pair[1]) + along_rows(sine_part, complex_pair[0])
    return (real_part * norming, imag_part * norming)


def complex_product(first_pair, second_pair):
    return (
        first_pair[0] * second_pair[0] - first_pair[1] * second_pair[1],
        first_pair[0] * second_pair[1] + first_pair[1] * second_pair[0],
    )


def conj_product(first_pair, second_pair):
    return (
        first_pair[0] * second_pair[0] + first_pair[1] * second_pair[1],
        first_pair[0] * second_pair[1] - first_pair[1] * second_pair[0],
    )


def on_device(
    query_proj, key_proj, value_proj, short_filter, long_filter, skip_gain, out_weight, cotangent
):
    block_rows = query_proj.shape[0]
    tap_count = short_filter.shape[1]
    block_count = lax.axis_size(SEQ)
    streams = jnp.stack([query_proj, key_proj, value_proj])
    earlier = from_behind(streams[:, block_rows - (tap_count - 1) :], SEQ, 1)
    extended = jnp.concatenate([earlier, streams], axis=1).astype(jnp.float32)
    shifted = [
        extended[:, tap_count - 1 - offset : tap_count - 1 - offset + block_rows]
        for offset in range(tap_count)
    ]
    filtered = sum(
        (short_filter[:, offset][:, None, :] * shifted[offset] for offset in range(tap_count))
    )
    query_short, key_short, value_short = (filtered[0], filtered[1], filtered[2])
    product = key_short * value_short
    forward_basis = odd_tables(block_rows, block_rows, 2 * block_rows, 0)
    spread_basis = odd_tables(block_rows, 2 * block_rows, 2 * block_rows, 0)
    fold_basis = odd_tables(2 * block_rows, block_rows, 2 * block_rows, 1)
    half_basis = odd_tables(block_rows, block_rows, 2 * block_rows, 1)
    block_basis = tables(2 * block_count, block_count, 2 * block_count)
    return_basis = tables(block_count, 2 * block_count, 2 * block_count)
    input_pair = rows_spectrum(product, forward_basis)
    filter_pair = rows_spectrum(long_filter, forward_basis)
    lanes = product.shape[1]
    moved_data = split_lanes(
        lax.all_to_all(
            jnp.concatenate([input_pair[0], input_pair[1], filter_pair[0], filter_pair[1]], axis=1)[
                None
            ],
            SEQ,
            split_axis=1,
            concat_axis=0,
            tiled=True,
        ),
        lanes,
    )
    input_spectrum = block_forward((moved_data[0], moved_data[1]), block_basis)
    filter_spectrum = block_forward((moved_data[2], moved_data[3]), block_basis)
    inverse_pair = block_inverse(complex_product(filter_spectrum, input_spectrum), return_basis)
    returned = split_lanes(
        lax.all_to_all(
            jnp.concatenate(inverse_pair, axis=-1), SEQ, split_axis=0, concat_axis=1, tiled=True
        ),
        lanes,
    )
    folded = rows_inverse((returned[0][0], returned[1][0]), fold_basis)
    carried = from_behind(folded[block_rows:], SEQ, 1)
    convolved = folded[:block_rows] + carried
    mixed_seq = convolved + skip_gain * product
    gated_values = (query_short * mixed_seq).astype(jnp.bfloat16)
    full_cotangent = lax.all_gather(cotangent, "ch", axis=1, tiled=True)
    full_cotangent, gated_values = lax.optimization_barrier((full_cotangent, gated_values))
    partial_value = jnp.dot(gated_values, out_weight, preferred_element_type=jnp.float32)
    layer_out = lax.psum_scatter(partial_value, "ch", scatter_dimension=1, tiled=True).astype(
        jnp.bfloat16
    )
    grad_gated = lax.dot_general(
        full_cotangent, out_weight, (((1,), (1,)), ((), ())), preferred_element_type=jnp.float32
    )
    outer = lax.axis_size("seq_hi")
    inner = lax.axis_size("seq_lo")
    feature_rows = full_cotangent.shape[1] // outer // inner
    local_rows = lax.all_gather(gated_values, "seq_hi", axis=0, tiled=True)
    local_features = lax.all_to_all(
        full_cotangent.reshape(block_rows, outer, inner, feature_rows),
        "seq_hi",
        split_axis=1,
        concat_axis=0,
        tiled=True,
    ).reshape(block_rows * outer, -1)
    weight_terms = lax.dot_general(
        local_features,
        local_rows,
        (((0,), (0,)), ((), ())),
        preferred_element_type=jnp.float32,
    )
    grad_mixed = grad_gated * query_short
    grad_query_short = grad_gated * mixed_seq
    following = from_behind(grad_mixed.astype(jnp.bfloat16), SEQ, -1).astype(grad_mixed.dtype)
    spread = jnp.concatenate([grad_mixed, following], axis=0)
    grad_pair = rows_spectrum(spread, spread_basis)
    moved_grad = split_lanes(
        lax.all_to_all(
            jnp.concatenate(grad_pair, axis=1)[None].astype(jnp.bfloat16),
            SEQ,
            split_axis=1,
            concat_axis=0,
            tiled=True,
        ).astype(jnp.float32),
        lanes,
    )
    grad_spectrum = block_forward(moved_grad, block_basis)
    input_back = block_inverse(conj_product(filter_spectrum, grad_spectrum), return_basis)
    filter_back = block_inverse(conj_product(input_spectrum, grad_spectrum), return_basis)
    returned_grad = split_lanes(
        lax.all_to_all(
            as_sent(jnp.concatenate(input_back + filter_back, axis=-1)),
            SEQ,
            split_axis=0,
            concat_axis=1,
            tiled=True,
        ),
        lanes,
    )
    weight_terms, layer_out, returned_grad = lax.optimization_barrier(
        (weight_terms, layer_out, returned_grad)
    )
    conv_grad = rows_inverse((returned_grad[0][0], returned_grad[1][0]), half_basis)
    grad_filter = rows_inverse((returned_grad[2][0], returned_grad[3][0]), half_basis)
    grad_product = conv_grad + skip_gain * grad_mixed
    grad_streams = jnp.stack(
        [grad_query_short, grad_product * value_short, grad_product * key_short]
    )
    later_rows = from_behind(grad_streams[:, : tap_count - 1], SEQ, -1)
    padded_grad = jnp.concatenate([grad_streams, later_rows], axis=1)
    grad_inputs = sum(
        (
            short_filter[:, offset][:, None, :] * padded_grad[:, offset : offset + block_rows]
            for offset in range(tap_count)
        )
    )
    short_terms = jnp.stack(
        [jnp.sum(grad_streams * shifted[offset], axis=1) for offset in range(tap_count)], axis=1
    )
    skip_terms = jnp.sum(grad_mixed * product, axis=0)
    channel_count = skip_terms.shape[0]
    sum_rows = short_terms.shape[0] * short_terms.shape[1] + 1
    padded_rows = -(-sum_rows // 8) * 8
    small_terms = jnp.concatenate(
        [
            short_terms.reshape(sum_rows - 1, channel_count),
            skip_terms[None],
            jnp.zeros((padded_rows - sum_rows, channel_count), jnp.float32),
        ]
    )
    outer_sum = sum_over_group(
        jnp.broadcast_to(small_terms, (outer,) + small_terms.shape), "seq_hi", 0
    )
    weight_blocks = weight_terms.reshape(inner, -1, channel_count)
    block_height = weight_blocks.shape[1]
    reduced = sum_over_group(
        jnp.concatenate(
            [weight_blocks, jnp.broadcast_to(outer_sum, (inner,) + outer_sum.shape)], axis=1
        ),
        "seq_lo",
        1,
    )
    grad_w_out_t = reduced[:block_height]
    summed = reduced[block_height:]
    grad_short = summed[: sum_rows - 1].reshape(short_terms.shape)
    grad_skip = summed[sum_rows - 1]
    return (
        layer_out,
        grad_inputs[0],
        grad_inputs[1],
        grad_inputs[2],
        grad_short,
        grad_filter,
        grad_skip,
        grad_w_out_t,
    )


def solution(mesh):
    in_specs = (
        P(SEQ, "ch"),
        P(SEQ, "ch"),
        P(SEQ, "ch"),
        P(None, None, "ch"),
        P(SEQ, "ch"),
        P("ch"),
        P("ch", None),
        P(SEQ, "ch"),
    )
    out_specs = (
        P(SEQ, "ch"),
        P(SEQ, "ch"),
        P(SEQ, "ch"),
        P(SEQ, "ch"),
        P(None, None, "ch"),
        P(SEQ, "ch"),
        P("ch"),
        P(SEQ, "ch"),
    )
    inner = 8
    seq_mesh = jax.sharding.Mesh(
        mesh.devices.reshape(mesh.shape["seq"] // inner, inner, mesh.shape["ch"]),
        ("seq_hi", "seq_lo", "ch"),
    )
    return jax.shard_map(
        on_device, mesh=seq_mesh, in_specs=in_specs, out_specs=out_specs, check_vma=False
    )
```

```python
import functools
import math

import jax
import jax.numpy as jnp
from jax import lax
from jax.experimental import pallas as pl
from jax.experimental.pallas import tpu as pltpu
from jax.sharding import PartitionSpec as P

exact_mode = lax.Precision.HIGHEST
SEQ = ("seq_hi", "seq_lo")


def from_behind(shard, axis, by):
    size = lax.axis_size(axis)
    pairs = [(i, i + by) for i in range(size) if 0 <= i + by < size]
    return lax.ppermute(shard, axis, pairs)


def as_sent(shard):

    def short(part):
        return part.astype(jnp.bfloat16) if part.dtype == jnp.float32 else part

    return jax.tree.map(short, shard)


def group_sum_kernel(axis, blocks_ref, out_ref, slots, local_sem, send_sems, recv_sems):
    count = lax.axis_size(axis)
    me = lax.axis_index(axis)
    place = {"seq_hi": lax.axis_index("seq_hi"), "seq_lo": lax.axis_index("seq_lo")}

    def member(index):
        where = dict(place, **{axis: index})
        return (where["seq_hi"], where["seq_lo"], lax.axis_index("ch"))

    barrier = pltpu.get_barrier_semaphore()
    for step in range(1, count):
        pl.semaphore_signal(
            barrier,
            1,
            device_id=member(lax.rem(me + step, count)),
            device_id_type=pl.DeviceIdType.MESH,
        )
    pl.semaphore_wait(barrier, count - 1)
    own = pltpu.make_async_copy(blocks_ref.at[me], slots.at[me], local_sem)
    own.start()
    outgoing = []
    for step in range(1, count):
        peer = lax.rem(me + step, count)
        copy = pltpu.make_async_remote_copy(
            src_ref=blocks_ref.at[peer],
            dst_ref=slots.at[me],
            send_sem=send_sems.at[step],
            recv_sem=recv_sems.at[me],
            device_id=member(peer),
            device_id_type=pl.DeviceIdType.MESH,
        )
        copy.start()
        outgoing.append(copy)
    own.wait()
    for step in range(1, count):
        source = lax.rem(me + count - step, count)
        outgoing[step - 1].wait_send()
        pltpu.make_async_remote_copy(
            src_ref=blocks_ref.at[source],
            dst_ref=slots.at[source],
            send_sem=send_sems.at[step],
            recv_sem=recv_sems.at[source],
            device_id=member(source),
            device_id_type=pl.DeviceIdType.MESH,
        ).wait_recv()
    total = slots[0]
    for slot in range(1, count):
        total = total + slots[slot]
    out_ref[...] = total


def sum_over_group(blocks, axis, kernel_id):
    count = blocks.shape[0]
    return pl.pallas_call(
        functools.partial(group_sum_kernel, axis),
        out_shape=jax.ShapeDtypeStruct(blocks.shape[1:], blocks.dtype),
        in_specs=[pl.BlockSpec(memory_space=pltpu.VMEM)],
        out_specs=pl.BlockSpec(memory_space=pltpu.VMEM),
        scratch_shapes=[
            pltpu.VMEM(blocks.shape, blocks.dtype),
            pltpu.SemaphoreType.DMA(()),
            pltpu.SemaphoreType.DMA((count,)),
            pltpu.SemaphoreType.DMA((count,)),
        ],
        compiler_params=pltpu.CompilerParams(collective_id=kernel_id, has_side_effects=True),
    )(blocks)


def split_lanes(merged, lanes):
    return tuple(
        merged[..., start : start + lanes] for start in range(0, merged.shape[-1], lanes)
    )


def tables(rows_out, cols_in, period):
    row_index = lax.broadcasted_iota(jnp.int32, (rows_out, cols_in), 0)
    col_index = lax.broadcasted_iota(jnp.int32, (rows_out, cols_in), 1)
    phase_angle = (row_index * col_index % period).astype(jnp.float32) * (2.0 * math.pi / period)
    return (jnp.cos(phase_angle), jnp.sin(phase_angle))


def odd_tables(rows_out, cols_in, period, odd_axis):
    row_index = lax.broadcasted_iota(jnp.int32, (rows_out, cols_in), 0)
    col_index = lax.broadcasted_iota(jnp.int32, (rows_out, cols_in), 1)
    if odd_axis == 0:
        row_index = 2 * row_index + 1
    else:
        col_index = 2 * col_index + 1
    phase_angle = (row_index * col_index % (2 * period)).astype(jnp.float32) * (math.pi / period)
    return (jnp.cos(phase_angle), jnp.sin(phase_angle))


def along_rows(factor, values):
    return jnp.tensordot(factor, values, axes=1, precision=exact_mode)


def rows_spectrum(signal, basis_pair):
    return (along_rows(basis_pair[0], signal), -along_rows(basis_pair[1], signal))


def rows_inverse(complex_pair, basis_pair):
    total = along_rows(basis_pair[0], complex_pair[0]) - along_rows(basis_pair[1], complex_pair[1])
    return total / basis_pair[0].shape[1]


def block_forward(complex_pair, basis_pair):
    cosine_part, sine_part = basis_pair
    real_part = along_rows(cosine_part, complex_pair[0]) + along_rows(sine_part, complex_pair[1])
    imag_part = along_rows(cosine_part, complex_pair[1]) - along_rows(sine_part, complex_pair[0])
    return (real_part, imag_part)


def block_inverse(complex_pair, basis_pair):
    cosine_part, sine_part = basis_pair
    norming = 1.0 / cosine_part.shape[1]
    real_part = along_rows(cosine_part, complex_pair[0]) - along_rows(sine_part, complex_pair[1])
    imag_part = along_rows(cosine_part, complex_pair[1]) + along_rows(sine_part, complex_pair[0])
    return (real_part * norming, imag_part * norming)


def complex_product(first_pair, second_pair):
    return (
        first_pair[0] * second_pair[0] - first_pair[1] * second_pair[1],
        first_pair[0] * second_pair[1] + first_pair[1] * second_pair[0],
    )


def conj_product(first_pair, second_pair):
    return (
        first_pair[0] * second_pair[0] + first_pair[1] * second_pair[1],
        first_pair[0] * second_pair[1] - first_pair[1] * second_pair[0],
    )


def on_device(
    query_proj, key_proj, value_proj, short_filter, long_filter, skip_gain, out_weight, cotangent
):
    block_rows = query_proj.shape[0]
    tap_count = short_filter.shape[1]
    block_count = lax.axis_size(SEQ)
    streams = jnp.stack([query_proj, key_proj, value_proj])
    earlier = from_behind(streams[:, block_rows - (tap_count - 1) :], SEQ, 1)
    extended = jnp.concatenate([earlier, streams], axis=1).astype(jnp.float32)
    shifted = [
        extended[:, tap_count - 1 - offset : tap_count - 1 - offset + block_rows]
        for offset in range(tap_count)
    ]
    filtered = sum(
        (short_filter[:, offset][:, None, :] * shifted[offset] for offset in range(tap_count))
    )
    query_short, key_short, value_short = (filtered[0], filtered[1], filtered[2])
    product = key_short * value_short
    forward_basis = odd_tables(block_rows, block_rows, 2 * block_rows, 0)
    spread_basis = odd_tables(block_rows, 2 * block_rows, 2 * block_rows, 0)
    fold_basis = odd_tables(2 * block_rows, block_rows, 2 * block_rows, 1)
    half_basis = odd_tables(block_rows, block_rows, 2 * block_rows, 1)
    block_basis = tables(2 * block_count, block_count, 2 * block_count)
    return_basis = tables(block_count, 2 * block_count, 2 * block_count)
    input_pair = rows_spectrum(product, forward_basis)
    filter_pair = rows_spectrum(long_filter, forward_basis)
    lanes = product.shape[1]
    moved_data = split_lanes(
        lax.all_to_all(
            jnp.concatenate([input_pair[0], input_pair[1], filter_pair[0], filter_pair[1]], axis=1)[
                None
            ],
            SEQ,
            split_axis=1,
            concat_axis=0,
            tiled=True,
        ),
        lanes,
    )
    input_spectrum = block_forward((moved_data[0], moved_data[1]), block_basis)
    filter_spectrum = block_forward((moved_data[2], moved_data[3]), block_basis)
    inverse_pair = block_inverse(complex_product(filter_spectrum, input_spectrum), return_basis)
    returned = split_lanes(
        lax.all_to_all(
            jnp.concatenate(inverse_pair, axis=-1), SEQ, split_axis=0, concat_axis=1, tiled=True
        ),
        lanes,
    )
    folded = rows_inverse((returned[0][0], returned[1][0]), fold_basis)
    carried = from_behind(folded[block_rows:], SEQ, 1)
    convolved = folded[:block_rows] + carried
    mixed_seq = convolved + skip_gain * product
    gated_values = (query_short * mixed_seq).astype(jnp.bfloat16)
    full_cotangent = lax.all_gather(cotangent, "ch", axis=1, tiled=True)
    full_cotangent, gated_values = lax.optimization_barrier((full_cotangent, gated_values))
    partial_value = jnp.dot(gated_values, out_weight, preferred_element_type=jnp.float32)
    layer_out = lax.psum_scatter(partial_value, "ch", scatter_dimension=1, tiled=True).astype(
        jnp.bfloat16
    )
    grad_gated = lax.dot_general(
        full_cotangent, out_weight, (((1,), (1,)), ((), ())), preferred_element_type=jnp.float32
    )
    outer = lax.axis_size("seq_hi")
    inner = lax.axis_size("seq_lo")
    feature_rows = full_cotangent.shape[1] // outer // inner
    local_rows = lax.all_gather(gated_values, "seq_hi", axis=0, tiled=True)
    local_features = lax.all_to_all(
        full_cotangent.reshape(block_rows, outer, inner, feature_rows),
        "seq_hi",
        split_axis=1,
        concat_axis=0,
        tiled=True,
    ).reshape(block_rows * outer, -1)
    weight_terms = lax.dot_general(
        local_features,
        local_rows,
        (((0,), (0,)), ((), ())),
        preferred_element_type=jnp.float32,
    )
    grad_mixed = grad_gated * query_short
    grad_query_short = grad_gated * mixed_seq
    following = from_behind(grad_mixed.astype(jnp.bfloat16), SEQ, -1).astype(grad_mixed.dtype)
    spread = jnp.concatenate([grad_mixed, following], axis=0)
    grad_pair = rows_spectrum(spread, spread_basis)
    moved_grad = split_lanes(
        lax.all_to_all(
            jnp.concatenate(grad_pair, axis=1)[None].astype(jnp.bfloat16),
            SEQ,
            split_axis=1,
            concat_axis=0,
            tiled=True,
        ).astype(jnp.float32),
        lanes,
    )
    grad_spectrum = block_forward(moved_grad, block_basis)
    input_back = block_inverse(conj_product(filter_spectrum, grad_spectrum), return_basis)
    filter_back = block_inverse(conj_product(input_spectrum, grad_spectrum), return_basis)
    returned_grad = split_lanes(
        lax.all_to_all(
            as_sent(jnp.concatenate(input_back + filter_back, axis=-1)),
            SEQ,
            split_axis=0,
            concat_axis=1,
            tiled=True,
        ),
        lanes,
    )
    grad_w_out_t = lax.psum_scatter(weight_terms, "seq_lo", scatter_dimension=0, tiled=True)
    grad_w_out_t, layer_out, returned_grad = lax.optimization_barrier(
        (grad_w_out_t, layer_out, returned_grad)
    )
    conv_grad = rows_inverse((returned_grad[0][0], returned_grad[1][0]), half_basis)
    grad_filter = rows_inverse((returned_grad[2][0], returned_grad[3][0]), half_basis)
    grad_product = conv_grad + skip_gain * grad_mixed
    grad_streams = jnp.stack(
        [grad_query_short, grad_product * value_short, grad_product * key_short]
    )
    later_rows = from_behind(grad_streams[:, : tap_count - 1], SEQ, -1)
    padded_grad = jnp.concatenate([grad_streams, later_rows], axis=1)
    grad_inputs = sum(
        (
            short_filter[:, offset][:, None, :] * padded_grad[:, offset : offset + block_rows]
            for offset in range(tap_count)
        )
    )
    short_terms = jnp.stack(
        [jnp.sum(grad_streams * shifted[offset], axis=1) for offset in range(tap_count)], axis=1
    )
    skip_terms = jnp.sum(grad_mixed * product, axis=0)
    channel_count = skip_terms.shape[0]
    sum_rows = short_terms.shape[0] * short_terms.shape[1] + 1
    padded_rows = -(-sum_rows // 8) * 8
    small_terms = jnp.concatenate(
        [
            short_terms.reshape(sum_rows - 1, channel_count),
            skip_terms[None],
            jnp.zeros((padded_rows - sum_rows, channel_count), jnp.float32),
        ]
    )
    outer_sum = sum_over_group(
        jnp.broadcast_to(small_terms, (outer,) + small_terms.shape), "seq_hi", 0
    )
    summed = sum_over_group(
        jnp.broadcast_to(outer_sum, (inner,) + outer_sum.shape), "seq_lo", 1
    )
    grad_short = summed[: sum_rows - 1].reshape(short_terms.shape)
    grad_skip = summed[sum_rows - 1]
    return (
        layer_out,
        grad_inputs[0],
        grad_inputs[1],
        grad_inputs[2],
        grad_short,
        grad_filter,
        grad_skip,
        grad_w_out_t,
    )


def solution(mesh):
    in_specs = (
        P(SEQ, "ch"),
        P(SEQ, "ch"),
        P(SEQ, "ch"),
        P(None, None, "ch"),
        P(SEQ, "ch"),
        P("ch"),
        P("ch", None),
        P(SEQ, "ch"),
    )
    out_specs = (
        P(SEQ, "ch"),
        P(SEQ, "ch"),
        P(SEQ, "ch"),
        P(SEQ, "ch"),
        P(None, None, "ch"),
        P(SEQ, "ch"),
        P("ch"),
        P(SEQ, "ch"),
    )
    inner = 8
    seq_mesh = jax.sharding.Mesh(
        mesh.devices.reshape(mesh.shape["seq"] // inner, inner, mesh.shape["ch"]),
        ("seq_hi", "seq_lo", "ch"),
    )
    return jax.shard_map(
        on_device, mesh=seq_mesh, in_specs=in_specs, out_specs=out_specs, check_vma=False
    )
```

```python
import functools
import math

import jax
import jax.numpy as jnp
from jax import lax
from jax.experimental import pallas as pl
from jax.experimental.pallas import tpu as pltpu
from jax.sharding import PartitionSpec as P

exact_mode = lax.Precision.HIGHEST
SEQ = ("seq_hi", "seq_lo")


def from_behind(shard, axis, by):
    size = lax.axis_size(axis)
    pairs = [(i, i + by) for i in range(size) if 0 <= i + by < size]
    return lax.ppermute(shard, axis, pairs)


def as_sent(shard):

    def short(part):
        return part.astype(jnp.bfloat16) if part.dtype == jnp.float32 else part

    return jax.tree.map(short, shard)


def group_sum_kernel(axis, blocks_ref, out_ref, slots, local_sem, send_sems, recv_sems):
    count = lax.axis_size(axis)
    me = lax.axis_index(axis)
    place = {"seq_hi": lax.axis_index("seq_hi"), "seq_lo": lax.axis_index("seq_lo")}

    def member(index):
        where = dict(place, **{axis: index})
        return (where["seq_hi"], where["seq_lo"], lax.axis_index("ch"))

    barrier = pltpu.get_barrier_semaphore()
    for step in range(1, count):
        pl.semaphore_signal(
            barrier,
            1,
            device_id=member(lax.rem(me + step, count)),
            device_id_type=pl.DeviceIdType.MESH,
        )
    pl.semaphore_wait(barrier, count - 1)
    own = pltpu.make_async_copy(blocks_ref.at[me], slots.at[me], local_sem)
    own.start()
    outgoing = []
    for step in range(1, count):
        peer = lax.rem(me + step, count)
        copy = pltpu.make_async_remote_copy(
            src_ref=blocks_ref.at[peer],
            dst_ref=slots.at[me],
            send_sem=send_sems.at[step],
            recv_sem=recv_sems.at[me],
            device_id=member(peer),
            device_id_type=pl.DeviceIdType.MESH,
        )
        copy.start()
        outgoing.append(copy)
    own.wait()
    for step in range(1, count):
        source = lax.rem(me + count - step, count)
        outgoing[step - 1].wait_send()
        pltpu.make_async_remote_copy(
            src_ref=blocks_ref.at[source],
            dst_ref=slots.at[source],
            send_sem=send_sems.at[step],
            recv_sem=recv_sems.at[source],
            device_id=member(source),
            device_id_type=pl.DeviceIdType.MESH,
        ).wait_recv()
    total = slots[0]
    for slot in range(1, count):
        total = total + slots[slot]
    out_ref[...] = total


def sum_over_group(blocks, axis, kernel_id):
    count = blocks.shape[0]
    return pl.pallas_call(
        functools.partial(group_sum_kernel, axis),
        out_shape=jax.ShapeDtypeStruct(blocks.shape[1:], blocks.dtype),
        in_specs=[pl.BlockSpec(memory_space=pltpu.VMEM)],
        out_specs=pl.BlockSpec(memory_space=pltpu.VMEM),
        scratch_shapes=[
            pltpu.VMEM(blocks.shape, blocks.dtype),
            pltpu.SemaphoreType.DMA(()),
            pltpu.SemaphoreType.DMA((count,)),
            pltpu.SemaphoreType.DMA((count,)),
        ],
        compiler_params=pltpu.CompilerParams(collective_id=kernel_id, has_side_effects=True),
    )(blocks)


def split_lanes(merged, lanes):
    return tuple(
        merged[..., start : start + lanes] for start in range(0, merged.shape[-1], lanes)
    )


def tables(rows_out, cols_in, period):
    row_index = lax.broadcasted_iota(jnp.int32, (rows_out, cols_in), 0)
    col_index = lax.broadcasted_iota(jnp.int32, (rows_out, cols_in), 1)
    phase_angle = (row_index * col_index % period).astype(jnp.float32) * (2.0 * math.pi / period)
    return (jnp.cos(phase_angle), jnp.sin(phase_angle))


def odd_tables(rows_out, cols_in, period, odd_axis):
    row_index = lax.broadcasted_iota(jnp.int32, (rows_out, cols_in), 0)
    col_index = lax.broadcasted_iota(jnp.int32, (rows_out, cols_in), 1)
    if odd_axis == 0:
        row_index = 2 * row_index + 1
    else:
        col_index = 2 * col_index + 1
    phase_angle = (row_index * col_index % (2 * period)).astype(jnp.float32) * (math.pi / period)
    return (jnp.cos(phase_angle), jnp.sin(phase_angle))


def along_rows(factor, values):
    return jnp.tensordot(factor, values, axes=1, precision=exact_mode)


def rows_spectrum(signal, basis_pair):
    return (along_rows(basis_pair[0], signal), -along_rows(basis_pair[1], signal))


def rows_inverse(complex_pair, basis_pair):
    total = along_rows(basis_pair[0], complex_pair[0]) - along_rows(basis_pair[1], complex_pair[1])
    return total / basis_pair[0].shape[1]


def block_forward(complex_pair, basis_pair):
    cosine_part, sine_part = basis_pair
    real_part = along_rows(cosine_part, complex_pair[0]) + along_rows(sine_part, complex_pair[1])
    imag_part = along_rows(cosine_part, complex_pair[1]) - along_rows(sine_part, complex_pair[0])
    return (real_part, imag_part)


def block_inverse(complex_pair, basis_pair):
    cosine_part, sine_part = basis_pair
    norming = 1.0 / cosine_part.shape[1]
    real_part = along_rows(cosine_part, complex_pair[0]) - along_rows(sine_part, complex_pair[1])
    imag_part = along_rows(cosine_part, complex_pair[1]) + along_rows(sine_part, complex_pair[0])
    return (real_part * norming, imag_part * norming)


def complex_product(first_pair, second_pair):
    return (
        first_pair[0] * second_pair[0] - first_pair[1] * second_pair[1],
        first_pair[0] * second_pair[1] + first_pair[1] * second_pair[0],
    )


def conj_product(first_pair, second_pair):
    return (
        first_pair[0] * second_pair[0] + first_pair[1] * second_pair[1],
        first_pair[0] * second_pair[1] - first_pair[1] * second_pair[0],
    )


def on_device(
    query_proj, key_proj, value_proj, short_filter, long_filter, skip_gain, out_weight, cotangent
):
    block_rows = query_proj.shape[0]
    tap_count = short_filter.shape[1]
    block_count = lax.axis_size(SEQ)
    streams = jnp.stack([query_proj, key_proj, value_proj])
    earlier = from_behind(streams[:, block_rows - (tap_count - 1) :], SEQ, 1)
    extended = jnp.concatenate([earlier, streams], axis=1).astype(jnp.float32)
    shifted = [
        extended[:, tap_count - 1 - offset : tap_count - 1 - offset + block_rows]
        for offset in range(tap_count)
    ]
    filtered = sum(
        (short_filter[:, offset][:, None, :] * shifted[offset] for offset in range(tap_count))
    )
    query_short, key_short, value_short = (filtered[0], filtered[1], filtered[2])
    product = key_short * value_short
    forward_basis = odd_tables(block_rows, block_rows, 2 * block_rows, 0)
    spread_basis = odd_tables(block_rows, 2 * block_rows, 2 * block_rows, 0)
    fold_basis = odd_tables(2 * block_rows, block_rows, 2 * block_rows, 1)
    half_basis = odd_tables(block_rows, block_rows, 2 * block_rows, 1)
    block_basis = tables(2 * block_count, block_count, 2 * block_count)
    return_basis = tables(block_count, 2 * block_count, 2 * block_count)
    input_pair = rows_spectrum(product, forward_basis)
    filter_pair = rows_spectrum(long_filter, forward_basis)
    lanes = product.shape[1]
    moved_data = split_lanes(
        lax.all_to_all(
            jnp.concatenate([input_pair[0], input_pair[1], filter_pair[0], filter_pair[1]], axis=1)[
                None
            ].astype(jnp.bfloat16),
            SEQ,
            split_axis=1,
            concat_axis=0,
            tiled=True,
        ).astype(jnp.float32),
        lanes,
    )
    input_spectrum = block_forward((moved_data[0], moved_data[1]), block_basis)
    filter_spectrum = block_forward((moved_data[2], moved_data[3]), block_basis)
    inverse_pair = block_inverse(complex_product(filter_spectrum, input_spectrum), return_basis)
    returned = split_lanes(
        lax.all_to_all(
            as_sent(jnp.concatenate(inverse_pair, axis=-1)),
            SEQ,
            split_axis=0,
            concat_axis=1,
            tiled=True,
        ).astype(jnp.float32),
        lanes,
    )
    folded = rows_inverse((returned[0][0], returned[1][0]), fold_basis)
    carried = from_behind(folded[block_rows:], SEQ, 1)
    convolved = folded[:block_rows] + carried
    mixed_seq = convolved + skip_gain * product
    gated_values = (query_short * mixed_seq).astype(jnp.bfloat16)
    full_cotangent = lax.all_gather(cotangent, "ch", axis=1, tiled=True)
    full_cotangent, gated_values = lax.optimization_barrier((full_cotangent, gated_values))
    partial_value = jnp.dot(gated_values, out_weight, preferred_element_type=jnp.float32)
    layer_out = lax.psum_scatter(partial_value, "ch", scatter_dimension=1, tiled=True).astype(
        jnp.bfloat16
    )
    grad_gated = lax.dot_general(
        full_cotangent, out_weight, (((1,), (1,)), ((), ())), preferred_element_type=jnp.float32
    )
    outer = lax.axis_size("seq_hi")
    inner = lax.axis_size("seq_lo")
    feature_rows = full_cotangent.shape[1] // outer // inner
    local_rows = lax.all_gather(gated_values, "seq_hi", axis=0, tiled=True)
    local_features = lax.all_to_all(
        full_cotangent.reshape(block_rows, outer, inner, feature_rows),
        "seq_hi",
        split_axis=1,
        concat_axis=0,
        tiled=True,
    ).reshape(block_rows * outer, -1)
    weight_terms = lax.dot_general(
        local_features,
        local_rows,
        (((0,), (0,)), ((), ())),
        preferred_element_type=jnp.float32,
    )
    grad_mixed = grad_gated * query_short
    grad_query_short = grad_gated * mixed_seq
    following = from_behind(grad_mixed.astype(jnp.bfloat16), SEQ, -1).astype(grad_mixed.dtype)
    spread = jnp.concatenate([grad_mixed, following], axis=0)
    grad_pair = rows_spectrum(spread, spread_basis)
    moved_grad = split_lanes(
        lax.all_to_all(
            jnp.concatenate(grad_pair, axis=1)[None].astype(jnp.bfloat16),
            SEQ,
            split_axis=1,
            concat_axis=0,
            tiled=True,
        ).astype(jnp.float32),
        lanes,
    )
    grad_spectrum = block_forward(moved_grad, block_basis)
    input_back = block_inverse(conj_product(filter_spectrum, grad_spectrum), return_basis)
    filter_back = block_inverse(conj_product(input_spectrum, grad_spectrum), return_basis)
    returned_grad = split_lanes(
        lax.all_to_all(
            as_sent(jnp.concatenate(input_back + filter_back, axis=-1)),
            SEQ,
            split_axis=0,
            concat_axis=1,
            tiled=True,
        ),
        lanes,
    )
    grad_w_out_t = lax.psum_scatter(weight_terms, "seq_lo", scatter_dimension=0, tiled=True)
    grad_w_out_t, layer_out, returned_grad = lax.optimization_barrier(
        (grad_w_out_t, layer_out, returned_grad)
    )
    conv_grad = rows_inverse((returned_grad[0][0], returned_grad[1][0]), half_basis)
    grad_filter = rows_inverse((returned_grad[2][0], returned_grad[3][0]), half_basis)
    grad_product = conv_grad + skip_gain * grad_mixed
    grad_streams = jnp.stack(
        [grad_query_short, grad_product * value_short, grad_product * key_short]
    )
    later_rows = from_behind(grad_streams[:, : tap_count - 1], SEQ, -1)
    padded_grad = jnp.concatenate([grad_streams, later_rows], axis=1)
    grad_inputs = sum(
        (
            short_filter[:, offset][:, None, :] * padded_grad[:, offset : offset + block_rows]
            for offset in range(tap_count)
        )
    )
    short_terms = jnp.stack(
        [jnp.sum(grad_streams * shifted[offset], axis=1) for offset in range(tap_count)], axis=1
    )
    skip_terms = jnp.sum(grad_mixed * product, axis=0)
    channel_count = skip_terms.shape[0]
    sum_rows = short_terms.shape[0] * short_terms.shape[1] + 1
    padded_rows = -(-sum_rows // 8) * 8
    small_terms = jnp.concatenate(
        [
            short_terms.reshape(sum_rows - 1, channel_count),
            skip_terms[None],
            jnp.zeros((padded_rows - sum_rows, channel_count), jnp.float32),
        ]
    )
    outer_sum = sum_over_group(
        jnp.broadcast_to(small_terms, (outer,) + small_terms.shape), "seq_hi", 0
    )
    summed = sum_over_group(
        jnp.broadcast_to(outer_sum, (inner,) + outer_sum.shape), "seq_lo", 1
    )
    grad_short = summed[: sum_rows - 1].reshape(short_terms.shape)
    grad_skip = summed[sum_rows - 1]
    return (
        layer_out,
        grad_inputs[0],
        grad_inputs[1],
        grad_inputs[2],
        grad_short,
        grad_filter,
        grad_skip,
        grad_w_out_t,
    )


def solution(mesh):
    in_specs = (
        P(SEQ, "ch"),
        P(SEQ, "ch"),
        P(SEQ, "ch"),
        P(None, None, "ch"),
        P(SEQ, "ch"),
        P("ch"),
        P("ch", None),
        P(SEQ, "ch"),
    )
    out_specs = (
        P(SEQ, "ch"),
        P(SEQ, "ch"),
        P(SEQ, "ch"),
        P(SEQ, "ch"),
        P(None, None, "ch"),
        P(SEQ, "ch"),
        P("ch"),
        P(SEQ, "ch"),
    )
    inner = 8
    seq_mesh = jax.sharding.Mesh(
        mesh.devices.reshape(mesh.shape["seq"] // inner, inner, mesh.shape["ch"]),
        ("seq_hi", "seq_lo", "ch"),
    )
    return jax.shard_map(
        on_device, mesh=seq_mesh, in_specs=in_specs, out_specs=out_specs, check_vma=False
    )
```

```python
import functools
import math

import jax
import jax.numpy as jnp
from jax import lax
from jax.experimental import pallas as pl
from jax.experimental.pallas import tpu as pltpu
from jax.sharding import PartitionSpec as P

exact_mode = lax.Precision.HIGHEST
SEQ = ("seq_hi", "seq_mid", "core")
LOW = ("seq_mid", "core")


def from_behind(shard, axis, by):
    size = lax.axis_size(axis)
    pairs = [(i, i + by) for i in range(size) if 0 <= i + by < size]
    return lax.ppermute(shard, axis, pairs)


def as_sent(shard):

    def short(part):
        return part.astype(jnp.bfloat16) if part.dtype == jnp.float32 else part

    return jax.tree.map(short, shard)


def group_sum_kernel(axis, blocks_ref, out_ref, slots, local_sem, send_sems, recv_sems):
    names = axis if isinstance(axis, tuple) else (axis,)
    count = lax.axis_size(names)
    me = lax.axis_index(names)

    def member(index):
        where = {name: lax.axis_index(name) for name in SEQ}
        for name in reversed(names):
            where[name] = index % lax.axis_size(name)
            index = index // lax.axis_size(name)
        return tuple(where[name] for name in SEQ) + (lax.axis_index("ch"),)

    barrier = pltpu.get_barrier_semaphore()
    for step in range(1, count):
        pl.semaphore_signal(
            barrier,
            1,
            device_id=member(lax.rem(me + step, count)),
            device_id_type=pl.DeviceIdType.MESH,
        )
    pl.semaphore_wait(barrier, count - 1)
    own = pltpu.make_async_copy(blocks_ref.at[me], slots.at[me], local_sem)
    own.start()
    outgoing = []
    for step in range(1, count):
        peer = lax.rem(me + step, count)
        copy = pltpu.make_async_remote_copy(
            src_ref=blocks_ref.at[peer],
            dst_ref=slots.at[me],
            send_sem=send_sems.at[step],
            recv_sem=recv_sems.at[me],
            device_id=member(peer),
            device_id_type=pl.DeviceIdType.MESH,
        )
        copy.start()
        outgoing.append(copy)
    own.wait()
    for step in range(1, count):
        source = lax.rem(me + count - step, count)
        outgoing[step - 1].wait_send()
        pltpu.make_async_remote_copy(
            src_ref=blocks_ref.at[source],
            dst_ref=slots.at[source],
            send_sem=send_sems.at[step],
            recv_sem=recv_sems.at[source],
            device_id=member(source),
            device_id_type=pl.DeviceIdType.MESH,
        ).wait_recv()
    total = slots[0]
    for slot in range(1, count):
        total = total + slots[slot]
    out_ref[...] = total


def sum_over_group(blocks, axis, kernel_id):
    count = blocks.shape[0]
    return pl.pallas_call(
        functools.partial(group_sum_kernel, axis),
        out_shape=jax.ShapeDtypeStruct(blocks.shape[1:], blocks.dtype),
        in_specs=[pl.BlockSpec(memory_space=pltpu.VMEM)],
        out_specs=pl.BlockSpec(memory_space=pltpu.VMEM),
        scratch_shapes=[
            pltpu.VMEM(blocks.shape, blocks.dtype),
            pltpu.SemaphoreType.DMA(()),
            pltpu.SemaphoreType.DMA((count,)),
            pltpu.SemaphoreType.DMA((count,)),
        ],
        compiler_params=pltpu.CompilerParams(collective_id=kernel_id, has_side_effects=True),
    )(blocks)


def split_lanes(merged, lanes):
    return tuple(
        merged[..., start : start + lanes] for start in range(0, merged.shape[-1], lanes)
    )


def tables(rows_out, cols_in, period):
    row_index = lax.broadcasted_iota(jnp.int32, (rows_out, cols_in), 0)
    col_index = lax.broadcasted_iota(jnp.int32, (rows_out, cols_in), 1)
    phase_angle = (row_index * col_index % period).astype(jnp.float32) * (2.0 * math.pi / period)
    return (jnp.cos(phase_angle), jnp.sin(phase_angle))


def odd_tables(rows_out, cols_in, period, odd_axis):
    row_index = lax.broadcasted_iota(jnp.int32, (rows_out, cols_in), 0)
    col_index = lax.broadcasted_iota(jnp.int32, (rows_out, cols_in), 1)
    if odd_axis == 0:
        row_index = 2 * row_index + 1
    else:
        col_index = 2 * col_index + 1
    phase_angle = (row_index * col_index % (2 * period)).astype(jnp.float32) * (math.pi / period)
    return (jnp.cos(phase_angle), jnp.sin(phase_angle))


def along_rows(factor, values):
    return jnp.tensordot(factor, values, axes=1, precision=exact_mode)


def rows_spectrum(signal, basis_pair):
    return (along_rows(basis_pair[0], signal), -along_rows(basis_pair[1], signal))


def rows_inverse(complex_pair, basis_pair):
    total = along_rows(basis_pair[0], complex_pair[0]) - along_rows(basis_pair[1], complex_pair[1])
    return total / basis_pair[0].shape[1]


def block_forward(complex_pair, basis_pair):
    cosine_part, sine_part = basis_pair
    real_part = along_rows(cosine_part, complex_pair[0]) + along_rows(sine_part, complex_pair[1])
    imag_part = along_rows(cosine_part, complex_pair[1]) - along_rows(sine_part, complex_pair[0])
    return (real_part, imag_part)


def block_inverse(complex_pair, basis_pair):
    cosine_part, sine_part = basis_pair
    norming = 1.0 / cosine_part.shape[1]
    real_part = along_rows(cosine_part, complex_pair[0]) - along_rows(sine_part, complex_pair[1])
    imag_part = along_rows(cosine_part, complex_pair[1]) + along_rows(sine_part, complex_pair[0])
    return (real_part * norming, imag_part * norming)


def complex_product(first_pair, second_pair):
    return (
        first_pair[0] * second_pair[0] - first_pair[1] * second_pair[1],
        first_pair[0] * second_pair[1] + first_pair[1] * second_pair[0],
    )


def conj_product(first_pair, second_pair):
    return (
        first_pair[0] * second_pair[0] + first_pair[1] * second_pair[1],
        first_pair[0] * second_pair[1] - first_pair[1] * second_pair[0],
    )


def on_device(
    query_proj, key_proj, value_proj, short_filter, long_filter, skip_gain, out_weight, cotangent
):
    block_rows = query_proj.shape[0]
    tap_count = short_filter.shape[1]
    block_count = lax.axis_size(SEQ)
    streams = jnp.stack([query_proj, key_proj, value_proj])
    earlier = from_behind(streams[:, block_rows - (tap_count - 1) :], SEQ, 1)
    extended = jnp.concatenate([earlier, streams], axis=1).astype(jnp.float32)
    shifted = [
        extended[:, tap_count - 1 - offset : tap_count - 1 - offset + block_rows]
        for offset in range(tap_count)
    ]
    filtered = sum(
        (short_filter[:, offset][:, None, :] * shifted[offset] for offset in range(tap_count))
    )
    query_short, key_short, value_short = (filtered[0], filtered[1], filtered[2])
    product = key_short * value_short
    forward_basis = odd_tables(block_rows, block_rows, 2 * block_rows, 0)
    spread_basis = odd_tables(block_rows, 2 * block_rows, 2 * block_rows, 0)
    fold_basis = odd_tables(2 * block_rows, block_rows, 2 * block_rows, 1)
    half_basis = odd_tables(block_rows, block_rows, 2 * block_rows, 1)
    block_basis = tables(2 * block_count, block_count, 2 * block_count)
    return_basis = tables(block_count, 2 * block_count, 2 * block_count)
    input_pair = rows_spectrum(product, forward_basis)
    filter_pair = rows_spectrum(long_filter, forward_basis)
    lanes = product.shape[1]
    moved_data = split_lanes(
        lax.all_to_all(
            jnp.concatenate([input_pair[0], input_pair[1], filter_pair[0], filter_pair[1]], axis=1)[
                None
            ].astype(jnp.bfloat16),
            SEQ,
            split_axis=1,
            concat_axis=0,
            tiled=True,
        ).astype(jnp.float32),
        lanes,
    )
    input_spectrum = block_forward((moved_data[0], moved_data[1]), block_basis)
    filter_spectrum = block_forward((moved_data[2], moved_data[3]), block_basis)
    inverse_pair = block_inverse(complex_product(filter_spectrum, input_spectrum), return_basis)
    returned = split_lanes(
        lax.all_to_all(
            as_sent(jnp.concatenate(inverse_pair, axis=-1)),
            SEQ,
            split_axis=0,
            concat_axis=1,
            tiled=True,
        ).astype(jnp.float32),
        lanes,
    )
    folded = rows_inverse((returned[0][0], returned[1][0]), fold_basis)
    carried = from_behind(folded[block_rows:], SEQ, 1)
    convolved = folded[:block_rows] + carried
    mixed_seq = convolved + skip_gain * product
    gated_values = (query_short * mixed_seq).astype(jnp.bfloat16)
    full_cotangent = lax.all_gather(cotangent, "ch", axis=1, tiled=True)
    full_cotangent, gated_values = lax.optimization_barrier((full_cotangent, gated_values))
    partial_value = jnp.dot(gated_values, out_weight, preferred_element_type=jnp.float32)
    layer_out = lax.psum_scatter(partial_value, "ch", scatter_dimension=1, tiled=True).astype(
        jnp.bfloat16
    )
    grad_gated = lax.dot_general(
        full_cotangent, out_weight, (((1,), (1,)), ((), ())), preferred_element_type=jnp.float32
    )
    outer = lax.axis_size("seq_hi")
    inner = lax.axis_size(LOW)
    pairs = lax.axis_size(("seq_hi", "seq_mid"))
    cores = lax.axis_size("core")
    feature_rows = full_cotangent.shape[1] // pairs // cores
    local_rows = lax.all_gather(gated_values, "core", axis=0, tiled=True)
    local_features = lax.all_to_all(
        full_cotangent.reshape(block_rows, pairs, cores, feature_rows),
        "core",
        split_axis=2,
        concat_axis=0,
        tiled=True,
    ).reshape(block_rows * cores, -1)
    weight_terms = lax.dot_general(
        local_features,
        local_rows,
        (((0,), (0,)), ((), ())),
        preferred_element_type=jnp.float32,
    )
    grad_mixed = grad_gated * query_short
    grad_query_short = grad_gated * mixed_seq
    following = from_behind(grad_mixed.astype(jnp.bfloat16), SEQ, -1).astype(grad_mixed.dtype)
    spread = jnp.concatenate([grad_mixed, following], axis=0)
    grad_pair = rows_spectrum(spread, spread_basis)
    moved_grad = split_lanes(
        lax.all_to_all(
            jnp.concatenate(grad_pair, axis=1)[None].astype(jnp.bfloat16),
            SEQ,
            split_axis=1,
            concat_axis=0,
            tiled=True,
        ).astype(jnp.float32),
        lanes,
    )
    grad_spectrum = block_forward(moved_grad, block_basis)
    input_back = block_inverse(conj_product(filter_spectrum, grad_spectrum), return_basis)
    filter_back = block_inverse(conj_product(input_spectrum, grad_spectrum), return_basis)
    returned_grad = split_lanes(
        lax.all_to_all(
            as_sent(jnp.concatenate(input_back + filter_back, axis=-1)),
            SEQ,
            split_axis=0,
            concat_axis=1,
            tiled=True,
        ),
        lanes,
    )
    grad_w_out_t = lax.psum_scatter(
        weight_terms, ("seq_hi", "seq_mid"), scatter_dimension=0, tiled=True
    )
    grad_w_out_t, layer_out, returned_grad = lax.optimization_barrier(
        (grad_w_out_t, layer_out, returned_grad)
    )
    conv_grad = rows_inverse((returned_grad[0][0], returned_grad[1][0]), half_basis)
    grad_filter = rows_inverse((returned_grad[2][0], returned_grad[3][0]), half_basis)
    grad_product = conv_grad + skip_gain * grad_mixed
    grad_streams = jnp.stack(
        [grad_query_short, grad_product * value_short, grad_product * key_short]
    )
    later_rows = from_behind(grad_streams[:, : tap_count - 1], SEQ, -1)
    padded_grad = jnp.concatenate([grad_streams, later_rows], axis=1)
    grad_inputs = sum(
        (
            short_filter[:, offset][:, None, :] * padded_grad[:, offset : offset + block_rows]
            for offset in range(tap_count)
        )
    )
    short_terms = jnp.stack(
        [jnp.sum(grad_streams * shifted[offset], axis=1) for offset in range(tap_count)], axis=1
    )
    skip_terms = jnp.sum(grad_mixed * product, axis=0)
    channel_count = skip_terms.shape[0]
    sum_rows = short_terms.shape[0] * short_terms.shape[1] + 1
    padded_rows = -(-sum_rows // 8) * 8
    small_terms = jnp.concatenate(
        [
            short_terms.reshape(sum_rows - 1, channel_count),
            skip_terms[None],
            jnp.zeros((padded_rows - sum_rows, channel_count), jnp.float32),
        ]
    )
    outer_sum = sum_over_group(
        jnp.broadcast_to(small_terms, (outer,) + small_terms.shape), "seq_hi", 0
    )
    summed = sum_over_group(
        jnp.broadcast_to(outer_sum, (inner,) + outer_sum.shape), LOW, 1
    )
    grad_short = summed[: sum_rows - 1].reshape(short_terms.shape)
    grad_skip = summed[sum_rows - 1]
    return (
        layer_out,
        grad_inputs[0],
        grad_inputs[1],
        grad_inputs[2],
        grad_short,
        grad_filter,
        grad_skip,
        grad_w_out_t,
    )


def solution(mesh):
    in_specs = (
        P(SEQ, "ch"),
        P(SEQ, "ch"),
        P(SEQ, "ch"),
        P(None, None, "ch"),
        P(SEQ, "ch"),
        P("ch"),
        P("ch", None),
        P(SEQ, "ch"),
    )
    out_specs = (
        P(SEQ, "ch"),
        P(SEQ, "ch"),
        P(SEQ, "ch"),
        P(SEQ, "ch"),
        P(None, None, "ch"),
        P(SEQ, "ch"),
        P("ch"),
        P(SEQ, "ch"),
    )
    cores = 2
    middle = 4
    seq_mesh = jax.sharding.Mesh(
        mesh.devices.reshape(
            mesh.shape["seq"] // (middle * cores), middle, cores, mesh.shape["ch"]
        ),
        SEQ + ("ch",),
    )
    return jax.shard_map(
        on_device, mesh=seq_mesh, in_specs=in_specs, out_specs=out_specs, check_vma=False
    )
```

```python
import functools
import math

import jax
import jax.numpy as jnp
from jax import lax
from jax.experimental import pallas as pl
from jax.experimental.pallas import tpu as pltpu
from jax.sharding import PartitionSpec as P

exact_mode = lax.Precision.HIGH
SEQ = ("seq_hi", "seq_lo")


def from_behind(shard, axis, by):
    size = lax.axis_size(axis)
    pairs = [(i, i + by) for i in range(size) if 0 <= i + by < size]
    return lax.ppermute(shard, axis, pairs)


def as_sent(shard):

    def short(part):
        return part.astype(jnp.bfloat16) if part.dtype == jnp.float32 else part

    return jax.tree.map(short, shard)


def group_sum_kernel(axis, blocks_ref, out_ref, slots, local_sem, send_sems, recv_sems):
    count = lax.axis_size(axis)
    me = lax.axis_index(axis)
    place = {"seq_hi": lax.axis_index("seq_hi"), "seq_lo": lax.axis_index("seq_lo")}

    def member(index):
        where = dict(place, **{axis: index})
        return (where["seq_hi"], where["seq_lo"], lax.axis_index("ch"))

    barrier = pltpu.get_barrier_semaphore()
    for step in range(1, count):
        pl.semaphore_signal(
            barrier,
            1,
            device_id=member(lax.rem(me + step, count)),
            device_id_type=pl.DeviceIdType.MESH,
        )
    pl.semaphore_wait(barrier, count - 1)
    own = pltpu.make_async_copy(blocks_ref.at[me], slots.at[me], local_sem)
    own.start()
    outgoing = []
    for step in range(1, count):
        peer = lax.rem(me + step, count)
        copy = pltpu.make_async_remote_copy(
            src_ref=blocks_ref.at[peer],
            dst_ref=slots.at[me],
            send_sem=send_sems.at[step],
            recv_sem=recv_sems.at[me],
            device_id=member(peer),
            device_id_type=pl.DeviceIdType.MESH,
        )
        copy.start()
        outgoing.append(copy)
    own.wait()
    for step in range(1, count):
        source = lax.rem(me + count - step, count)
        outgoing[step - 1].wait_send()
        pltpu.make_async_remote_copy(
            src_ref=blocks_ref.at[source],
            dst_ref=slots.at[source],
            send_sem=send_sems.at[step],
            recv_sem=recv_sems.at[source],
            device_id=member(source),
            device_id_type=pl.DeviceIdType.MESH,
        ).wait_recv()
    total = slots[0]
    for slot in range(1, count):
        total = total + slots[slot]
    out_ref[...] = total


def sum_over_group(blocks, axis, kernel_id):
    count = blocks.shape[0]
    return pl.pallas_call(
        functools.partial(group_sum_kernel, axis),
        out_shape=jax.ShapeDtypeStruct(blocks.shape[1:], blocks.dtype),
        in_specs=[pl.BlockSpec(memory_space=pltpu.VMEM)],
        out_specs=pl.BlockSpec(memory_space=pltpu.VMEM),
        scratch_shapes=[
            pltpu.VMEM(blocks.shape, blocks.dtype),
            pltpu.SemaphoreType.DMA(()),
            pltpu.SemaphoreType.DMA((count,)),
            pltpu.SemaphoreType.DMA((count,)),
        ],
        compiler_params=pltpu.CompilerParams(collective_id=kernel_id, has_side_effects=True),
    )(blocks)


def split_lanes(merged, lanes):
    return tuple(
        merged[..., start : start + lanes] for start in range(0, merged.shape[-1], lanes)
    )


def tables(rows_out, cols_in, period):
    row_index = lax.broadcasted_iota(jnp.int32, (rows_out, cols_in), 0)
    col_index = lax.broadcasted_iota(jnp.int32, (rows_out, cols_in), 1)
    phase_angle = (row_index * col_index % period).astype(jnp.float32) * (2.0 * math.pi / period)
    return (jnp.cos(phase_angle), jnp.sin(phase_angle))


def odd_tables(rows_out, cols_in, period, odd_axis):
    row_index = lax.broadcasted_iota(jnp.int32, (rows_out, cols_in), 0)
    col_index = lax.broadcasted_iota(jnp.int32, (rows_out, cols_in), 1)
    if odd_axis == 0:
        row_index = 2 * row_index + 1
    else:
        col_index = 2 * col_index + 1
    phase_angle = (row_index * col_index % (2 * period)).astype(jnp.float32) * (math.pi / period)
    return (jnp.cos(phase_angle), jnp.sin(phase_angle))


def along_rows(factor, values):
    return jnp.tensordot(factor, values, axes=1, precision=exact_mode)


def rows_spectrum(signal, basis_pair):
    return (along_rows(basis_pair[0], signal), -along_rows(basis_pair[1], signal))


def rows_inverse(complex_pair, basis_pair):
    total = along_rows(basis_pair[0], complex_pair[0]) - along_rows(basis_pair[1], complex_pair[1])
    return total / basis_pair[0].shape[1]


def block_forward(complex_pair, basis_pair):
    cosine_part, sine_part = basis_pair
    real_part = along_rows(cosine_part, complex_pair[0]) + along_rows(sine_part, complex_pair[1])
    imag_part = along_rows(cosine_part, complex_pair[1]) - along_rows(sine_part, complex_pair[0])
    return (real_part, imag_part)


def block_inverse(complex_pair, basis_pair):
    cosine_part, sine_part = basis_pair
    norming = 1.0 / cosine_part.shape[1]
    real_part = along_rows(cosine_part, complex_pair[0]) - along_rows(sine_part, complex_pair[1])
    imag_part = along_rows(cosine_part, complex_pair[1]) + along_rows(sine_part, complex_pair[0])
    return (real_part * norming, imag_part * norming)


def complex_product(first_pair, second_pair):
    return (
        first_pair[0] * second_pair[0] - first_pair[1] * second_pair[1],
        first_pair[0] * second_pair[1] + first_pair[1] * second_pair[0],
    )


def conj_product(first_pair, second_pair):
    return (
        first_pair[0] * second_pair[0] + first_pair[1] * second_pair[1],
        first_pair[0] * second_pair[1] - first_pair[1] * second_pair[0],
    )


def on_device(
    query_proj, key_proj, value_proj, short_filter, long_filter, skip_gain, out_weight, cotangent
):
    block_rows = query_proj.shape[0]
    tap_count = short_filter.shape[1]
    block_count = lax.axis_size(SEQ)
    streams = jnp.stack([query_proj, key_proj, value_proj])
    earlier = from_behind(streams[:, block_rows - (tap_count - 1) :], SEQ, 1)
    extended = jnp.concatenate([earlier, streams], axis=1).astype(jnp.float32)
    shifted = [
        extended[:, tap_count - 1 - offset : tap_count - 1 - offset + block_rows]
        for offset in range(tap_count)
    ]
    filtered = sum(
        (short_filter[:, offset][:, None, :] * shifted[offset] for offset in range(tap_count))
    )
    query_short, key_short, value_short = (filtered[0], filtered[1], filtered[2])
    product = key_short * value_short
    forward_basis = odd_tables(block_rows, block_rows, 2 * block_rows, 0)
    spread_basis = odd_tables(block_rows, 2 * block_rows, 2 * block_rows, 0)
    fold_basis = odd_tables(2 * block_rows, block_rows, 2 * block_rows, 1)
    half_basis = odd_tables(block_rows, block_rows, 2 * block_rows, 1)
    block_basis = tables(2 * block_count, block_count, 2 * block_count)
    return_basis = tables(block_count, 2 * block_count, 2 * block_count)
    input_pair = rows_spectrum(product, forward_basis)
    filter_pair = rows_spectrum(long_filter, forward_basis)
    lanes = product.shape[1]
    moved_data = split_lanes(
        lax.all_to_all(
            jnp.concatenate([input_pair[0], input_pair[1], filter_pair[0], filter_pair[1]], axis=1)[
                None
            ].astype(jnp.bfloat16),
            SEQ,
            split_axis=1,
            concat_axis=0,
            tiled=True,
        ).astype(jnp.float32),
        lanes,
    )
    input_spectrum = block_forward((moved_data[0], moved_data[1]), block_basis)
    filter_spectrum = block_forward((moved_data[2], moved_data[3]), block_basis)
    inverse_pair = block_inverse(complex_product(filter_spectrum, input_spectrum), return_basis)
    returned = split_lanes(
        lax.all_to_all(
            as_sent(jnp.concatenate(inverse_pair, axis=-1)),
            SEQ,
            split_axis=0,
            concat_axis=1,
            tiled=True,
        ).astype(jnp.float32),
        lanes,
    )
    folded = rows_inverse((returned[0][0], returned[1][0]), fold_basis)
    carried = from_behind(folded[block_rows:], SEQ, 1)
    convolved = folded[:block_rows] + carried
    mixed_seq = convolved + skip_gain * product
    gated_values = (query_short * mixed_seq).astype(jnp.bfloat16)
    full_cotangent = lax.all_gather(cotangent, "ch", axis=1, tiled=True)
    full_cotangent, gated_values = lax.optimization_barrier((full_cotangent, gated_values))
    partial_value = jnp.dot(gated_values, out_weight, preferred_element_type=jnp.float32)
    layer_out = lax.psum_scatter(partial_value, "ch", scatter_dimension=1, tiled=True).astype(
        jnp.bfloat16
    )
    grad_gated = lax.dot_general(
        full_cotangent, out_weight, (((1,), (1,)), ((), ())), preferred_element_type=jnp.float32
    )
    outer = lax.axis_size("seq_hi")
    inner = lax.axis_size("seq_lo")
    feature_rows = full_cotangent.shape[1] // outer // inner
    local_rows = lax.all_gather(gated_values, "seq_hi", axis=0, tiled=True)
    local_features = lax.all_to_all(
        full_cotangent.reshape(block_rows, outer, inner, feature_rows),
        "seq_hi",
        split_axis=1,
        concat_axis=0,
        tiled=True,
    ).reshape(block_rows * outer, -1)
    weight_terms = lax.dot_general(
        local_features,
        local_rows,
        (((0,), (0,)), ((), ())),
        preferred_element_type=jnp.float32,
    )
    grad_mixed = grad_gated * query_short
    grad_query_short = grad_gated * mixed_seq
    following = from_behind(grad_mixed.astype(jnp.bfloat16), SEQ, -1).astype(grad_mixed.dtype)
    spread = jnp.concatenate([grad_mixed, following], axis=0)
    grad_pair = rows_spectrum(spread, spread_basis)
    moved_grad = split_lanes(
        lax.all_to_all(
            jnp.concatenate(grad_pair, axis=1)[None].astype(jnp.bfloat16),
            SEQ,
            split_axis=1,
            concat_axis=0,
            tiled=True,
        ).astype(jnp.float32),
        lanes,
    )
    grad_spectrum = block_forward(moved_grad, block_basis)
    input_back = block_inverse(conj_product(filter_spectrum, grad_spectrum), return_basis)
    filter_back = block_inverse(conj_product(input_spectrum, grad_spectrum), return_basis)
    returned_grad = split_lanes(
        lax.all_to_all(
            as_sent(jnp.concatenate(input_back + filter_back, axis=-1)),
            SEQ,
            split_axis=0,
            concat_axis=1,
            tiled=True,
        ),
        lanes,
    )
    grad_w_out_t = lax.psum_scatter(weight_terms, "seq_lo", scatter_dimension=0, tiled=True)
    grad_w_out_t, layer_out, returned_grad = lax.optimization_barrier(
        (grad_w_out_t, layer_out, returned_grad)
    )
    conv_grad = rows_inverse((returned_grad[0][0], returned_grad[1][0]), half_basis)
    grad_filter = rows_inverse((returned_grad[2][0], returned_grad[3][0]), half_basis)
    grad_product = conv_grad + skip_gain * grad_mixed
    grad_streams = jnp.stack(
        [grad_query_short, grad_product * value_short, grad_product * key_short]
    )
    later_rows = from_behind(grad_streams[:, : tap_count - 1], SEQ, -1)
    padded_grad = jnp.concatenate([grad_streams, later_rows], axis=1)
    grad_inputs = sum(
        (
            short_filter[:, offset][:, None, :] * padded_grad[:, offset : offset + block_rows]
            for offset in range(tap_count)
        )
    )
    short_terms = jnp.stack(
        [jnp.sum(grad_streams * shifted[offset], axis=1) for offset in range(tap_count)], axis=1
    )
    skip_terms = jnp.sum(grad_mixed * product, axis=0)
    channel_count = skip_terms.shape[0]
    sum_rows = short_terms.shape[0] * short_terms.shape[1] + 1
    padded_rows = -(-sum_rows // 8) * 8
    small_terms = jnp.concatenate(
        [
            short_terms.reshape(sum_rows - 1, channel_count),
            skip_terms[None],
            jnp.zeros((padded_rows - sum_rows, channel_count), jnp.float32),
        ]
    )
    outer_sum = sum_over_group(
        jnp.broadcast_to(small_terms, (outer,) + small_terms.shape), "seq_hi", 0
    )
    summed = sum_over_group(
        jnp.broadcast_to(outer_sum, (inner,) + outer_sum.shape), "seq_lo", 1
    )
    grad_short = summed[: sum_rows - 1].reshape(short_terms.shape)
    grad_skip = summed[sum_rows - 1]
    return (
        layer_out,
        grad_inputs[0],
        grad_inputs[1],
        grad_inputs[2],
        grad_short,
        grad_filter,
        grad_skip,
        grad_w_out_t,
    )


def solution(mesh):
    in_specs = (
        P(SEQ, "ch"),
        P(SEQ, "ch"),
        P(SEQ, "ch"),
        P(None, None, "ch"),
        P(SEQ, "ch"),
        P("ch"),
        P("ch", None),
        P(SEQ, "ch"),
    )
    out_specs = (
        P(SEQ, "ch"),
        P(SEQ, "ch"),
        P(SEQ, "ch"),
        P(SEQ, "ch"),
        P(None, None, "ch"),
        P(SEQ, "ch"),
        P("ch"),
        P(SEQ, "ch"),
    )
    inner = 8
    seq_mesh = jax.sharding.Mesh(
        mesh.devices.reshape(mesh.shape["seq"] // inner, inner, mesh.shape["ch"]),
        ("seq_hi", "seq_lo", "ch"),
    )
    return jax.shard_map(
        on_device, mesh=seq_mesh, in_specs=in_specs, out_specs=out_specs, check_vma=False
    )
```

```python
import functools
import math

import jax
import jax.numpy as jnp
from jax import lax
from jax.experimental import pallas as pl
from jax.experimental.pallas import tpu as pltpu
from jax.sharding import PartitionSpec as P

exact_mode = lax.Precision.HIGH
SEQ = ("seq_hi", "seq_lo")


def from_behind(shard, axis, by):
    size = lax.axis_size(axis)
    pairs = [(i, i + by) for i in range(size) if 0 <= i + by < size]
    return lax.ppermute(shard, axis, pairs)


def as_sent(shard):

    def short(part):
        return part.astype(jnp.bfloat16) if part.dtype == jnp.float32 else part

    return jax.tree.map(short, shard)


def group_sum_kernel(axis, blocks_ref, out_ref, slots, local_sem, send_sems, recv_sems):
    count = lax.axis_size(axis)
    me = lax.axis_index(axis)
    place = {"seq_hi": lax.axis_index("seq_hi"), "seq_lo": lax.axis_index("seq_lo")}

    def member(index):
        where = dict(place, **{axis: index})
        return (where["seq_hi"], where["seq_lo"], lax.axis_index("ch"))

    barrier = pltpu.get_barrier_semaphore()
    for step in range(1, count):
        pl.semaphore_signal(
            barrier,
            1,
            device_id=member(lax.rem(me + step, count)),
            device_id_type=pl.DeviceIdType.MESH,
        )
    pl.semaphore_wait(barrier, count - 1)
    own = pltpu.make_async_copy(blocks_ref.at[me], slots.at[me], local_sem)
    own.start()
    outgoing = []
    for step in range(1, count):
        peer = lax.rem(me + step, count)
        copy = pltpu.make_async_remote_copy(
            src_ref=blocks_ref.at[peer],
            dst_ref=slots.at[me],
            send_sem=send_sems.at[step],
            recv_sem=recv_sems.at[me],
            device_id=member(peer),
            device_id_type=pl.DeviceIdType.MESH,
        )
        copy.start()
        outgoing.append(copy)
    own.wait()
    for step in range(1, count):
        source = lax.rem(me + count - step, count)
        outgoing[step - 1].wait_send()
        pltpu.make_async_remote_copy(
            src_ref=blocks_ref.at[source],
            dst_ref=slots.at[source],
            send_sem=send_sems.at[step],
            recv_sem=recv_sems.at[source],
            device_id=member(source),
            device_id_type=pl.DeviceIdType.MESH,
        ).wait_recv()
    total = slots[0]
    for slot in range(1, count):
        total = total + slots[slot]
    out_ref[...] = total


def sum_over_group(blocks, axis, kernel_id):
    count = blocks.shape[0]
    return pl.pallas_call(
        functools.partial(group_sum_kernel, axis),
        out_shape=jax.ShapeDtypeStruct(blocks.shape[1:], blocks.dtype),
        in_specs=[pl.BlockSpec(memory_space=pltpu.VMEM)],
        out_specs=pl.BlockSpec(memory_space=pltpu.VMEM),
        scratch_shapes=[
            pltpu.VMEM(blocks.shape, blocks.dtype),
            pltpu.SemaphoreType.DMA(()),
            pltpu.SemaphoreType.DMA((count,)),
            pltpu.SemaphoreType.DMA((count,)),
        ],
        compiler_params=pltpu.CompilerParams(collective_id=kernel_id, has_side_effects=True),
    )(blocks)


def split_lanes(merged, lanes):
    return tuple(
        merged[..., start : start + lanes] for start in range(0, merged.shape[-1], lanes)
    )


def tables(rows_out, cols_in, period):
    row_index = lax.broadcasted_iota(jnp.int32, (rows_out, cols_in), 0)
    col_index = lax.broadcasted_iota(jnp.int32, (rows_out, cols_in), 1)
    phase_angle = (row_index * col_index % period).astype(jnp.float32) * (2.0 * math.pi / period)
    return (jnp.cos(phase_angle), jnp.sin(phase_angle))


def odd_tables(rows_out, cols_in, period, odd_axis):
    row_index = lax.broadcasted_iota(jnp.int32, (rows_out, cols_in), 0)
    col_index = lax.broadcasted_iota(jnp.int32, (rows_out, cols_in), 1)
    if odd_axis == 0:
        row_index = 2 * row_index + 1
    else:
        col_index = 2 * col_index + 1
    phase_angle = (row_index * col_index % (2 * period)).astype(jnp.float32) * (math.pi / period)
    return (jnp.cos(phase_angle), jnp.sin(phase_angle))


def along_rows(factor, values):
    return jnp.tensordot(factor, values, axes=1, precision=exact_mode)


def rows_spectrum(signal, basis_pair):
    return (along_rows(basis_pair[0], signal), -along_rows(basis_pair[1], signal))


def rows_inverse(complex_pair, basis_pair):
    total = along_rows(basis_pair[0], complex_pair[0]) - along_rows(basis_pair[1], complex_pair[1])
    return total / basis_pair[0].shape[1]


def block_forward(complex_pair, basis_pair):
    cosine_part, sine_part = basis_pair
    real_part = along_rows(cosine_part, complex_pair[0]) + along_rows(sine_part, complex_pair[1])
    imag_part = along_rows(cosine_part, complex_pair[1]) - along_rows(sine_part, complex_pair[0])
    return (real_part, imag_part)


def block_inverse(complex_pair, basis_pair):
    cosine_part, sine_part = basis_pair
    norming = 1.0 / cosine_part.shape[1]
    real_part = along_rows(cosine_part, complex_pair[0]) - along_rows(sine_part, complex_pair[1])
    imag_part = along_rows(cosine_part, complex_pair[1]) + along_rows(sine_part, complex_pair[0])
    return (real_part * norming, imag_part * norming)


def complex_product(first_pair, second_pair):
    return (
        first_pair[0] * second_pair[0] - first_pair[1] * second_pair[1],
        first_pair[0] * second_pair[1] + first_pair[1] * second_pair[0],
    )


def conj_product(first_pair, second_pair):
    return (
        first_pair[0] * second_pair[0] + first_pair[1] * second_pair[1],
        first_pair[0] * second_pair[1] - first_pair[1] * second_pair[0],
    )


def on_device(
    query_proj, key_proj, value_proj, short_filter, long_filter, skip_gain, out_weight, cotangent
):
    block_rows = query_proj.shape[0]
    tap_count = short_filter.shape[1]
    block_count = lax.axis_size(SEQ)
    streams = jnp.stack([query_proj, key_proj, value_proj])
    earlier = from_behind(streams[:, block_rows - (tap_count - 1) :], SEQ, 1)
    extended = jnp.concatenate([earlier, streams], axis=1).astype(jnp.float32)
    shifted = [
        extended[:, tap_count - 1 - offset : tap_count - 1 - offset + block_rows]
        for offset in range(tap_count)
    ]
    filtered = sum(
        (short_filter[:, offset][:, None, :] * shifted[offset] for offset in range(tap_count))
    )
    query_short, key_short, value_short = (filtered[0], filtered[1], filtered[2])
    product = key_short * value_short
    forward_basis = odd_tables(block_rows, block_rows, 2 * block_rows, 0)
    spread_basis = odd_tables(block_rows, 2 * block_rows, 2 * block_rows, 0)
    fold_basis = odd_tables(2 * block_rows, block_rows, 2 * block_rows, 1)
    half_basis = odd_tables(block_rows, block_rows, 2 * block_rows, 1)
    block_basis = tables(2 * block_count, block_count, 2 * block_count)
    return_basis = tables(block_count, 2 * block_count, 2 * block_count)
    input_pair = rows_spectrum(product, forward_basis)
    filter_pair = rows_spectrum(long_filter, forward_basis)
    lanes = product.shape[1]
    moved_data = split_lanes(
        lax.all_to_all(
            jnp.concatenate([input_pair[0], input_pair[1], filter_pair[0], filter_pair[1]], axis=1)[
                None
            ].astype(jnp.bfloat16),
            SEQ,
            split_axis=1,
            concat_axis=0,
            tiled=True,
        ).astype(jnp.float32),
        lanes,
    )
    input_spectrum = block_forward((moved_data[0], moved_data[1]), block_basis)
    filter_spectrum = block_forward((moved_data[2], moved_data[3]), block_basis)
    inverse_pair = block_inverse(complex_product(filter_spectrum, input_spectrum), return_basis)
    returned = split_lanes(
        lax.all_to_all(
            as_sent(jnp.concatenate(inverse_pair, axis=-1)),
            SEQ,
            split_axis=0,
            concat_axis=1,
            tiled=True,
        ).astype(jnp.float32),
        lanes,
    )
    folded = rows_inverse((returned[0][0], returned[1][0]), fold_basis)
    carried = from_behind(folded[block_rows:], SEQ, 1)
    convolved = folded[:block_rows] + carried
    mixed_seq = convolved + skip_gain * product
    gated_values = (query_short * mixed_seq).astype(jnp.bfloat16)
    full_cotangent = lax.all_gather(cotangent, "ch", axis=1, tiled=True)
    full_cotangent, gated_values = lax.optimization_barrier((full_cotangent, gated_values))
    partial_value = jnp.dot(gated_values, out_weight, preferred_element_type=jnp.float32)
    layer_out = lax.psum_scatter(partial_value, "ch", scatter_dimension=1, tiled=True).astype(
        jnp.bfloat16
    )
    grad_gated = lax.dot_general(
        full_cotangent, out_weight, (((1,), (1,)), ((), ())), preferred_element_type=jnp.float32
    )
    outer = lax.axis_size("seq_hi")
    inner = lax.axis_size("seq_lo")
    feature_rows = full_cotangent.shape[1] // outer // inner
    local_rows = lax.all_gather(gated_values, "seq_lo", axis=0, tiled=True)
    local_features = lax.all_to_all(
        full_cotangent.reshape(block_rows, outer, inner, feature_rows),
        "seq_lo",
        split_axis=2,
        concat_axis=0,
        tiled=True,
    ).reshape(block_rows * inner, -1)
    weight_terms = lax.dot_general(
        local_features,
        local_rows,
        (((0,), (0,)), ((), ())),
        preferred_element_type=jnp.float32,
    )
    grad_mixed = grad_gated * query_short
    grad_query_short = grad_gated * mixed_seq
    following = from_behind(grad_mixed.astype(jnp.bfloat16), SEQ, -1).astype(grad_mixed.dtype)
    spread = jnp.concatenate([grad_mixed, following], axis=0)
    grad_pair = rows_spectrum(spread, spread_basis)
    moved_grad = split_lanes(
        lax.all_to_all(
            jnp.concatenate(grad_pair, axis=1)[None].astype(jnp.bfloat16),
            SEQ,
            split_axis=1,
            concat_axis=0,
            tiled=True,
        ).astype(jnp.float32),
        lanes,
    )
    grad_spectrum = block_forward(moved_grad, block_basis)
    input_back = block_inverse(conj_product(filter_spectrum, grad_spectrum), return_basis)
    filter_back = block_inverse(conj_product(input_spectrum, grad_spectrum), return_basis)
    returned_grad = split_lanes(
        lax.all_to_all(
            as_sent(jnp.concatenate(input_back + filter_back, axis=-1)),
            SEQ,
            split_axis=0,
            concat_axis=1,
            tiled=True,
        ),
        lanes,
    )
    grad_w_out_t = lax.psum_scatter(weight_terms, "seq_hi", scatter_dimension=0, tiled=True)
    grad_w_out_t, layer_out, returned_grad = lax.optimization_barrier(
        (grad_w_out_t, layer_out, returned_grad)
    )
    conv_grad = rows_inverse((returned_grad[0][0], returned_grad[1][0]), half_basis)
    grad_filter = rows_inverse((returned_grad[2][0], returned_grad[3][0]), half_basis)
    grad_product = conv_grad + skip_gain * grad_mixed
    grad_streams = jnp.stack(
        [grad_query_short, grad_product * value_short, grad_product * key_short]
    )
    later_rows = from_behind(grad_streams[:, : tap_count - 1], SEQ, -1)
    padded_grad = jnp.concatenate([grad_streams, later_rows], axis=1)
    grad_inputs = sum(
        (
            short_filter[:, offset][:, None, :] * padded_grad[:, offset : offset + block_rows]
            for offset in range(tap_count)
        )
    )
    short_terms = jnp.stack(
        [jnp.sum(grad_streams * shifted[offset], axis=1) for offset in range(tap_count)], axis=1
    )
    skip_terms = jnp.sum(grad_mixed * product, axis=0)
    channel_count = skip_terms.shape[0]
    sum_rows = short_terms.shape[0] * short_terms.shape[1] + 1
    padded_rows = -(-sum_rows // 8) * 8
    small_terms = jnp.concatenate(
        [
            short_terms.reshape(sum_rows - 1, channel_count),
            skip_terms[None],
            jnp.zeros((padded_rows - sum_rows, channel_count), jnp.float32),
        ]
    )
    outer_sum = sum_over_group(
        jnp.broadcast_to(small_terms, (outer,) + small_terms.shape), "seq_hi", 0
    )
    summed = sum_over_group(
        jnp.broadcast_to(outer_sum, (inner,) + outer_sum.shape), "seq_lo", 1
    )
    grad_short = summed[: sum_rows - 1].reshape(short_terms.shape)
    grad_skip = summed[sum_rows - 1]
    return (
        layer_out,
        grad_inputs[0],
        grad_inputs[1],
        grad_inputs[2],
        grad_short,
        grad_filter,
        grad_skip,
        grad_w_out_t,
    )


def solution(mesh):
    in_specs = (
        P(SEQ, "ch"),
        P(SEQ, "ch"),
        P(SEQ, "ch"),
        P(None, None, "ch"),
        P(SEQ, "ch"),
        P("ch"),
        P("ch", None),
        P(SEQ, "ch"),
    )
    out_specs = (
        P(SEQ, "ch"),
        P(SEQ, "ch"),
        P(SEQ, "ch"),
        P(SEQ, "ch"),
        P(None, None, "ch"),
        P(SEQ, "ch"),
        P("ch"),
        P(SEQ, "ch"),
    )
    inner = 8
    seq_mesh = jax.sharding.Mesh(
        mesh.devices.reshape(mesh.shape["seq"] // inner, inner, mesh.shape["ch"]),
        ("seq_hi", "seq_lo", "ch"),
    )
    return jax.shard_map(
        on_device, mesh=seq_mesh, in_specs=in_specs, out_specs=out_specs, check_vma=False
    )
```

```python
import functools
import math

import jax
import jax.numpy as jnp
from jax import lax
from jax.experimental import pallas as pl
from jax.experimental.pallas import tpu as pltpu
from jax.sharding import PartitionSpec as P

exact_mode = lax.Precision.HIGH
SEQ = ("seq_hi", "seq_lo")


def from_behind(shard, axis, by):
    size = lax.axis_size(axis)
    pairs = [(i, i + by) for i in range(size) if 0 <= i + by < size]
    return lax.ppermute(shard, axis, pairs)


def as_sent(shard):

    def short(part):
        return part.astype(jnp.bfloat16) if part.dtype == jnp.float32 else part

    return jax.tree.map(short, shard)


def group_sum_kernel(axis, shape_out, part_ref, *refs):
    outs = refs[: len(shape_out)]
    slots, local_sem, send_sems, recv_sems = refs[len(shape_out) :]
    count = lax.axis_size(axis)
    me = lax.axis_index(axis)
    place = {"seq_hi": lax.axis_index("seq_hi"), "seq_lo": lax.axis_index("seq_lo")}

    def member(index):
        where = dict(place, **{axis: index})
        return (where["seq_hi"], where["seq_lo"], lax.axis_index("ch"))

    barrier = pltpu.get_barrier_semaphore()
    for step in range(1, count):
        pl.semaphore_signal(
            barrier,
            1,
            device_id=member(lax.rem(me + step, count)),
            device_id_type=pl.DeviceIdType.MESH,
        )
    pl.semaphore_wait(barrier, count - 1)
    own = pltpu.make_async_copy(part_ref, slots.at[me], local_sem)
    own.start()
    outgoing = []
    for step in range(1, count):
        peer = lax.rem(me + step, count)
        copy = pltpu.make_async_remote_copy(
            src_ref=part_ref,
            dst_ref=slots.at[me],
            send_sem=send_sems.at[step],
            recv_sem=recv_sems.at[me],
            device_id=member(peer),
            device_id_type=pl.DeviceIdType.MESH,
        )
        copy.start()
        outgoing.append(copy)
    own.wait()
    for step in range(1, count):
        source = lax.rem(me + count - step, count)
        outgoing[step - 1].wait_send()
        pltpu.make_async_remote_copy(
            src_ref=part_ref,
            dst_ref=slots.at[source],
            send_sem=send_sems.at[step],
            recv_sem=recv_sems.at[source],
            device_id=member(source),
            device_id_type=pl.DeviceIdType.MESH,
        ).wait_recv()
    total = slots[0]
    for slot in range(1, count):
        total = total + slots[slot]
    if len(outs) == 1:
        outs[0][...] = total
        return
    short_ref, skip_ref = outs
    streams, taps = short_ref.shape[0], short_ref.shape[1]
    for stream in range(streams):
        short_ref[stream] = total[stream * taps : (stream + 1) * taps]
    skip_ref[...] = total[streams * taps : streams * taps + 1]


def sum_over_group(part, axis, kernel_id, shape_out=None):
    count = lax.axis_size(axis)
    shape_out = shape_out or (part.shape,)
    return pl.pallas_call(
        functools.partial(group_sum_kernel, axis, shape_out),
        out_shape=[jax.ShapeDtypeStruct(shape, part.dtype) for shape in shape_out],
        in_specs=[pl.BlockSpec(memory_space=pltpu.VMEM)],
        out_specs=[pl.BlockSpec(memory_space=pltpu.VMEM) for _ in shape_out],
        scratch_shapes=[
            pltpu.VMEM((count,) + part.shape, part.dtype),
            pltpu.SemaphoreType.DMA(()),
            pltpu.SemaphoreType.DMA((count,)),
            pltpu.SemaphoreType.DMA((count,)),
        ],
        compiler_params=pltpu.CompilerParams(collective_id=kernel_id, has_side_effects=True),
    )(part)


def split_lanes(merged, lanes):
    return tuple(
        merged[..., start : start + lanes] for start in range(0, merged.shape[-1], lanes)
    )


def tables(rows_out, cols_in, period):
    row_index = lax.broadcasted_iota(jnp.int32, (rows_out, cols_in), 0)
    col_index = lax.broadcasted_iota(jnp.int32, (rows_out, cols_in), 1)
    phase_angle = (row_index * col_index % period).astype(jnp.float32) * (2.0 * math.pi / period)
    return (jnp.cos(phase_angle), jnp.sin(phase_angle))


def odd_tables(rows_out, cols_in, period, odd_axis):
    row_index = lax.broadcasted_iota(jnp.int32, (rows_out, cols_in), 0)
    col_index = lax.broadcasted_iota(jnp.int32, (rows_out, cols_in), 1)
    if odd_axis == 0:
        row_index = 2 * row_index + 1
    else:
        col_index = 2 * col_index + 1
    phase_angle = (row_index * col_index % (2 * period)).astype(jnp.float32) * (math.pi / period)
    return (jnp.cos(phase_angle), jnp.sin(phase_angle))


def along_rows(factor, values):
    return jnp.tensordot(factor, values, axes=1, precision=exact_mode)


def rows_spectrum(signal, basis_pair):
    return (along_rows(basis_pair[0], signal), -along_rows(basis_pair[1], signal))


def rows_inverse(complex_pair, basis_pair):
    total = along_rows(basis_pair[0], complex_pair[0]) - along_rows(basis_pair[1], complex_pair[1])
    return total / basis_pair[0].shape[1]


def block_forward(complex_pair, basis_pair):
    cosine_part, sine_part = basis_pair
    real_part = along_rows(cosine_part, complex_pair[0]) + along_rows(sine_part, complex_pair[1])
    imag_part = along_rows(cosine_part, complex_pair[1]) - along_rows(sine_part, complex_pair[0])
    return (real_part, imag_part)


def block_inverse(complex_pair, basis_pair):
    cosine_part, sine_part = basis_pair
    norming = 1.0 / cosine_part.shape[1]
    real_part = along_rows(cosine_part, complex_pair[0]) - along_rows(sine_part, complex_pair[1])
    imag_part = along_rows(cosine_part, complex_pair[1]) + along_rows(sine_part, complex_pair[0])
    return (real_part * norming, imag_part * norming)


def complex_product(first_pair, second_pair):
    return (
        first_pair[0] * second_pair[0] - first_pair[1] * second_pair[1],
        first_pair[0] * second_pair[1] + first_pair[1] * second_pair[0],
    )


def conj_product(first_pair, second_pair):
    return (
        first_pair[0] * second_pair[0] + first_pair[1] * second_pair[1],
        first_pair[0] * second_pair[1] - first_pair[1] * second_pair[0],
    )


def on_device(
    query_proj, key_proj, value_proj, short_filter, long_filter, skip_gain, out_weight, cotangent
):
    block_rows = query_proj.shape[0]
    tap_count = short_filter.shape[1]
    block_count = lax.axis_size(SEQ)
    streams = jnp.stack([query_proj, key_proj, value_proj])
    earlier = from_behind(streams[:, block_rows - (tap_count - 1) :], SEQ, 1)
    extended = jnp.concatenate([earlier, streams], axis=1).astype(jnp.float32)
    shifted = [
        extended[:, tap_count - 1 - offset : tap_count - 1 - offset + block_rows]
        for offset in range(tap_count)
    ]
    filtered = sum(
        (short_filter[:, offset][:, None, :] * shifted[offset] for offset in range(tap_count))
    )
    query_short, key_short, value_short = (filtered[0], filtered[1], filtered[2])
    product = key_short * value_short
    forward_basis = odd_tables(block_rows, block_rows, 2 * block_rows, 0)
    spread_basis = odd_tables(block_rows, 2 * block_rows, 2 * block_rows, 0)
    fold_basis = odd_tables(2 * block_rows, block_rows, 2 * block_rows, 1)
    half_basis = odd_tables(block_rows, block_rows, 2 * block_rows, 1)
    block_basis = tables(2 * block_count, block_count, 2 * block_count)
    return_basis = tables(block_count, 2 * block_count, 2 * block_count)
    input_pair = rows_spectrum(product, forward_basis)
    filter_pair = rows_spectrum(long_filter, forward_basis)
    lanes = product.shape[1]
    moved_data = split_lanes(
        lax.all_to_all(
            jnp.concatenate([input_pair[0], input_pair[1], filter_pair[0], filter_pair[1]], axis=1)[
                None
            ].astype(jnp.bfloat16),
            SEQ,
            split_axis=1,
            concat_axis=0,
            tiled=True,
        ).astype(jnp.float32),
        lanes,
    )
    input_spectrum = block_forward((moved_data[0], moved_data[1]), block_basis)
    filter_spectrum = block_forward((moved_data[2], moved_data[3]), block_basis)
    inverse_pair = block_inverse(complex_product(filter_spectrum, input_spectrum), return_basis)
    returned = split_lanes(
        lax.all_to_all(
            as_sent(jnp.concatenate(inverse_pair, axis=-1)),
            SEQ,
            split_axis=0,
            concat_axis=1,
            tiled=True,
        ).astype(jnp.float32),
        lanes,
    )
    folded = rows_inverse((returned[0][0], returned[1][0]), fold_basis)
    carried = from_behind(folded[block_rows:], SEQ, 1)
    convolved = folded[:block_rows] + carried
    mixed_seq = convolved + skip_gain * product
    gated_values = (query_short * mixed_seq).astype(jnp.bfloat16)
    full_cotangent = lax.all_gather(cotangent, "ch", axis=1, tiled=True)
    full_cotangent, gated_values = lax.optimization_barrier((full_cotangent, gated_values))
    partial_value = jnp.dot(gated_values, out_weight, preferred_element_type=jnp.float32)
    layer_out = lax.psum_scatter(partial_value, "ch", scatter_dimension=1, tiled=True).astype(
        jnp.bfloat16
    )
    grad_gated = lax.dot_general(
        full_cotangent, out_weight, (((1,), (1,)), ((), ())), preferred_element_type=jnp.float32
    )
    outer = lax.axis_size("seq_hi")
    inner = lax.axis_size("seq_lo")
    feature_rows = full_cotangent.shape[1] // outer // inner
    local_rows = lax.all_gather(gated_values, "seq_lo", axis=0, tiled=True)
    local_features = lax.all_to_all(
        full_cotangent.reshape(block_rows, outer, inner, feature_rows),
        "seq_lo",
        split_axis=2,
        concat_axis=0,
        tiled=True,
    ).reshape(block_rows * inner, -1)
    weight_terms = lax.dot_general(
        local_features,
        local_rows,
        (((0,), (0,)), ((), ())),
        preferred_element_type=jnp.float32,
    )
    grad_mixed = grad_gated * query_short
    grad_query_short = grad_gated * mixed_seq
    following = from_behind(grad_mixed.astype(jnp.bfloat16), SEQ, -1).astype(grad_mixed.dtype)
    spread = jnp.concatenate([grad_mixed, following], axis=0)
    grad_pair = rows_spectrum(spread, spread_basis)
    moved_grad = split_lanes(
        lax.all_to_all(
            jnp.concatenate(grad_pair, axis=1)[None].astype(jnp.bfloat16),
            SEQ,
            split_axis=1,
            concat_axis=0,
            tiled=True,
        ).astype(jnp.float32),
        lanes,
    )
    grad_spectrum = block_forward(moved_grad, block_basis)
    input_back = block_inverse(conj_product(filter_spectrum, grad_spectrum), return_basis)
    filter_back = block_inverse(conj_product(input_spectrum, grad_spectrum), return_basis)
    returned_grad = split_lanes(
        lax.all_to_all(
            as_sent(jnp.concatenate(input_back + filter_back, axis=-1)),
            SEQ,
            split_axis=0,
            concat_axis=1,
            tiled=True,
        ),
        lanes,
    )
    grad_w_out_t = lax.psum_scatter(weight_terms, "seq_hi", scatter_dimension=0, tiled=True)
    grad_w_out_t, layer_out, returned_grad = lax.optimization_barrier(
        (grad_w_out_t, layer_out, returned_grad)
    )
    conv_grad = rows_inverse((returned_grad[0][0], returned_grad[1][0]), half_basis)
    grad_filter = rows_inverse((returned_grad[2][0], returned_grad[3][0]), half_basis)
    grad_product = conv_grad + skip_gain * grad_mixed
    grad_streams = jnp.stack(
        [grad_query_short, grad_product * value_short, grad_product * key_short]
    )
    later_rows = from_behind(grad_streams[:, : tap_count - 1], SEQ, -1)
    padded_grad = jnp.concatenate([grad_streams, later_rows], axis=1)
    grad_inputs = sum(
        (
            short_filter[:, offset][:, None, :] * padded_grad[:, offset : offset + block_rows]
            for offset in range(tap_count)
        )
    )
    short_terms = jnp.stack(
        [jnp.sum(grad_streams * shifted[offset], axis=1) for offset in range(tap_count)], axis=1
    )
    skip_terms = jnp.sum(grad_mixed * product, axis=0)
    channel_count = skip_terms.shape[0]
    sum_rows = short_terms.shape[0] * short_terms.shape[1] + 1
    padded_rows = -(-sum_rows // 8) * 8
    small_terms = jnp.concatenate(
        [
            short_terms.reshape(sum_rows - 1, channel_count),
            skip_terms[None],
            jnp.zeros((padded_rows - sum_rows, channel_count), jnp.float32),
        ]
    )
    (outer_sum,) = sum_over_group(small_terms, "seq_hi", 0)
    grad_short, skip_row = sum_over_group(
        outer_sum, "seq_lo", 1, (short_terms.shape, (1, channel_count))
    )
    grad_skip = skip_row[0]
    return (
        layer_out,
        grad_inputs[0],
        grad_inputs[1],
        grad_inputs[2],
        grad_short,
        grad_filter,
        grad_skip,
        grad_w_out_t,
    )


def solution(mesh):
    in_specs = (
        P(SEQ, "ch"),
        P(SEQ, "ch"),
        P(SEQ, "ch"),
        P(None, None, "ch"),
        P(SEQ, "ch"),
        P("ch"),
        P("ch", None),
        P(SEQ, "ch"),
    )
    out_specs = (
        P(SEQ, "ch"),
        P(SEQ, "ch"),
        P(SEQ, "ch"),
        P(SEQ, "ch"),
        P(None, None, "ch"),
        P(SEQ, "ch"),
        P("ch"),
        P(SEQ, "ch"),
    )
    inner = 8
    seq_mesh = jax.sharding.Mesh(
        mesh.devices.reshape(mesh.shape["seq"] // inner, inner, mesh.shape["ch"]),
        ("seq_hi", "seq_lo", "ch"),
    )
    return jax.shard_map(
        on_device, mesh=seq_mesh, in_specs=in_specs, out_specs=out_specs, check_vma=False
    )
```

```python
import functools
import math

import jax
import jax.numpy as jnp
from jax import lax
from jax.experimental import pallas as pl
from jax.experimental.pallas import tpu as pltpu
from jax.sharding import PartitionSpec as P

exact_mode = lax.Precision.HIGH
SEQ = ("seq_hi", "seq_lo")


def from_behind(shard, axis, by):
    size = lax.axis_size(axis)
    pairs = [(i, i + by) for i in range(size) if 0 <= i + by < size]
    return lax.ppermute(shard, axis, pairs)


def as_sent(shard):

    def short(part):
        return part.astype(jnp.bfloat16) if part.dtype == jnp.float32 else part

    return jax.tree.map(short, shard)


def group_sum_kernel(axis, shape_out, part_ref, *refs):
    outs = refs[: len(shape_out)]
    slots, local_sem, send_sems, recv_sems = refs[len(shape_out) :]
    count = lax.axis_size(axis)
    me = lax.axis_index(axis)
    place = {"seq_hi": lax.axis_index("seq_hi"), "seq_lo": lax.axis_index("seq_lo")}

    def member(index):
        where = dict(place, **{axis: index})
        return (where["seq_hi"], where["seq_lo"], lax.axis_index("ch"))

    barrier = pltpu.get_barrier_semaphore()
    for step in range(1, count):
        pl.semaphore_signal(
            barrier,
            1,
            device_id=member(lax.rem(me + step, count)),
            device_id_type=pl.DeviceIdType.MESH,
        )
    pl.semaphore_wait(barrier, count - 1)
    own = pltpu.make_async_copy(part_ref, slots.at[me], local_sem)
    own.start()
    outgoing = []
    for step in range(1, count):
        peer = lax.rem(me + step, count)
        copy = pltpu.make_async_remote_copy(
            src_ref=part_ref,
            dst_ref=slots.at[me],
            send_sem=send_sems.at[step],
            recv_sem=recv_sems.at[me],
            device_id=member(peer),
            device_id_type=pl.DeviceIdType.MESH,
        )
        copy.start()
        outgoing.append(copy)
    own.wait()
    for step in range(1, count):
        source = lax.rem(me + count - step, count)
        outgoing[step - 1].wait_send()
        pltpu.make_async_remote_copy(
            src_ref=part_ref,
            dst_ref=slots.at[source],
            send_sem=send_sems.at[step],
            recv_sem=recv_sems.at[source],
            device_id=member(source),
            device_id_type=pl.DeviceIdType.MESH,
        ).wait_recv()
    total = slots[0]
    for slot in range(1, count):
        total = total + slots[slot]
    if len(outs) == 1:
        outs[0][...] = total
        return
    short_ref, skip_ref = outs
    streams, taps = short_ref.shape[0], short_ref.shape[1]
    for stream in range(streams):
        short_ref[stream] = total[stream * taps : (stream + 1) * taps]
    skip_ref[...] = total[streams * taps : streams * taps + 1]


def sum_over_group(part, axis, kernel_id, shape_out=None):
    count = lax.axis_size(axis)
    shape_out = shape_out or (part.shape,)
    return pl.pallas_call(
        functools.partial(group_sum_kernel, axis, shape_out),
        out_shape=[jax.ShapeDtypeStruct(shape, part.dtype) for shape in shape_out],
        in_specs=[pl.BlockSpec(memory_space=pltpu.VMEM)],
        out_specs=[pl.BlockSpec(memory_space=pltpu.VMEM) for _ in shape_out],
        scratch_shapes=[
            pltpu.VMEM((count,) + part.shape, part.dtype),
            pltpu.SemaphoreType.DMA(()),
            pltpu.SemaphoreType.DMA((count,)),
            pltpu.SemaphoreType.DMA((count,)),
        ],
        compiler_params=pltpu.CompilerParams(collective_id=kernel_id, has_side_effects=True),
    )(part)


def split_lanes(merged, lanes):
    return tuple(
        merged[..., start : start + lanes] for start in range(0, merged.shape[-1], lanes)
    )


def tables(rows_out, cols_in, period):
    row_index = lax.broadcasted_iota(jnp.int32, (rows_out, cols_in), 0)
    col_index = lax.broadcasted_iota(jnp.int32, (rows_out, cols_in), 1)
    phase_angle = (row_index * col_index % period).astype(jnp.float32) * (2.0 * math.pi / period)
    return (jnp.cos(phase_angle), jnp.sin(phase_angle))


def odd_tables(rows_out, cols_in, period, odd_axis):
    row_index = lax.broadcasted_iota(jnp.int32, (rows_out, cols_in), 0)
    col_index = lax.broadcasted_iota(jnp.int32, (rows_out, cols_in), 1)
    if odd_axis == 0:
        row_index = 2 * row_index + 1
    else:
        col_index = 2 * col_index + 1
    phase_angle = (row_index * col_index % (2 * period)).astype(jnp.float32) * (math.pi / period)
    return (jnp.cos(phase_angle), jnp.sin(phase_angle))


def along_rows(factor, values):
    return jnp.tensordot(factor, values, axes=1, precision=exact_mode)


def rows_spectrum(signal, basis_pair):
    return (along_rows(basis_pair[0], signal), -along_rows(basis_pair[1], signal))


def rows_inverse(complex_pair, basis_pair):
    total = along_rows(basis_pair[0], complex_pair[0]) - along_rows(basis_pair[1], complex_pair[1])
    return total / basis_pair[0].shape[1]


def block_forward(complex_pair, basis_pair):
    cosine_part, sine_part = basis_pair
    real_part = along_rows(cosine_part, complex_pair[0]) + along_rows(sine_part, complex_pair[1])
    imag_part = along_rows(cosine_part, complex_pair[1]) - along_rows(sine_part, complex_pair[0])
    return (real_part, imag_part)


def block_inverse(complex_pair, basis_pair):
    cosine_part, sine_part = basis_pair
    norming = 1.0 / cosine_part.shape[1]
    real_part = along_rows(cosine_part, complex_pair[0]) - along_rows(sine_part, complex_pair[1])
    imag_part = along_rows(cosine_part, complex_pair[1]) + along_rows(sine_part, complex_pair[0])
    return (real_part * norming, imag_part * norming)


def complex_product(first_pair, second_pair):
    return (
        first_pair[0] * second_pair[0] - first_pair[1] * second_pair[1],
        first_pair[0] * second_pair[1] + first_pair[1] * second_pair[0],
    )


def conj_product(first_pair, second_pair):
    return (
        first_pair[0] * second_pair[0] + first_pair[1] * second_pair[1],
        first_pair[0] * second_pair[1] - first_pair[1] * second_pair[0],
    )


def on_device(
    query_proj, key_proj, value_proj, short_filter, long_filter, skip_gain, out_weight, cotangent
):
    block_rows = query_proj.shape[0]
    tap_count = short_filter.shape[1]
    block_count = lax.axis_size(SEQ)
    streams = jnp.stack([query_proj, key_proj, value_proj])
    earlier = from_behind(streams[:, block_rows - (tap_count - 1) :], SEQ, 1)
    extended = jnp.concatenate([earlier, streams], axis=1).astype(jnp.float32)
    shifted = [
        extended[:, tap_count - 1 - offset : tap_count - 1 - offset + block_rows]
        for offset in range(tap_count)
    ]
    filtered = sum(
        (short_filter[:, offset][:, None, :] * shifted[offset] for offset in range(tap_count))
    )
    query_short, key_short, value_short = (filtered[0], filtered[1], filtered[2])
    product = key_short * value_short
    forward_basis = odd_tables(block_rows, block_rows, 2 * block_rows, 0)
    spread_basis = odd_tables(block_rows, 2 * block_rows, 2 * block_rows, 0)
    fold_basis = odd_tables(2 * block_rows, block_rows, 2 * block_rows, 1)
    half_basis = odd_tables(block_rows, block_rows, 2 * block_rows, 1)
    block_basis = tables(2 * block_count, block_count, 2 * block_count)
    return_basis = tables(block_count, 2 * block_count, 2 * block_count)
    input_pair = rows_spectrum(product, forward_basis)
    filter_pair = rows_spectrum(long_filter, forward_basis)
    lanes = product.shape[1]
    moved_data = split_lanes(
        lax.all_to_all(
            jnp.concatenate([input_pair[0], input_pair[1], filter_pair[0], filter_pair[1]], axis=1)[
                None
            ].astype(jnp.bfloat16),
            SEQ,
            split_axis=1,
            concat_axis=0,
            tiled=True,
        ).astype(jnp.float32),
        lanes,
    )
    input_spectrum = block_forward((moved_data[0], moved_data[1]), block_basis)
    filter_spectrum = block_forward((moved_data[2], moved_data[3]), block_basis)
    inverse_pair = block_inverse(complex_product(filter_spectrum, input_spectrum), return_basis)
    returned = split_lanes(
        lax.all_to_all(
            as_sent(jnp.concatenate(inverse_pair, axis=-1)),
            SEQ,
            split_axis=0,
            concat_axis=1,
            tiled=True,
        ).astype(jnp.float32),
        lanes,
    )
    folded = rows_inverse((returned[0][0], returned[1][0]), fold_basis)
    carried = from_behind(folded[block_rows:], SEQ, 1)
    convolved = folded[:block_rows] + carried
    mixed_seq = convolved + skip_gain * product
    gated_values = (query_short * mixed_seq).astype(jnp.bfloat16)
    full_cotangent = lax.all_gather(cotangent, "ch", axis=1, tiled=True)
    full_cotangent, gated_values = lax.optimization_barrier((full_cotangent, gated_values))
    partial_value = jnp.dot(gated_values, out_weight, preferred_element_type=jnp.float32)
    layer_out = lax.psum_scatter(partial_value, "ch", scatter_dimension=1, tiled=True).astype(
        jnp.bfloat16
    )
    grad_gated = lax.dot_general(
        full_cotangent, out_weight, (((1,), (1,)), ((), ())), preferred_element_type=jnp.float32
    )
    outer = lax.axis_size("seq_hi")
    inner = lax.axis_size("seq_lo")
    feature_rows = full_cotangent.shape[1] // outer // inner
    local_rows = lax.all_gather(gated_values, "seq_lo", axis=0, tiled=True)
    local_features = lax.all_to_all(
        full_cotangent.reshape(block_rows, outer, inner, feature_rows),
        "seq_lo",
        split_axis=2,
        concat_axis=0,
        tiled=True,
    ).reshape(block_rows * inner, -1)
    weight_terms = lax.dot_general(
        local_features,
        local_rows,
        (((0,), (0,)), ((), ())),
        preferred_element_type=jnp.float32,
    )
    grad_mixed = grad_gated * query_short
    grad_query_short = grad_gated * mixed_seq
    following = from_behind(grad_mixed.astype(jnp.bfloat16), SEQ, -1).astype(grad_mixed.dtype)
    spread = jnp.concatenate([grad_mixed, following], axis=0)
    grad_pair = rows_spectrum(spread, spread_basis)
    moved_grad = split_lanes(
        lax.all_to_all(
            jnp.concatenate(grad_pair, axis=1)[None].astype(jnp.bfloat16),
            SEQ,
            split_axis=1,
            concat_axis=0,
            tiled=True,
        ).astype(jnp.float32),
        lanes,
    )
    grad_spectrum = block_forward(moved_grad, block_basis)
    input_back = block_inverse(conj_product(filter_spectrum, grad_spectrum), return_basis)
    filter_back = block_inverse(conj_product(input_spectrum, grad_spectrum), return_basis)
    returned_grad = split_lanes(
        lax.all_to_all(
            as_sent(jnp.concatenate(input_back + filter_back, axis=-1)),
            SEQ,
            split_axis=0,
            concat_axis=1,
            tiled=True,
        ),
        lanes,
    )
    grad_w_out_t = lax.psum_scatter(weight_terms, "seq_hi", scatter_dimension=0, tiled=True)
    grad_w_out_t, returned_grad = lax.optimization_barrier((grad_w_out_t, returned_grad))
    conv_grad = rows_inverse((returned_grad[0][0], returned_grad[1][0]), half_basis)
    grad_filter = rows_inverse((returned_grad[2][0], returned_grad[3][0]), half_basis)
    grad_product = conv_grad + skip_gain * grad_mixed
    grad_streams = jnp.stack(
        [grad_query_short, grad_product * value_short, grad_product * key_short]
    )
    later_rows = from_behind(grad_streams[:, : tap_count - 1], SEQ, -1)
    padded_grad = jnp.concatenate([grad_streams, later_rows], axis=1)
    grad_inputs = sum(
        (
            short_filter[:, offset][:, None, :] * padded_grad[:, offset : offset + block_rows]
            for offset in range(tap_count)
        )
    )
    short_terms = jnp.stack(
        [jnp.sum(grad_streams * shifted[offset], axis=1) for offset in range(tap_count)], axis=1
    )
    skip_terms = jnp.sum(grad_mixed * product, axis=0)
    channel_count = skip_terms.shape[0]
    sum_rows = short_terms.shape[0] * short_terms.shape[1] + 1
    padded_rows = -(-sum_rows // 8) * 8
    small_terms = jnp.concatenate(
        [
            short_terms.reshape(sum_rows - 1, channel_count),
            skip_terms[None],
            jnp.zeros((padded_rows - sum_rows, channel_count), jnp.float32),
        ]
    )
    (outer_sum,) = sum_over_group(small_terms, "seq_hi", 0)
    grad_short, skip_row = sum_over_group(
        outer_sum, "seq_lo", 1, (short_terms.shape, (1, channel_count))
    )
    grad_skip = skip_row[0]
    return (
        layer_out,
        grad_inputs[0],
        grad_inputs[1],
        grad_inputs[2],
        grad_short,
        grad_filter,
        grad_skip,
        grad_w_out_t,
    )


def solution(mesh):
    in_specs = (
        P(SEQ, "ch"),
        P(SEQ, "ch"),
        P(SEQ, "ch"),
        P(None, None, "ch"),
        P(SEQ, "ch"),
        P("ch"),
        P("ch", None),
        P(SEQ, "ch"),
    )
    out_specs = (
        P(SEQ, "ch"),
        P(SEQ, "ch"),
        P(SEQ, "ch"),
        P(SEQ, "ch"),
        P(None, None, "ch"),
        P(SEQ, "ch"),
        P("ch"),
        P(SEQ, "ch"),
    )
    inner = 8
    seq_mesh = jax.sharding.Mesh(
        mesh.devices.reshape(mesh.shape["seq"] // inner, inner, mesh.shape["ch"]),
        ("seq_hi", "seq_lo", "ch"),
    )
    return jax.shard_map(
        on_device, mesh=seq_mesh, in_specs=in_specs, out_specs=out_specs, check_vma=False
    )
```

```python
import functools
import math

import jax
import jax.numpy as jnp
from jax import lax
from jax.experimental import pallas as pl
from jax.experimental.pallas import tpu as pltpu
from jax.sharding import PartitionSpec as P

exact_mode = lax.Precision.HIGH
SEQ = ("seq_hi", "seq_lo")


def from_behind(shard, axis, by):
    size = lax.axis_size(axis)
    pairs = [(i, i + by) for i in range(size) if 0 <= i + by < size]
    return lax.ppermute(shard, axis, pairs)


def as_sent(shard):

    def short(part):
        return part.astype(jnp.bfloat16) if part.dtype == jnp.float32 else part

    return jax.tree.map(short, shard)


def group_sum_kernel(axis, shape_out, part_ref, *refs):
    outs = refs[: len(shape_out)]
    slots, local_sem, send_sems, recv_sems = refs[len(shape_out) :]
    count = lax.axis_size(axis)
    me = lax.axis_index(axis)
    place = {"seq_hi": lax.axis_index("seq_hi"), "seq_lo": lax.axis_index("seq_lo")}

    def member(index):
        where = dict(place, **{axis: index})
        return (where["seq_hi"], where["seq_lo"], lax.axis_index("ch"))

    barrier = pltpu.get_barrier_semaphore()
    for step in range(1, count):
        pl.semaphore_signal(
            barrier,
            1,
            device_id=member(lax.rem(me + step, count)),
            device_id_type=pl.DeviceIdType.MESH,
        )
    pl.semaphore_wait(barrier, count - 1)
    own = pltpu.make_async_copy(part_ref, slots.at[me], local_sem)
    own.start()
    outgoing = []
    for step in range(1, count):
        peer = lax.rem(me + step, count)
        copy = pltpu.make_async_remote_copy(
            src_ref=part_ref,
            dst_ref=slots.at[me],
            send_sem=send_sems.at[step],
            recv_sem=recv_sems.at[me],
            device_id=member(peer),
            device_id_type=pl.DeviceIdType.MESH,
        )
        copy.start()
        outgoing.append(copy)
    own.wait()
    for step in range(1, count):
        source = lax.rem(me + count - step, count)
        outgoing[step - 1].wait_send()
        pltpu.make_async_remote_copy(
            src_ref=part_ref,
            dst_ref=slots.at[source],
            send_sem=send_sems.at[step],
            recv_sem=recv_sems.at[source],
            device_id=member(source),
            device_id_type=pl.DeviceIdType.MESH,
        ).wait_recv()
    total = slots[0]
    for slot in range(1, count):
        total = total + slots[slot]
    if len(outs) == 1:
        outs[0][...] = total
        return
    short_ref, skip_ref = outs
    streams, taps = short_ref.shape[0], short_ref.shape[1]
    for stream in range(streams):
        short_ref[stream] = total[stream * taps : (stream + 1) * taps]
    skip_ref[...] = total[streams * taps : streams * taps + 1]


def sum_over_group(part, axis, kernel_id, shape_out=None):
    count = lax.axis_size(axis)
    shape_out = shape_out or (part.shape,)
    return pl.pallas_call(
        functools.partial(group_sum_kernel, axis, shape_out),
        out_shape=[jax.ShapeDtypeStruct(shape, part.dtype) for shape in shape_out],
        in_specs=[pl.BlockSpec(memory_space=pltpu.VMEM)],
        out_specs=[pl.BlockSpec(memory_space=pltpu.VMEM) for _ in shape_out],
        scratch_shapes=[
            pltpu.VMEM((count,) + part.shape, part.dtype),
            pltpu.SemaphoreType.DMA(()),
            pltpu.SemaphoreType.DMA((count,)),
            pltpu.SemaphoreType.DMA((count,)),
        ],
        compiler_params=pltpu.CompilerParams(collective_id=kernel_id, has_side_effects=True),
    )(part)


def split_lanes(merged, lanes):
    return tuple(
        merged[..., start : start + lanes] for start in range(0, merged.shape[-1], lanes)
    )


def tables(rows_out, cols_in, period):
    row_index = lax.broadcasted_iota(jnp.int32, (rows_out, cols_in), 0)
    col_index = lax.broadcasted_iota(jnp.int32, (rows_out, cols_in), 1)
    phase_angle = (row_index * col_index % period).astype(jnp.float32) * (2.0 * math.pi / period)
    return (jnp.cos(phase_angle), jnp.sin(phase_angle))


def odd_tables(rows_out, cols_in, period, odd_axis):
    row_index = lax.broadcasted_iota(jnp.int32, (rows_out, cols_in), 0)
    col_index = lax.broadcasted_iota(jnp.int32, (rows_out, cols_in), 1)
    if odd_axis == 0:
        row_index = 2 * row_index + 1
    else:
        col_index = 2 * col_index + 1
    phase_angle = (row_index * col_index % (2 * period)).astype(jnp.float32) * (math.pi / period)
    return (jnp.cos(phase_angle), jnp.sin(phase_angle))


def along_rows(factor, values):
    return jnp.tensordot(factor, values, axes=1, precision=exact_mode)


def rows_spectrum(signal, basis_pair):
    return (along_rows(basis_pair[0], signal), -along_rows(basis_pair[1], signal))


def rows_inverse(complex_pair, basis_pair):
    total = along_rows(basis_pair[0], complex_pair[0]) - along_rows(basis_pair[1], complex_pair[1])
    return total / basis_pair[0].shape[1]


def block_forward(complex_pair, basis_pair):
    cosine_part, sine_part = basis_pair
    real_part = along_rows(cosine_part, complex_pair[0]) + along_rows(sine_part, complex_pair[1])
    imag_part = along_rows(cosine_part, complex_pair[1]) - along_rows(sine_part, complex_pair[0])
    return (real_part, imag_part)


def block_inverse(complex_pair, basis_pair):
    cosine_part, sine_part = basis_pair
    norming = 1.0 / cosine_part.shape[1]
    real_part = along_rows(cosine_part, complex_pair[0]) - along_rows(sine_part, complex_pair[1])
    imag_part = along_rows(cosine_part, complex_pair[1]) + along_rows(sine_part, complex_pair[0])
    return (real_part * norming, imag_part * norming)


def complex_product(first_pair, second_pair):
    return (
        first_pair[0] * second_pair[0] - first_pair[1] * second_pair[1],
        first_pair[0] * second_pair[1] + first_pair[1] * second_pair[0],
    )


def conj_product(first_pair, second_pair):
    return (
        first_pair[0] * second_pair[0] + first_pair[1] * second_pair[1],
        first_pair[0] * second_pair[1] - first_pair[1] * second_pair[0],
    )


def on_device(
    query_proj, key_proj, value_proj, short_filter, long_filter, skip_gain, out_weight, cotangent
):
    block_rows = query_proj.shape[0]
    tap_count = short_filter.shape[1]
    block_count = lax.axis_size(SEQ)
    streams = jnp.stack([query_proj, key_proj, value_proj])
    earlier = from_behind(streams[:, block_rows - (tap_count - 1) :], SEQ, 1)
    extended = jnp.concatenate([earlier, streams], axis=1).astype(jnp.float32)
    shifted = [
        extended[:, tap_count - 1 - offset : tap_count - 1 - offset + block_rows]
        for offset in range(tap_count)
    ]
    filtered = sum(
        (short_filter[:, offset][:, None, :] * shifted[offset] for offset in range(tap_count))
    )
    query_short, key_short, value_short = (filtered[0], filtered[1], filtered[2])
    product = key_short * value_short
    forward_basis = odd_tables(block_rows, block_rows, 2 * block_rows, 0)
    spread_basis = odd_tables(block_rows, 2 * block_rows, 2 * block_rows, 0)
    fold_basis = odd_tables(2 * block_rows, block_rows, 2 * block_rows, 1)
    half_basis = odd_tables(block_rows, block_rows, 2 * block_rows, 1)
    block_basis = tables(2 * block_count, block_count, 2 * block_count)
    return_basis = tables(block_count, 2 * block_count, 2 * block_count)
    input_pair = rows_spectrum(product, forward_basis)
    filter_pair = rows_spectrum(long_filter, forward_basis)
    lanes = product.shape[1]
    moved_data = split_lanes(
        lax.all_to_all(
            jnp.concatenate([input_pair[0], input_pair[1], filter_pair[0], filter_pair[1]], axis=1)[
                None
            ].astype(jnp.bfloat16),
            SEQ,
            split_axis=1,
            concat_axis=0,
            tiled=True,
        ).astype(jnp.float32),
        lanes,
    )
    input_spectrum = block_forward((moved_data[0], moved_data[1]), block_basis)
    filter_spectrum = block_forward((moved_data[2], moved_data[3]), block_basis)
    inverse_pair = block_inverse(complex_product(filter_spectrum, input_spectrum), return_basis)
    returned = split_lanes(
        lax.all_to_all(
            as_sent(jnp.concatenate(inverse_pair, axis=-1)),
            SEQ,
            split_axis=0,
            concat_axis=1,
            tiled=True,
        ).astype(jnp.float32),
        lanes,
    )
    folded = rows_inverse((returned[0][0], returned[1][0]), fold_basis)
    carried = from_behind(folded[block_rows:], SEQ, 1)
    convolved = folded[:block_rows] + carried
    mixed_seq = convolved + skip_gain * product
    gated_values = (query_short * mixed_seq).astype(jnp.bfloat16)
    full_cotangent = lax.all_gather(cotangent, "ch", axis=1, tiled=True)
    full_cotangent, gated_values = lax.optimization_barrier((full_cotangent, gated_values))
    partial_value = jnp.dot(gated_values, out_weight, preferred_element_type=jnp.float32)
    layer_out = lax.psum_scatter(partial_value, "ch", scatter_dimension=1, tiled=True).astype(
        jnp.bfloat16
    )
    grad_gated = lax.dot_general(
        full_cotangent, out_weight, (((1,), (1,)), ((), ())), preferred_element_type=jnp.float32
    )
    outer = lax.axis_size("seq_hi")
    inner = lax.axis_size("seq_lo")
    feature_rows = full_cotangent.shape[1] // outer // inner
    local_rows = lax.all_gather(gated_values, "seq_lo", axis=0, tiled=True)
    local_features = lax.all_to_all(
        full_cotangent.reshape(block_rows, outer, inner, feature_rows),
        "seq_lo",
        split_axis=2,
        concat_axis=0,
        tiled=True,
    ).reshape(block_rows * inner, -1)
    weight_terms = lax.dot_general(
        local_features,
        local_rows,
        (((0,), (0,)), ((), ())),
        preferred_element_type=jnp.float32,
    )
    grad_mixed = grad_gated * query_short
    grad_query_short = grad_gated * mixed_seq
    following = from_behind(grad_mixed.astype(jnp.bfloat16), SEQ, -1).astype(grad_mixed.dtype)
    spread = jnp.concatenate([grad_mixed, following], axis=0)
    grad_pair = rows_spectrum(spread, spread_basis)
    moved_grad = split_lanes(
        lax.all_to_all(
            jnp.concatenate(grad_pair, axis=1)[None].astype(jnp.bfloat16),
            SEQ,
            split_axis=1,
            concat_axis=0,
            tiled=True,
        ).astype(jnp.float32),
        lanes,
    )
    grad_spectrum = block_forward(moved_grad, block_basis)
    input_back = block_inverse(conj_product(filter_spectrum, grad_spectrum), return_basis)
    filter_back = block_inverse(conj_product(input_spectrum, grad_spectrum), return_basis)
    returned_grad = split_lanes(
        lax.all_to_all(
            as_sent(jnp.concatenate(input_back + filter_back, axis=-1)),
            SEQ,
            split_axis=0,
            concat_axis=1,
            tiled=True,
        ),
        lanes,
    )
    grad_w_out_t = lax.psum_scatter(weight_terms, "seq_hi", scatter_dimension=0, tiled=True)
    grad_w_out_t, layer_out, returned_grad = lax.optimization_barrier(
        (grad_w_out_t, layer_out, returned_grad)
    )
    conv_grad = rows_inverse((returned_grad[0][0], returned_grad[1][0]), half_basis)
    grad_filter = rows_inverse((returned_grad[2][0], returned_grad[3][0]), half_basis)
    grad_product = conv_grad + skip_gain * grad_mixed
    grad_streams = jnp.stack(
        [grad_query_short, grad_product * value_short, grad_product * key_short]
    )
    later_rows = from_behind(grad_streams[:, : tap_count - 1], SEQ, -1)
    padded_grad = jnp.concatenate([grad_streams, later_rows], axis=1)
    grad_inputs = sum(
        (
            short_filter[:, offset][:, None, :] * padded_grad[:, offset : offset + block_rows]
            for offset in range(tap_count)
        )
    )
    short_terms = jnp.stack(
        [jnp.sum(grad_streams * shifted[offset], axis=1) for offset in range(tap_count)], axis=1
    )
    skip_terms = jnp.sum(grad_mixed * product, axis=0)
    channel_count = skip_terms.shape[0]
    sum_rows = short_terms.shape[0] * short_terms.shape[1] + 1
    padded_rows = -(-sum_rows // 8) * 8
    small_terms = jnp.concatenate(
        [
            short_terms.reshape(sum_rows - 1, channel_count),
            skip_terms[None],
            jnp.zeros((padded_rows - sum_rows, channel_count), jnp.float32),
        ]
    )
    (inner_sum,) = sum_over_group(small_terms, "seq_lo", 0)
    grad_short, skip_row = sum_over_group(
        inner_sum, "seq_hi", 1, (short_terms.shape, (1, channel_count))
    )
    grad_skip = skip_row[0]
    return (
        layer_out,
        grad_inputs[0],
        grad_inputs[1],
        grad_inputs[2],
        grad_short,
        grad_filter,
        grad_skip,
        grad_w_out_t,
    )


def solution(mesh):
    in_specs = (
        P(SEQ, "ch"),
        P(SEQ, "ch"),
        P(SEQ, "ch"),
        P(None, None, "ch"),
        P(SEQ, "ch"),
        P("ch"),
        P("ch", None),
        P(SEQ, "ch"),
    )
    out_specs = (
        P(SEQ, "ch"),
        P(SEQ, "ch"),
        P(SEQ, "ch"),
        P(SEQ, "ch"),
        P(None, None, "ch"),
        P(SEQ, "ch"),
        P("ch"),
        P(SEQ, "ch"),
    )
    inner = 8
    seq_mesh = jax.sharding.Mesh(
        mesh.devices.reshape(mesh.shape["seq"] // inner, inner, mesh.shape["ch"]),
        ("seq_hi", "seq_lo", "ch"),
    )
    return jax.shard_map(
        on_device, mesh=seq_mesh, in_specs=in_specs, out_specs=out_specs, check_vma=False
    )
```

```python
import functools
import math

import jax
import jax.numpy as jnp
from jax import lax
from jax.experimental import pallas as pl
from jax.experimental.pallas import tpu as pltpu
from jax.sharding import PartitionSpec as P

exact_mode = lax.Precision.HIGH
SEQ = ("seq_hi", "seq_lo")


def from_behind(shard, axis, by):
    size = lax.axis_size(axis)
    pairs = [(i, i + by) for i in range(size) if 0 <= i + by < size]
    return lax.ppermute(shard, axis, pairs)


def as_sent(shard):

    def short(part):
        return part.astype(jnp.bfloat16) if part.dtype == jnp.float32 else part

    return jax.tree.map(short, shard)


def group_sum_kernel(axis, shape_out, part_ref, *refs):
    outs = refs[: len(shape_out)]
    slots, local_sem, send_sems, recv_sems = refs[len(shape_out) :]
    count = lax.axis_size(axis)
    me = lax.axis_index(axis)
    place = {"seq_hi": lax.axis_index("seq_hi"), "seq_lo": lax.axis_index("seq_lo")}

    def member(index):
        where = dict(place, **{axis: index})
        return (where["seq_hi"], where["seq_lo"], lax.axis_index("ch"))

    barrier = pltpu.get_barrier_semaphore()
    for step in range(1, count):
        pl.semaphore_signal(
            barrier,
            1,
            device_id=member(lax.rem(me + step, count)),
            device_id_type=pl.DeviceIdType.MESH,
        )
    pl.semaphore_wait(barrier, count - 1)
    own = pltpu.make_async_copy(part_ref, slots.at[me], local_sem)
    own.start()
    outgoing = []
    for step in range(1, count):
        peer = lax.rem(me + step, count)
        copy = pltpu.make_async_remote_copy(
            src_ref=part_ref,
            dst_ref=slots.at[me],
            send_sem=send_sems.at[step],
            recv_sem=recv_sems.at[me],
            device_id=member(peer),
            device_id_type=pl.DeviceIdType.MESH,
        )
        copy.start()
        outgoing.append(copy)
    own.wait()
    for step in range(1, count):
        source = lax.rem(me + count - step, count)
        outgoing[step - 1].wait_send()
        pltpu.make_async_remote_copy(
            src_ref=part_ref,
            dst_ref=slots.at[source],
            send_sem=send_sems.at[step],
            recv_sem=recv_sems.at[source],
            device_id=member(source),
            device_id_type=pl.DeviceIdType.MESH,
        ).wait_recv()
    total = slots[0]
    for slot in range(1, count):
        total = total + slots[slot]
    if len(outs) == 1:
        outs[0][...] = total
        return
    short_ref, skip_ref = outs
    streams, taps = short_ref.shape[0], short_ref.shape[1]
    for stream in range(streams):
        short_ref[stream] = total[stream * taps : (stream + 1) * taps]
    skip_ref[...] = total[streams * taps : streams * taps + 1]


def sum_over_group(part, axis, kernel_id, shape_out=None):
    count = lax.axis_size(axis)
    shape_out = shape_out or (part.shape,)
    return pl.pallas_call(
        functools.partial(group_sum_kernel, axis, shape_out),
        out_shape=[jax.ShapeDtypeStruct(shape, part.dtype) for shape in shape_out],
        in_specs=[pl.BlockSpec(memory_space=pltpu.VMEM)],
        out_specs=[pl.BlockSpec(memory_space=pltpu.VMEM) for _ in shape_out],
        scratch_shapes=[
            pltpu.VMEM((count,) + part.shape, part.dtype),
            pltpu.SemaphoreType.DMA(()),
            pltpu.SemaphoreType.DMA((count,)),
            pltpu.SemaphoreType.DMA((count,)),
        ],
        compiler_params=pltpu.CompilerParams(collective_id=kernel_id, has_side_effects=True),
    )(part)


def split_lanes(merged, lanes):
    return tuple(
        merged[..., start : start + lanes] for start in range(0, merged.shape[-1], lanes)
    )


def tables(rows_out, cols_in, period):
    row_index = lax.broadcasted_iota(jnp.int32, (rows_out, cols_in), 0)
    col_index = lax.broadcasted_iota(jnp.int32, (rows_out, cols_in), 1)
    phase_angle = (row_index * col_index % period).astype(jnp.float32) * (2.0 * math.pi / period)
    return (jnp.cos(phase_angle), jnp.sin(phase_angle))


def odd_tables(rows_out, cols_in, period, odd_axis):
    row_index = lax.broadcasted_iota(jnp.int32, (rows_out, cols_in), 0)
    col_index = lax.broadcasted_iota(jnp.int32, (rows_out, cols_in), 1)
    if odd_axis == 0:
        row_index = 2 * row_index + 1
    else:
        col_index = 2 * col_index + 1
    phase_angle = (row_index * col_index % (2 * period)).astype(jnp.float32) * (math.pi / period)
    return (jnp.cos(phase_angle), jnp.sin(phase_angle))


def along_rows(factor, values):
    return jnp.tensordot(factor, values, axes=1, precision=exact_mode)


def rows_spectrum(signal, basis_pair):
    return (along_rows(basis_pair[0], signal), -along_rows(basis_pair[1], signal))


def rows_inverse(complex_pair, basis_pair):
    total = along_rows(basis_pair[0], complex_pair[0]) - along_rows(basis_pair[1], complex_pair[1])
    return total / basis_pair[0].shape[1]


def block_forward(complex_pair, basis_pair):
    cosine_part, sine_part = basis_pair

    def one_pass(factor, values):
        return jnp.tensordot(factor, values, axes=1, precision=lax.Precision.DEFAULT)

    real_part = one_pass(cosine_part, complex_pair[0]) + one_pass(sine_part, complex_pair[1])
    imag_part = one_pass(cosine_part, complex_pair[1]) - one_pass(sine_part, complex_pair[0])
    return (real_part, imag_part)


def block_inverse(complex_pair, basis_pair):
    cosine_part, sine_part = basis_pair
    norming = 1.0 / cosine_part.shape[1]
    real_part = along_rows(cosine_part, complex_pair[0]) - along_rows(sine_part, complex_pair[1])
    imag_part = along_rows(cosine_part, complex_pair[1]) + along_rows(sine_part, complex_pair[0])
    return (real_part * norming, imag_part * norming)


def complex_product(first_pair, second_pair):
    return (
        first_pair[0] * second_pair[0] - first_pair[1] * second_pair[1],
        first_pair[0] * second_pair[1] + first_pair[1] * second_pair[0],
    )


def conj_product(first_pair, second_pair):
    return (
        first_pair[0] * second_pair[0] + first_pair[1] * second_pair[1],
        first_pair[0] * second_pair[1] - first_pair[1] * second_pair[0],
    )


def on_device(
    query_proj, key_proj, value_proj, short_filter, long_filter, skip_gain, out_weight, cotangent
):
    block_rows = query_proj.shape[0]
    tap_count = short_filter.shape[1]
    block_count = lax.axis_size(SEQ)
    streams = jnp.stack([query_proj, key_proj, value_proj])
    earlier = from_behind(streams[:, block_rows - (tap_count - 1) :], SEQ, 1)
    extended = jnp.concatenate([earlier, streams], axis=1).astype(jnp.float32)
    shifted = [
        extended[:, tap_count - 1 - offset : tap_count - 1 - offset + block_rows]
        for offset in range(tap_count)
    ]
    filtered = sum(
        (short_filter[:, offset][:, None, :] * shifted[offset] for offset in range(tap_count))
    )
    query_short, key_short, value_short = (filtered[0], filtered[1], filtered[2])
    product = key_short * value_short
    forward_basis = odd_tables(block_rows, block_rows, 2 * block_rows, 0)
    spread_basis = odd_tables(block_rows, 2 * block_rows, 2 * block_rows, 0)
    fold_basis = odd_tables(2 * block_rows, block_rows, 2 * block_rows, 1)
    half_basis = odd_tables(block_rows, block_rows, 2 * block_rows, 1)
    block_basis = tables(2 * block_count, block_count, 2 * block_count)
    return_basis = tables(block_count, 2 * block_count, 2 * block_count)
    input_pair = rows_spectrum(product, forward_basis)
    filter_pair = rows_spectrum(long_filter, forward_basis)
    lanes = product.shape[1]
    moved_data = split_lanes(
        lax.all_to_all(
            jnp.concatenate([input_pair[0], input_pair[1], filter_pair[0], filter_pair[1]], axis=1)[
                None
            ].astype(jnp.bfloat16),
            SEQ,
            split_axis=1,
            concat_axis=0,
            tiled=True,
        ).astype(jnp.float32),
        lanes,
    )
    input_spectrum = block_forward((moved_data[0], moved_data[1]), block_basis)
    filter_spectrum = block_forward((moved_data[2], moved_data[3]), block_basis)
    inverse_pair = block_inverse(complex_product(filter_spectrum, input_spectrum), return_basis)
    returned = split_lanes(
        lax.all_to_all(
            as_sent(jnp.concatenate(inverse_pair, axis=-1)),
            SEQ,
            split_axis=0,
            concat_axis=1,
            tiled=True,
        ).astype(jnp.float32),
        lanes,
    )
    folded = rows_inverse((returned[0][0], returned[1][0]), fold_basis)
    carried = from_behind(folded[block_rows:], SEQ, 1)
    convolved = folded[:block_rows] + carried
    mixed_seq = convolved + skip_gain * product
    gated_values = (query_short * mixed_seq).astype(jnp.bfloat16)
    full_cotangent = lax.all_gather(cotangent, "ch", axis=1, tiled=True)
    full_cotangent, gated_values = lax.optimization_barrier((full_cotangent, gated_values))
    partial_value = jnp.dot(gated_values, out_weight, preferred_element_type=jnp.float32)
    layer_out = lax.psum_scatter(partial_value, "ch", scatter_dimension=1, tiled=True).astype(
        jnp.bfloat16
    )
    grad_gated = lax.dot_general(
        full_cotangent, out_weight, (((1,), (1,)), ((), ())), preferred_element_type=jnp.float32
    )
    outer = lax.axis_size("seq_hi")
    inner = lax.axis_size("seq_lo")
    feature_rows = full_cotangent.shape[1] // outer // inner
    local_rows = lax.all_gather(gated_values, "seq_lo", axis=0, tiled=True)
    local_features = lax.all_to_all(
        full_cotangent.reshape(block_rows, outer, inner, feature_rows),
        "seq_lo",
        split_axis=2,
        concat_axis=0,
        tiled=True,
    ).reshape(block_rows * inner, -1)
    weight_terms = lax.dot_general(
        local_features,
        local_rows,
        (((0,), (0,)), ((), ())),
        preferred_element_type=jnp.float32,
    )
    grad_mixed = grad_gated * query_short
    grad_query_short = grad_gated * mixed_seq
    following = from_behind(grad_mixed.astype(jnp.bfloat16), SEQ, -1).astype(grad_mixed.dtype)
    spread = jnp.concatenate([grad_mixed, following], axis=0)
    grad_pair = rows_spectrum(spread, spread_basis)
    moved_grad = split_lanes(
        lax.all_to_all(
            jnp.concatenate(grad_pair, axis=1)[None].astype(jnp.bfloat16),
            SEQ,
            split_axis=1,
            concat_axis=0,
            tiled=True,
        ).astype(jnp.float32),
        lanes,
    )
    grad_spectrum = block_forward(moved_grad, block_basis)
    input_back = block_inverse(conj_product(filter_spectrum, grad_spectrum), return_basis)
    filter_back = block_inverse(conj_product(input_spectrum, grad_spectrum), return_basis)
    returned_grad = split_lanes(
        lax.all_to_all(
            as_sent(jnp.concatenate(input_back + filter_back, axis=-1)),
            SEQ,
            split_axis=0,
            concat_axis=1,
            tiled=True,
        ),
        lanes,
    )
    grad_w_out_t = lax.psum_scatter(weight_terms, "seq_hi", scatter_dimension=0, tiled=True)
    grad_w_out_t, layer_out, returned_grad = lax.optimization_barrier(
        (grad_w_out_t, layer_out, returned_grad)
    )
    conv_grad = rows_inverse((returned_grad[0][0], returned_grad[1][0]), half_basis)
    grad_filter = rows_inverse((returned_grad[2][0], returned_grad[3][0]), half_basis)
    grad_product = conv_grad + skip_gain * grad_mixed
    grad_streams = jnp.stack(
        [grad_query_short, grad_product * value_short, grad_product * key_short]
    )
    later_rows = from_behind(grad_streams[:, : tap_count - 1], SEQ, -1)
    padded_grad = jnp.concatenate([grad_streams, later_rows], axis=1)
    grad_inputs = sum(
        (
            short_filter[:, offset][:, None, :] * padded_grad[:, offset : offset + block_rows]
            for offset in range(tap_count)
        )
    )
    short_terms = jnp.stack(
        [jnp.sum(grad_streams * shifted[offset], axis=1) for offset in range(tap_count)], axis=1
    )
    skip_terms = jnp.sum(grad_mixed * product, axis=0)
    channel_count = skip_terms.shape[0]
    sum_rows = short_terms.shape[0] * short_terms.shape[1] + 1
    padded_rows = -(-sum_rows // 8) * 8
    small_terms = jnp.concatenate(
        [
            short_terms.reshape(sum_rows - 1, channel_count),
            skip_terms[None],
            jnp.zeros((padded_rows - sum_rows, channel_count), jnp.float32),
        ]
    )
    (outer_sum,) = sum_over_group(small_terms, "seq_hi", 0)
    grad_short, skip_row = sum_over_group(
        outer_sum, "seq_lo", 1, (short_terms.shape, (1, channel_count))
    )
    grad_skip = skip_row[0]
    return (
        layer_out,
        grad_inputs[0],
        grad_inputs[1],
        grad_inputs[2],
        grad_short,
        grad_filter,
        grad_skip,
        grad_w_out_t,
    )


def solution(mesh):
    in_specs = (
        P(SEQ, "ch"),
        P(SEQ, "ch"),
        P(SEQ, "ch"),
        P(None, None, "ch"),
        P(SEQ, "ch"),
        P("ch"),
        P("ch", None),
        P(SEQ, "ch"),
    )
    out_specs = (
        P(SEQ, "ch"),
        P(SEQ, "ch"),
        P(SEQ, "ch"),
        P(SEQ, "ch"),
        P(None, None, "ch"),
        P(SEQ, "ch"),
        P("ch"),
        P(SEQ, "ch"),
    )
    inner = 8
    seq_mesh = jax.sharding.Mesh(
        mesh.devices.reshape(mesh.shape["seq"] // inner, inner, mesh.shape["ch"]),
        ("seq_hi", "seq_lo", "ch"),
    )
    return jax.shard_map(
        on_device, mesh=seq_mesh, in_specs=in_specs, out_specs=out_specs, check_vma=False
    )
```

```python
import functools
import math

import jax
import jax.numpy as jnp
from jax import lax
from jax.experimental import pallas as pl
from jax.experimental.pallas import tpu as pltpu
from jax.sharding import PartitionSpec as P

exact_mode = lax.Precision.HIGH
SEQ = ("seq_hi", "seq_lo")


def from_behind(shard, axis, by):
    size = lax.axis_size(axis)
    pairs = [(i, i + by) for i in range(size) if 0 <= i + by < size]
    return lax.ppermute(shard, axis, pairs)


def as_sent(shard):

    def short(part):
        return part.astype(jnp.bfloat16) if part.dtype == jnp.float32 else part

    return jax.tree.map(short, shard)


def group_sum_kernel(axis, shape_out, part_ref, *refs):
    outs = refs[: len(shape_out)]
    slots, local_sem, send_sems, recv_sems = refs[len(shape_out) :]
    count = lax.axis_size(axis)
    me = lax.axis_index(axis)
    place = {"seq_hi": lax.axis_index("seq_hi"), "seq_lo": lax.axis_index("seq_lo")}

    def member(index):
        where = dict(place, **{axis: index})
        return (where["seq_hi"], where["seq_lo"], lax.axis_index("ch"))

    barrier = pltpu.get_barrier_semaphore()
    for step in range(1, count):
        pl.semaphore_signal(
            barrier,
            1,
            device_id=member(lax.rem(me + step, count)),
            device_id_type=pl.DeviceIdType.MESH,
        )
    pl.semaphore_wait(barrier, count - 1)
    own = pltpu.make_async_copy(part_ref, slots.at[me], local_sem)
    own.start()
    outgoing = []
    for step in range(1, count):
        peer = lax.rem(me + step, count)
        copy = pltpu.make_async_remote_copy(
            src_ref=part_ref,
            dst_ref=slots.at[me],
            send_sem=send_sems.at[step],
            recv_sem=recv_sems.at[me],
            device_id=member(peer),
            device_id_type=pl.DeviceIdType.MESH,
        )
        copy.start()
        outgoing.append(copy)
    own.wait()
    for step in range(1, count):
        source = lax.rem(me + count - step, count)
        outgoing[step - 1].wait_send()
        pltpu.make_async_remote_copy(
            src_ref=part_ref,
            dst_ref=slots.at[source],
            send_sem=send_sems.at[step],
            recv_sem=recv_sems.at[source],
            device_id=member(source),
            device_id_type=pl.DeviceIdType.MESH,
        ).wait_recv()
    total = slots[0]
    for slot in range(1, count):
        total = total + slots[slot]
    if len(outs) == 1:
        outs[0][...] = total
        return
    short_ref, skip_ref = outs
    streams, taps = short_ref.shape[0], short_ref.shape[1]
    for stream in range(streams):
        short_ref[stream] = total[stream * taps : (stream + 1) * taps]
    skip_ref[...] = total[streams * taps : streams * taps + 1]


def sum_over_group(part, axis, kernel_id, shape_out=None):
    count = lax.axis_size(axis)
    shape_out = shape_out or (part.shape,)
    return pl.pallas_call(
        functools.partial(group_sum_kernel, axis, shape_out),
        out_shape=[jax.ShapeDtypeStruct(shape, part.dtype) for shape in shape_out],
        in_specs=[pl.BlockSpec(memory_space=pltpu.VMEM)],
        out_specs=[pl.BlockSpec(memory_space=pltpu.VMEM) for _ in shape_out],
        scratch_shapes=[
            pltpu.VMEM((count,) + part.shape, part.dtype),
            pltpu.SemaphoreType.DMA(()),
            pltpu.SemaphoreType.DMA((count,)),
            pltpu.SemaphoreType.DMA((count,)),
        ],
        compiler_params=pltpu.CompilerParams(collective_id=kernel_id, has_side_effects=True),
    )(part)


def split_lanes(merged, lanes):
    return tuple(
        merged[..., start : start + lanes] for start in range(0, merged.shape[-1], lanes)
    )


def tables(rows_out, cols_in, period):
    row_index = lax.broadcasted_iota(jnp.int32, (rows_out, cols_in), 0)
    col_index = lax.broadcasted_iota(jnp.int32, (rows_out, cols_in), 1)
    phase_angle = (row_index * col_index % period).astype(jnp.float32) * (2.0 * math.pi / period)
    return (jnp.cos(phase_angle), jnp.sin(phase_angle))


def odd_tables(rows_out, cols_in, period, odd_axis):
    row_index = lax.broadcasted_iota(jnp.int32, (rows_out, cols_in), 0)
    col_index = lax.broadcasted_iota(jnp.int32, (rows_out, cols_in), 1)
    if odd_axis == 0:
        row_index = 2 * row_index + 1
    else:
        col_index = 2 * col_index + 1
    phase_angle = (row_index * col_index % (2 * period)).astype(jnp.float32) * (math.pi / period)
    return (jnp.cos(phase_angle), jnp.sin(phase_angle))


def along_rows(factor, values):
    return jnp.tensordot(factor, values, axes=1, precision=exact_mode)


def rows_spectrum(signal, basis_pair):
    return (along_rows(basis_pair[0], signal), -along_rows(basis_pair[1], signal))


def rows_inverse(complex_pair, basis_pair):
    total = along_rows(basis_pair[0], complex_pair[0]) - along_rows(basis_pair[1], complex_pair[1])
    return total / basis_pair[0].shape[1]


def block_forward(complex_pair, basis_pair):
    cosine_part, sine_part = basis_pair

    def one_pass(factor, values):
        return jnp.tensordot(factor, values, axes=1, precision=lax.Precision.DEFAULT)

    real_part = one_pass(cosine_part, complex_pair[0]) + one_pass(sine_part, complex_pair[1])
    imag_part = one_pass(cosine_part, complex_pair[1]) - one_pass(sine_part, complex_pair[0])
    return (real_part, imag_part)


def block_inverse(complex_pair, basis_pair):
    cosine_part, sine_part = basis_pair
    norming = 1.0 / cosine_part.shape[1]
    real_part = along_rows(cosine_part, complex_pair[0]) - along_rows(sine_part, complex_pair[1])
    imag_part = along_rows(cosine_part, complex_pair[1]) + along_rows(sine_part, complex_pair[0])
    return (real_part * norming, imag_part * norming)


def complex_product(first_pair, second_pair):
    return (
        first_pair[0] * second_pair[0] - first_pair[1] * second_pair[1],
        first_pair[0] * second_pair[1] + first_pair[1] * second_pair[0],
    )


def conj_product(first_pair, second_pair):
    return (
        first_pair[0] * second_pair[0] + first_pair[1] * second_pair[1],
        first_pair[0] * second_pair[1] - first_pair[1] * second_pair[0],
    )


def on_device(
    query_proj, key_proj, value_proj, short_filter, long_filter, skip_gain, out_weight, cotangent
):
    block_rows = query_proj.shape[0]
    tap_count = short_filter.shape[1]
    block_count = lax.axis_size(SEQ)
    streams = jnp.stack([query_proj, key_proj, value_proj])
    earlier = from_behind(streams[:, block_rows - (tap_count - 1) :], SEQ, 1)
    extended = jnp.concatenate([earlier, streams], axis=1).astype(jnp.float32)
    shifted = [
        extended[:, tap_count - 1 - offset : tap_count - 1 - offset + block_rows]
        for offset in range(tap_count)
    ]
    filtered = sum(
        (short_filter[:, offset][:, None, :] * shifted[offset] for offset in range(tap_count))
    )
    query_short, key_short, value_short = (filtered[0], filtered[1], filtered[2])
    product = key_short * value_short
    forward_basis = odd_tables(block_rows, block_rows, 2 * block_rows, 0)
    spread_basis = odd_tables(block_rows, 2 * block_rows, 2 * block_rows, 0)
    fold_basis = odd_tables(2 * block_rows, block_rows, 2 * block_rows, 1)
    half_basis = odd_tables(block_rows, block_rows, 2 * block_rows, 1)
    block_basis = tables(2 * block_count, block_count, 2 * block_count)
    return_basis = tables(block_count, 2 * block_count, 2 * block_count)
    lanes = product.shape[1]
    both_pair = rows_spectrum(jnp.concatenate([product, long_filter], axis=1), forward_basis)
    moved_data = split_lanes(
        lax.all_to_all(
            jnp.concatenate(both_pair, axis=1)[None].astype(jnp.bfloat16),
            SEQ,
            split_axis=1,
            concat_axis=0,
            tiled=True,
        ).astype(jnp.float32),
        lanes,
    )
    input_spectrum = block_forward((moved_data[0], moved_data[2]), block_basis)
    filter_spectrum = block_forward((moved_data[1], moved_data[3]), block_basis)
    inverse_pair = block_inverse(complex_product(filter_spectrum, input_spectrum), return_basis)
    returned = split_lanes(
        lax.all_to_all(
            as_sent(jnp.concatenate(inverse_pair, axis=-1)),
            SEQ,
            split_axis=0,
            concat_axis=1,
            tiled=True,
        ).astype(jnp.float32),
        lanes,
    )
    folded = rows_inverse((returned[0][0], returned[1][0]), fold_basis)
    carried = from_behind(folded[block_rows:], SEQ, 1)
    convolved = folded[:block_rows] + carried
    mixed_seq = convolved + skip_gain * product
    gated_values = (query_short * mixed_seq).astype(jnp.bfloat16)
    full_cotangent = lax.all_gather(cotangent, "ch", axis=1, tiled=True)
    full_cotangent, gated_values = lax.optimization_barrier((full_cotangent, gated_values))
    partial_value = jnp.dot(gated_values, out_weight, preferred_element_type=jnp.float32)
    layer_out = lax.psum_scatter(partial_value, "ch", scatter_dimension=1, tiled=True).astype(
        jnp.bfloat16
    )
    grad_gated = lax.dot_general(
        full_cotangent, out_weight, (((1,), (1,)), ((), ())), preferred_element_type=jnp.float32
    )
    outer = lax.axis_size("seq_hi")
    inner = lax.axis_size("seq_lo")
    feature_rows = full_cotangent.shape[1] // outer // inner
    local_rows = lax.all_gather(gated_values, "seq_lo", axis=0, tiled=True)
    local_features = lax.all_to_all(
        full_cotangent.reshape(block_rows, outer, inner, feature_rows),
        "seq_lo",
        split_axis=2,
        concat_axis=0,
        tiled=True,
    ).reshape(block_rows * inner, -1)
    weight_terms = lax.dot_general(
        local_features,
        local_rows,
        (((0,), (0,)), ((), ())),
        preferred_element_type=jnp.float32,
    )
    grad_mixed = grad_gated * query_short
    grad_query_short = grad_gated * mixed_seq
    following = from_behind(grad_mixed.astype(jnp.bfloat16), SEQ, -1).astype(grad_mixed.dtype)
    spread = jnp.concatenate([grad_mixed, following], axis=0)
    grad_pair = rows_spectrum(spread, spread_basis)
    moved_grad = split_lanes(
        lax.all_to_all(
            jnp.concatenate(grad_pair, axis=1)[None].astype(jnp.bfloat16),
            SEQ,
            split_axis=1,
            concat_axis=0,
            tiled=True,
        ).astype(jnp.float32),
        lanes,
    )
    grad_spectrum = block_forward(moved_grad, block_basis)
    input_back = block_inverse(conj_product(filter_spectrum, grad_spectrum), return_basis)
    filter_back = block_inverse(conj_product(input_spectrum, grad_spectrum), return_basis)
    returned_grad = split_lanes(
        lax.all_to_all(
            as_sent(
                jnp.concatenate(
                    [input_back[0], filter_back[0], input_back[1], filter_back[1]], axis=-1
                )
            ),
            SEQ,
            split_axis=0,
            concat_axis=1,
            tiled=True,
        ),
        lanes,
    )
    grad_w_out_t = lax.psum_scatter(weight_terms, "seq_hi", scatter_dimension=0, tiled=True)
    grad_w_out_t, layer_out, returned_grad = lax.optimization_barrier(
        (grad_w_out_t, layer_out, returned_grad)
    )
    both_back = rows_inverse(
        (
            jnp.concatenate([returned_grad[0][0], returned_grad[1][0]], axis=-1),
            jnp.concatenate([returned_grad[2][0], returned_grad[3][0]], axis=-1),
        ),
        half_basis,
    )
    conv_grad, grad_filter = split_lanes(both_back, lanes)
    grad_product = conv_grad + skip_gain * grad_mixed
    grad_streams = jnp.stack(
        [grad_query_short, grad_product * value_short, grad_product * key_short]
    )
    later_rows = from_behind(grad_streams[:, : tap_count - 1], SEQ, -1)
    padded_grad = jnp.concatenate([grad_streams, later_rows], axis=1)
    grad_inputs = sum(
        (
            short_filter[:, offset][:, None, :] * padded_grad[:, offset : offset + block_rows]
            for offset in range(tap_count)
        )
    )
    short_terms = jnp.stack(
        [jnp.sum(grad_streams * shifted[offset], axis=1) for offset in range(tap_count)], axis=1
    )
    skip_terms = jnp.sum(grad_mixed * product, axis=0)
    channel_count = skip_terms.shape[0]
    sum_rows = short_terms.shape[0] * short_terms.shape[1] + 1
    padded_rows = -(-sum_rows // 8) * 8
    small_terms = jnp.concatenate(
        [
            short_terms.reshape(sum_rows - 1, channel_count),
            skip_terms[None],
            jnp.zeros((padded_rows - sum_rows, channel_count), jnp.float32),
        ]
    )
    (outer_sum,) = sum_over_group(small_terms, "seq_hi", 0)
    grad_short, skip_row = sum_over_group(
        outer_sum, "seq_lo", 1, (short_terms.shape, (1, channel_count))
    )
    grad_skip = skip_row[0]
    return (
        layer_out,
        grad_inputs[0],
        grad_inputs[1],
        grad_inputs[2],
        grad_short,
        grad_filter,
        grad_skip,
        grad_w_out_t,
    )


def solution(mesh):
    in_specs = (
        P(SEQ, "ch"),
        P(SEQ, "ch"),
        P(SEQ, "ch"),
        P(None, None, "ch"),
        P(SEQ, "ch"),
        P("ch"),
        P("ch", None),
        P(SEQ, "ch"),
    )
    out_specs = (
        P(SEQ, "ch"),
        P(SEQ, "ch"),
        P(SEQ, "ch"),
        P(SEQ, "ch"),
        P(None, None, "ch"),
        P(SEQ, "ch"),
        P("ch"),
        P(SEQ, "ch"),
    )
    inner = 8
    seq_mesh = jax.sharding.Mesh(
        mesh.devices.reshape(mesh.shape["seq"] // inner, inner, mesh.shape["ch"]),
        ("seq_hi", "seq_lo", "ch"),
    )
    return jax.shard_map(
        on_device, mesh=seq_mesh, in_specs=in_specs, out_specs=out_specs, check_vma=False
    )
```
